32 devices in a mesh: dp: 8 (over y, x, core), tensor: 4 (over z).
Axes of the slice: x: 2, y: 2, z: 4, core: 2. Of those that a mesh axis runs over, the one named last changes fastest.
Arguments:
- tokens: bfloat16 [16384, 768], P(('dp', 'tensor')), may hold values from -6 to 6
- time_embed: bfloat16 [8, 128], P('dp'), may hold values from -6 to 6
- ada_weight: bfloat16 [128, 4608], P(None, 'dp'), may hold values from -1 to 1
- ada_bias: bfloat16 [4608], P('dp'), may hold values from -4 to 4
- norm1_gain: bfloat16 [768], P('dp'), may hold values from 0.5 to 1.5
- qkv_weight: bfloat16 [3, 768, 768], P(None, 'dp', 'tensor'), may hold values from -1 to 1
- out_weight: bfloat16 [768, 768], P('tensor', 'dp'), may hold values from -2 to 2
- norm2_gain: bfloat16 [768], P('dp'), may hold values from 0.5 to 1.5
- up_weight: bfloat16 [768, 3072], P('dp', 'tensor'), may hold values from -0.21875 to 0.21875
- up_bias: bfloat16 [3072], P(('tensor', 'dp')), may hold values from -4 to 4
- down_weight: bfloat16 [3072, 768], P('tensor', 'dp'), may hold values from -0.109375 to 0.109375
- down_bias: bfloat16 [768], P('dp'), may hold values from -4 to 4
- out_grad: bfloat16 [16384, 768], P(('dp', 'tensor')), may hold values from -6 to 6
Outputs:
- output: bfloat16 [16384, 768], P(('dp', 'tensor'))
- input_grad: bfloat16 [16384, 768], P(('dp', 'tensor'))
- time_grad: float32 [8, 128], P('dp')
- ada_weight_grad: float32 [128, 4608], P(None, 'dp')
- ada_bias_grad: float32 [4608], P('dp')
- norm1_gain_grad: float32 [768], P('dp')
- qkv_weight_grad: float32 [3, 768, 768], P(None, 'dp', 'tensor')
- out_weight_grad: float32 [768, 768], P('tensor', 'dp')
- norm2_gain_grad: float32 [768], P('dp')
- up_weight_grad: float32 [768, 3072], P('dp', 'tensor')
- up_bias_grad: float32 [3072], P(('tensor', 'dp'))
- down_weight_grad: float32 [3072, 768], P('tensor', 'dp')
- down_bias_grad: float32 [768], P('dp')
The draws below stay inside these ranges and needn't reach their ends.
All inputs are finite; a program needn't handle non-finite values.
Results may differ from the reference program's by a relative error of at most 0.017.
The reference program's roundings to bfloat16 on the way count: a program that leaves them out, or rounds other values in their place, can miss the bound.
Values may be sent and summed in bfloat16 or wider, within the bound.
No kernel may reach another device: no remote copies, remote signals or barrier semaphores. Data moves between devices by JAX's collectives and lax.ppermute only.
A program may use at most 192 MiB of HBM per device.

```python
import math
import jax
import jax.numpy as jnp
from jax import lax

D = 768
HEADS = 12
HEAD_DIM = 64
FF = 3072
COND = 128
LEN = 2048
SEQS = 8
TOKENS = 16384


def drawn_values(key, shape, deviation, bound):
    values = jnp.clip(jax.random.normal(key, shape, jnp.float32) * deviation, -bound, bound)
    return values.astype(jnp.bfloat16)


def draw_time_embed(key, part):
    return drawn_values(jax.random.fold_in(key, 11), (SEQS, COND), 1.0, 6.0)


def draw_ada_weight(key, part):
    deviation = (4.0 * COND) ** (-0.5)
    return drawn_values(jax.random.fold_in(key, 12), (COND, 6 * D), deviation, 6.0 * deviation)


def draw_qkv_weight(key, part):
    deviation = (D / 2.0) ** (-0.5)
    return drawn_values(jax.random.fold_in(key, 13), (3, D, D), deviation, 6.0 * deviation)


def strengthened(array, own_key, source, target, shards_of, factor):
    def block_of(axis_at):
        return (jnp.arange(array.shape[axis_at]) // (array.shape[axis_at] // shards_of)).reshape((-1,) + (1,) * (array.ndim - 1 - axis_at))

    near = jax.random.permutation(own_key, shards_of)[block_of(target)]
    other_side = (block_of(target) + shards_of // 2) % shards_of
    return jnp.where((block_of(source) == near) | (block_of(source) == other_side), factor * array, array)


def levels(stream_key, dims, cuts, least, top_value):
    level = 1.0
    for position, shards_of in cuts:
        steps = jax.random.uniform(jax.random.fold_in(jax.random.fold_in(stream_key, 6), position), (shards_of,), jnp.float32, least / len(cuts), top_value / len(cuts))
        level = level * jnp.repeat(jnp.exp(steps), dims[position] // shards_of).reshape((-1,) + (1,) * (len(dims) - 1 - position))
    return level


def centred(key, dims, scale, reach, cuts=(), kind=jnp.bfloat16):
    level = levels(key, dims, cuts, -0.22, 0.18) if cuts else 1.0
    values = jax.random.normal(key, dims, jnp.float32) * scale * level
    return jnp.minimum(jnp.maximum(values, -reach), reach).astype(kind)


def heavy_noise(own_key, dims, scale, limit, cuts, heavy, kind=jnp.bfloat16):
    entries = scale * jax.random.normal(own_key, dims, jnp.float32)
    if cuts:
        entries = entries * levels(own_key, dims, cuts, -0.22, 0.18)
    return jnp.clip(strengthened(entries, jax.random.fold_in(own_key, 3), *heavy), -limit, limit).astype(kind)


def setup_inputs(seed: int = 0) -> dict:
    seeds = jax.random.split(jax.random.key(seed), 14)
    tokens = centred(seeds[0], (TOKENS, D), 1.0, 6.0, ((0, 32),))
    time_embed = draw_time_embed(jax.random.fold_in(seeds[13], 71), 0)
    ada_weight = draw_ada_weight(jax.random.fold_in(seeds[13], 71), 0)
    ada_bias = centred(seeds[3], (6 * D,), 0.3, 4.0, ((0, 8),))
    norm1_gain = jnp.clip(1.0 + 0.1 * jax.random.normal(seeds[4], (D,), jnp.float32), 0.5, 1.5).astype(jnp.bfloat16)
    qkv_weight = draw_qkv_weight(jax.random.fold_in(seeds[13], 71), 0)
    out_weight = centred(seeds[6], (D, D), 8 ** -0.5, 2.0, ((0, 4), (1, 8)))
    norm2_gain = jnp.clip(1.0 + 0.1 * jax.random.normal(seeds[7], (D,), jnp.float32), 0.5, 1.5).astype(jnp.bfloat16)
    up_weight = centred(seeds[8], (D, FF), D ** -0.5, 0.21875, ((0, 8), (1, 4)))
    up_bias = centred(seeds[9], (FF,), 0.5, 4.0, ((0, 32),))
    down_weight = centred(seeds[10], (FF, D), FF ** -0.5, 0.109375, ((0, 4), (1, 8)))
    down_bias = centred(seeds[11], (D,), 0.3, 4.0, ((0, 8),))
    out_grad = heavy_noise(seeds[12], (TOKENS, D), 1.0, 6.0, ((0, 32),), (0, 1, 32, 2.75))
    return {"tokens": tokens, "time_embed": time_embed, "ada_weight": ada_weight, "ada_bias": ada_bias, "norm1_gain": norm1_gain, "qkv_weight": qkv_weight, "out_weight": out_weight, "norm2_gain": norm2_gain, "up_weight": up_weight, "up_bias": up_bias, "down_weight": down_weight, "down_bias": down_bias, "out_grad": out_grad}


EPSILON = 1e-05
ROPE_BASE = 10000.0
HIGHEST = lax.Precision.HIGHEST

@jax.custom_vjp
def low(v):
    return lax.optimization_barrier(v.astype(jnp.bfloat16)).astype(jnp.float32)

@jax.custom_vjp
def low_back(v):
    return v

def low_keep(v):
    return (low(v), None)

def low_pass(kept, grad):
    return (grad,)

def back_keep(v):
    return (v, None)

def back_low(kept, grad):
    return (low(grad),)
low.defvjp(low_keep, low_pass)
low_back.defvjp(back_keep, back_low)

def rotate_half(values):
    middle = values.shape[-1] // 2
    return jnp.concatenate([-values[..., middle:], values[..., :middle]], axis=-1)

def rope_tables(positions, head_dim):
    middle = head_dim // 2
    frequency = jnp.exp(jnp.arange(middle, dtype=jnp.float32) * (-2.0 * math.log(ROPE_BASE) / head_dim))
    angles = positions.astype(jnp.float32)[:, None] * frequency[None, :]
    angles = jnp.concatenate([angles, angles], axis=-1)
    return (jnp.cos(angles)[:, None, :], jnp.sin(angles)[:, None, :])

def normalize(rows):
    center = lax.optimization_barrier(jnp.mean(rows, axis=-1, keepdims=True))
    shifted = rows - center
    inverse = lax.rsqrt(lax.optimization_barrier(jnp.mean(shifted * shifted, axis=-1, keepdims=True)) + EPSILON)
    return shifted * inverse

def gelu_tanh(values):
    return jax.nn.gelu(values, approximate=True)

def attend(queries, key_rows, value_rows):
    length = queries.shape[0]
    block_rows = min(512, length)
    factor = 1.0 / math.sqrt(HEAD_DIM)

    def one_block(query_block):
        scores = low_back(jnp.einsum('qhd,khd->hqk', query_block, key_rows, precision=HIGHEST) * factor)
        highest = lax.optimization_barrier(jnp.max(scores, axis=-1, keepdims=True))
        exponent = jnp.exp(scores - highest)
        weights = exponent / lax.optimization_barrier(jnp.sum(exponent, axis=-1, keepdims=True))
        return jnp.einsum('hqk,khd->qhd', low(weights), value_rows, precision=HIGHEST)
    blocks = lax.map(jax.checkpoint(one_block), queries.reshape(length // block_rows, block_rows, HEADS, HEAD_DIM))
    return blocks.reshape(length, HEADS * HEAD_DIM)

def layer(inputs, time_row, ada_weight, ada_bias, norm1_gain, qkv_weight, out_weight, norm2_gain, up_weight, up_bias, down_weight, down_bias):
    length = inputs.shape[0]
    modulation = low_back(jnp.dot(time_row, ada_weight, precision=HIGHEST) + ada_bias)
    shift_one, scale_one, gate_one, shift_two, scale_two, gate_two = jnp.split(modulation, 6)
    hidden_one = low(normalize(inputs) * norm1_gain * (1.0 + scale_one) + shift_one)
    projected = jnp.einsum('ld,cde->cle', hidden_one, qkv_weight, precision=HIGHEST)
    cosine_table, sine_table = rope_tables(jnp.arange(length), HEAD_DIM)

    def rotate_rows(values):
        per_head = values.reshape(length, HEADS, HEAD_DIM)
        return per_head * cosine_table + rotate_half(per_head) * sine_table
    queries = low(rotate_rows(low_back(projected[0])))
    key_rows = low(rotate_rows(low_back(projected[1])))
    value_rows = low(low_back(projected[2])).reshape(length, HEADS, HEAD_DIM)
    attention = low_back(low(attend(queries, key_rows, value_rows)))
    branch_one = low_back(jnp.dot(attention, out_weight, precision=HIGHEST))
    residual = inputs + gate_one * branch_one
    hidden_two = low(normalize(residual) * norm2_gain * (1.0 + scale_two) + shift_two)
    pre_act = low_back(jnp.dot(hidden_two, up_weight, precision=HIGHEST) + up_bias)
    activated = low(gelu_tanh(pre_act))
    branch_two = low_back(jnp.dot(activated, down_weight, precision=HIGHEST) + down_bias)
    return residual + gate_two * branch_two

def reference(tokens, time_embed, ada_weight, ada_bias, norm1_gain, qkv_weight, out_weight, norm2_gain, up_weight, up_bias, down_weight, down_bias, out_grad):
    params = tuple((weight_arg.astype(jnp.float32) for weight_arg in (ada_weight, ada_bias, norm1_gain, qkv_weight, out_weight, norm2_gain, up_weight, up_bias, down_weight, down_bias)))
    seq_total = time_embed.shape[0]
    inputs = tokens.reshape(seq_total, LEN, D)
    cotangent = out_grad.reshape(seq_total, LEN, D)

    def one_sequence(totals, sequence_items):
        input_seq, time_seq, grad_seq = sequence_items
        output_seq, pullback = jax.vjp(layer, input_seq.astype(jnp.float32), time_seq.astype(jnp.float32), *params)
        gradients = pullback(grad_seq.astype(jnp.float32))
        totals = tuple((running + addend for running, addend in zip(totals, gradients[2:])))
        return (totals, (output_seq.astype(jnp.bfloat16), gradients[0].astype(jnp.bfloat16), gradients[1]))
    starting = tuple((jnp.zeros_like(weight_arg) for weight_arg in params))
    totals, (outputs, input_grads, time_grads) = lax.scan(one_sequence, starting, (inputs, time_embed, cotangent))
    return (outputs.reshape(TOKENS, D), input_grads.reshape(TOKENS, D), time_grads, totals[0], totals[1], totals[2], totals[3], totals[4], totals[5], totals[6], totals[7], totals[8], totals[9])
```

```python
import functools
import math

import jax
import jax.numpy as jnp
from jax import lax
from jax.experimental import pallas as pl
from jax.experimental.pallas import tpu as pltpu
from jax.sharding import PartitionSpec as P

HEAD_DIM = 64
EPSILON = 1e-05
ROPE_BASE = 10000.0
GROUP = 4
PLANE_OF = (0, 3, 1, 2)
SEQ_OF = (0, 2, 3, 1)
AXES = ("dp", "tensor")
f32 = jnp.float32
bf16 = jnp.bfloat16


def permute(array, dp_size, target):
    pairs = []
    for d in range(dp_size):
        for z in range(GROUP):
            to_d, to_z = target(d, z)
            pairs.append((d * GROUP + z, to_d * GROUP + to_z))
    return lax.ppermute(array, AXES, pairs)


def swap_dp(array, dp_size, mask):
    return permute(array, dp_size, lambda d, z: (d ^ mask, z))


def swap_z(array, dp_size, mask):
    return permute(array, dp_size, lambda d, z: (d, z ^ mask))


def to_group(array, dp_size):
    return permute(array, dp_size, lambda d, z: (d // GROUP * GROUP + z, PLANE_OF[d % GROUP]))


def from_group(array, dp_size):
    return permute(array, dp_size, lambda d, z: (d // GROUP * GROUP + SEQ_OF[z], d % GROUP))


def reorder(array, index):
    count = array.shape[0]
    for k in range(count.bit_length() - 1):
        pairs = array.reshape(count >> (k + 1), 2, 1 << k, *array.shape[1:])
        pairs = jnp.concatenate([pairs[:, 1:], pairs[:, :1]], axis=1).reshape(array.shape)
        array = jnp.where((index >> k) % 2 == 1, pairs, array)
    return array


def seq_of(plane):
    return jnp.where(plane == 0, 0, jnp.where(plane == 3, 1, plane + 1))


def gather_dp(array, dp_size, me):
    if dp_size != 8:
        return lax.all_gather(array, "dp", axis=0, tiled=False)
    blocks = [array] + [swap_dp(array, dp_size, k) for k in range(1, 8)]
    return reorder(jnp.stack(blocks), me)


def place_kernel(where_ref, own, x, y, d0, d1, c_own, c_x, c_y, c_d0, c_d1, out, sems):
    rows = own.shape[1]
    me, slot = where_ref[0], where_ref[1]
    copies = []
    for ref, rel, first in (
        (own, 0, 0),
        (x, 2, 0),
        (y, 4, 0),
        (d0, 6, 0),
        (d1, 6, 2),
        (c_own, 1, 0),
        (c_x, 3, 0),
        (c_y, 5, 0),
        (c_d0, 7, 0),
        (c_d1, 7, 2),
    ):
        start = pl.multiple_of((me ^ rel) * rows, rows)
        for t in range(ref.shape[0]):
            copy = pltpu.make_async_copy(
                ref.at[t], out.at[(first + t) ^ slot, pl.ds(start, rows)], sems.at[len(copies)]
            )
            copy.start()
            copies.append(copy)
    for copy in copies:
        copy.wait()


def gather_weights(shard, dp_size, me, slot):
    rows, columns = shard.shape
    if dp_size != 8:
        full = lax.all_gather(shard, "dp", axis=0, tiled=True)
        full = jnp.stack([full] + [swap_z(full, dp_size, t) for t in range(1, GROUP)])
        return reorder(full, slot)
    own = jnp.stack([shard] + [swap_z(shard, dp_size, t) for t in range(1, GROUP)])
    x = swap_dp(own, dp_size, 2)
    y = swap_dp(own, dp_size, 4)
    d0 = swap_dp(x[:2], dp_size, 4)
    d1 = swap_dp(y[2:], dp_size, 2)
    near = (own, x, y, d0, d1)
    far = tuple(swap_dp(piece, dp_size, 1) for piece in near)
    return pl.pallas_call(
        place_kernel,
        out_shape=jax.ShapeDtypeStruct((GROUP, dp_size * rows, columns), shard.dtype),
        in_specs=[pl.BlockSpec(memory_space=pltpu.SMEM)] + [pl.BlockSpec(memory_space=pl.ANY)] * 10,
        out_specs=pl.BlockSpec(memory_space=pltpu.VMEM),
        scratch_shapes=[pltpu.SemaphoreType.DMA((32,))],
        compiler_params=pltpu.CompilerParams(vmem_limit_bytes=24 << 20),
        name="place",
    )(jnp.stack([me, slot]).astype(jnp.int32), *near, *far)


def spread_kernel(where_ref, grad, out, sems):
    rows = out.shape[2]
    me, slot = where_ref[0], where_ref[1]
    copies = []
    for k, rel in enumerate((0, 2, 4, 6, 1, 3, 5, 7)):
        start = pl.multiple_of((me ^ rel) * rows, rows)
        for t in range(GROUP):
            copy = pltpu.make_async_copy(
                grad.at[t ^ slot, pl.ds(start, rows)], out.at[k, t], sems.at[len(copies)]
            )
            copy.start()
            copies.append(copy)
    for copy in copies:
        copy.wait()


def plus(a, b):
    return (a.astype(f32) + b.astype(f32)).astype(bf16)


def reduce_weights(grad, dp_size, me, slot):
    columns = grad.shape[2]
    rows = grad.shape[1] // dp_size
    if dp_size != 8:
        grad = reorder(grad, slot)
        grad = lax.psum_scatter(grad, "dp", scatter_dimension=1, tiled=True)
        total = grad[0].astype(f32)
        for t in range(1, GROUP):
            total = total + swap_z(grad[t], dp_size, t).astype(f32)
        return total
    parts = pl.pallas_call(
        spread_kernel,
        out_shape=jax.ShapeDtypeStruct((8, GROUP, rows, columns), grad.dtype),
        in_specs=[
            pl.BlockSpec(memory_space=pltpu.SMEM),
            pl.BlockSpec(memory_space=pltpu.VMEM),
        ],
        out_specs=pl.BlockSpec(memory_space=pl.ANY),
        scratch_shapes=[pltpu.SemaphoreType.DMA((32,))],
        compiler_params=pltpu.CompilerParams(vmem_limit_bytes=24 << 20),
        name="spread",
    )(jnp.stack([me, slot]).astype(jnp.int32), grad)
    far = swap_dp(parts[4:], dp_size, 1)
    diagonal = plus(parts[3], far[3])
    from_x = swap_dp(diagonal[:2], dp_size, 2)
    from_y = swap_dp(diagonal[2:], dp_size, 4)
    x = parts[1].astype(f32) + far[1].astype(f32)
    y = parts[2].astype(f32) + far[2].astype(f32)
    x = jnp.concatenate([x[:2], x[2:] + from_y.astype(f32)]).astype(bf16)
    y = jnp.concatenate([y[:2] + from_x.astype(f32), y[2:]]).astype(bf16)
    from_x = swap_dp(x, dp_size, 2)
    from_y = swap_dp(y, dp_size, 4)
    own = (
        parts[0].astype(f32) + far[0].astype(f32) + from_x.astype(f32) + from_y.astype(f32)
    )
    total = own[0]
    for t in range(1, GROUP):
        total = total + swap_z(own[t].astype(bf16), dp_size, t).astype(f32)
    return total


def attend_kernel(a0, a1, a2, a3, o0, o1, o2, o3, lse, key_t, value_t, key):
    pieces = (a0, a1, a2, a3)
    block = a0.shape[1]
    for i, piece in enumerate(pieces):
        columns = slice(i * block, (i + 1) * block)
        key_t[:, columns] = piece[HEAD_DIM : 2 * HEAD_DIM]
        value_t[:, columns] = piece[2 * HEAD_DIM :]
    key[...] = key_t[...].T
    for i, (piece, out) in enumerate(zip(pieces, (o0, o1, o2, o3))):
        query = piece[:HEAD_DIM] * bf16(HEAD_DIM**-0.5)
        scores = jnp.dot(key[...], query, preferred_element_type=f32)
        highest = jnp.max(scores, axis=0, keepdims=True)
        exponent = jnp.exp(scores - highest)
        totals = jnp.sum(exponent, axis=0, keepdims=True)
        mixture = jnp.dot(value_t[...], exponent.astype(bf16), preferred_element_type=f32)
        out[...] = (mixture / totals).astype(bf16)
        lse[i : i + 1, :] = highest + jnp.log(totals)


def attend(pieces):
    block = pieces[0].shape[1]
    length = GROUP * block
    vmem = pl.BlockSpec(memory_space=pltpu.VMEM)
    *outs, lse = pl.pallas_call(
        attend_kernel,
        out_shape=[jax.ShapeDtypeStruct((HEAD_DIM, block), bf16)] * GROUP
        + [jax.ShapeDtypeStruct((GROUP, block), f32)],
        in_specs=[vmem] * GROUP,
        out_specs=[vmem] * (GROUP + 1),
        scratch_shapes=[
            pltpu.VMEM((HEAD_DIM, length), bf16),
            pltpu.VMEM((HEAD_DIM, length), bf16),
            pltpu.VMEM((length, HEAD_DIM), bf16),
        ],
        compiler_params=pltpu.CompilerParams(vmem_limit_bytes=40 << 20),
        cost_estimate=pl.CostEstimate(
            flops=16 * length * length * HEAD_DIM,
            bytes_accessed=2 * 4 * length * HEAD_DIM,
            transcendentals=length * length,
        ),
        name="attend",
    )(*pieces)
    return outs, lse


def attend_back_kernel(*refs):
    pieces, grads = refs[0:4], refs[4:8]
    lse, cosine, sine = refs[8:11]
    outs = refs[11:15]
    key_t, key, value_t, query_grad, key_grad, value_grad = refs[15:]
    block = pieces[0].shape[1]
    rows = min(256, block)
    for i, piece in enumerate(pieces):
        columns = slice(i * block, (i + 1) * block)
        key_t[:, columns] = piece[HEAD_DIM : 2 * HEAD_DIM]
        value_t[:, columns] = piece[2 * HEAD_DIM :]
        key[columns, :] = piece[HEAD_DIM : 2 * HEAD_DIM].T
    for i, (piece, grad) in enumerate(zip(pieces, grads)):
        log_total = lse[i : i + 1, :].T
        for c in range(block // rows):
            at = slice(c * rows, (c + 1) * rows)
            query_t = piece[:HEAD_DIM, at] * bf16(HEAD_DIM**-0.5)
            grad_t = grad[:, at]
            scores = jnp.dot(query_t.T, key_t[...], preferred_element_type=f32)
            weights = jnp.exp(scores - log_total[at])
            pull = jnp.dot(grad_t.T, value_t[...], preferred_element_type=f32)
            centre = jnp.sum(weights * pull, axis=1, keepdims=True)
            score_grad = (weights * (pull - centre)).astype(bf16)
            value_term = jnp.dot(grad_t, weights.astype(bf16), preferred_element_type=f32)
            key_term = jnp.dot(query_t, score_grad, preferred_element_type=f32)
            if i == 0 and c == 0:
                value_grad[...] = value_term
                key_grad[...] = key_term
            else:
                value_grad[...] += value_term
                key_grad[...] += key_term
            query_grad[:, i * block + c * rows : i * block + (c + 1) * rows] = (
                jnp.dot(score_grad, key[...], preferred_element_type=f32) * HEAD_DIM**-0.5
            ).T
    half = HEAD_DIM // 2
    for i, out in enumerate(outs):
        columns = slice(i * block, (i + 1) * block)
        cos, sin = cosine[:, columns], sine[:, columns]
        for first, source in ((0, query_grad), (HEAD_DIM, key_grad)):
            upper, lower = source[:half, columns], source[half:, columns]
            out[first : first + half] = (upper * cos + lower * sin).astype(bf16)
            out[first + half : first + HEAD_DIM] = (lower * cos - upper * sin).astype(bf16)
        out[2 * HEAD_DIM :] = value_grad[:, columns].astype(bf16)


def attend_back(pieces, grads, lse, cosine, sine):
    block = pieces[0].shape[1]
    length = GROUP * block
    vmem = pl.BlockSpec(memory_space=pltpu.VMEM)
    return pl.pallas_call(
        attend_back_kernel,
        out_shape=[jax.ShapeDtypeStruct((3 * HEAD_DIM, block), bf16)] * GROUP,
        in_specs=[vmem] * 11,
        out_specs=[vmem] * GROUP,
        scratch_shapes=[
            pltpu.VMEM((HEAD_DIM, length), bf16),
            pltpu.VMEM((length, HEAD_DIM), bf16),
            pltpu.VMEM((HEAD_DIM, length), bf16),
            pltpu.VMEM((HEAD_DIM, length), f32),
            pltpu.VMEM((HEAD_DIM, length), f32),
            pltpu.VMEM((HEAD_DIM, length), f32),
        ],
        compiler_params=pltpu.CompilerParams(vmem_limit_bytes=48 << 20),
        cost_estimate=pl.CostEstimate(
            flops=40 * length * length * HEAD_DIM,
            bytes_accessed=2 * 8 * length * HEAD_DIM,
            transcendentals=length * length,
        ),
        name="attend_back",
    )(*pieces, *grads, lse, cosine, sine)


def normalize(rows):
    center = jnp.mean(rows, axis=1, keepdims=True)
    shifted = rows - center
    inverse = lax.rsqrt(jnp.mean(shifted * shifted, axis=1, keepdims=True) + EPSILON)
    return shifted * inverse, inverse


def norm_back(scaled, normed, inverse):
    return inverse * (
        scaled
        - jnp.mean(scaled, axis=1, keepdims=True)
        - normed * jnp.mean(scaled * normed, axis=1, keepdims=True)
    )


def gelu_tanh(values):
    return jax.nn.gelu(values, approximate=True)


def einsum(spec, a, b):
    return jnp.einsum(spec, a, b, preferred_element_type=f32)


def per_device(
    dp_size,
    tokens,
    time_embed,
    ada_weight,
    ada_bias,
    norm1_gain,
    qkv_weight,
    out_weight,
    norm2_gain,
    up_weight,
    up_bias,
    down_weight,
    down_bias,
    out_grad,
):
    me = lax.axis_index("dp")
    z = lax.axis_index("tensor")
    position = me % GROUP
    rows, width = tokens.shape
    heads = qkv_weight.shape[2] // HEAD_DIM
    wide = heads * HEAD_DIM
    hidden = up_weight.shape[1]
    cond = time_embed.shape[1]

    first_shard = jnp.concatenate([*qkv_weight, out_weight.T], axis=1)
    second_shard = jnp.concatenate([up_weight, down_weight.T], axis=1)
    first_full = gather_weights(first_shard, dp_size, me, position)
    second_full = gather_weights(second_shard, dp_size, me, jnp.int32(0))
    qkv_full, out_full = first_full[:, :, : 3 * wide], first_full[:, :, 3 * wide :]
    up_full, down_full = second_full[:, :, :hidden], second_full[:, :, hidden:]

    moved = to_group(tokens, dp_size)
    upstream = to_group(out_grad, dp_size).astype(f32)

    per = norm1_gain.shape[0]
    lanes = max(per, cond, up_bias.shape[0])

    def fit(row):
        return jnp.pad(row, (0, lanes - row.shape[0]))

    small = jnp.stack(
        [fit(time_embed[0]), fit(norm1_gain), fit(norm2_gain), fit(down_bias), fit(up_bias)]
    )
    small = gather_dp(small, dp_size, me)
    embeds = small[:, 0, :cond]
    gain_one = small[:, 1, :per].reshape(1, width).astype(f32)
    gain_two = small[:, 2, :per].reshape(1, width).astype(f32)
    bias_down = small[:, 3, :per].reshape(1, width).astype(f32)
    bias_up = small[:, 4, : up_bias.shape[0]].reshape(1, hidden)
    bias_up = jnp.stack([bias_up] + [swap_z(bias_up, dp_size, t) for t in range(1, GROUP)])
    bias_up = bias_up.astype(f32)
    slices = einsum("sc,ce->se", embeds, ada_weight) + ada_bias.astype(f32)
    sequence = me // GROUP * GROUP + seq_of(z)
    modulation = gather_dp(slices, dp_size, me)
    modulation = lax.dynamic_index_in_dim(modulation, sequence, 1).reshape(6, 1, width)
    shift_one, scale_one, gate_one, shift_two, scale_two, gate_two = modulation
    ada_full = gather_dp(ada_weight, dp_size, me)

    half = HEAD_DIM // 2
    frequency = jnp.exp(
        jnp.arange(half, dtype=f32) * (-2.0 * math.log(ROPE_BASE) / HEAD_DIM)
    )
    quarter = position ^ jnp.arange(GROUP, dtype=jnp.int32)
    places = (quarter[:, None] * rows + jnp.arange(rows, dtype=jnp.int32)[None, :]).reshape(-1)
    angles = frequency[:, None] * places.astype(f32)[None, :]
    cosine, sine = jnp.cos(angles), jnp.sin(angles)

    inputs = moved.astype(f32)
    normed_one, inverse_one = normalize(inputs)
    factor_one = gain_one * (1.0 + scale_one)
    hidden_one = (normed_one * gain_one * (1.0 + scale_one) + shift_one).astype(bf16)
    projected = einsum("ld,tdc->tcl", hidden_one, qkv_full)
    projected = projected.reshape(GROUP, 3, heads, 2, half, rows)
    cos_own, sin_own = cosine[:, :rows], sine[:, :rows]
    upper, lower = projected[:, :2, :, 0], projected[:, :2, :, 1]
    rotated = jnp.stack(
        [upper * cos_own - lower * sin_own, lower * cos_own + upper * sin_own], axis=3
    )
    packed = jnp.concatenate([rotated, projected[:, 2:]], axis=1).astype(bf16)
    packed = packed.transpose(0, 2, 1, 3, 4, 5).reshape(GROUP, heads, 3 * HEAD_DIM, rows)

    def exchange(blocks):
        return [blocks[0]] + [swap_dp(blocks[r], dp_size, r) for r in range(1, GROUP)]

    saved, mixtures = [], []
    for h in range(heads):
        pieces = exchange([packed[r, h] for r in range(GROUP)])
        outs, lse = attend(pieces)
        saved.append((pieces, lse))
        mixtures.append(exchange(outs))
    attention = jnp.stack(
        [jnp.concatenate([mixtures[h][r] for h in range(heads)]) for r in range(GROUP)]
    )
    branch_one = einsum("rfl,rdf->ld", attention, out_full)

    residual = inputs + gate_one * branch_one
    normed_two, inverse_two = normalize(residual)
    hidden_two = (normed_two * gain_two * (1.0 + scale_two) + shift_two).astype(bf16)
    pre = einsum("ld,tdf->tlf", hidden_two, up_full) + bias_up
    activated = gelu_tanh(pre).astype(bf16)
    branch_two = einsum("tlf,tdf->ld", activated, down_full) + bias_down
    output = (residual + gate_two * branch_two).astype(bf16)
    output = from_group(output, dp_size)

    branch_two_grad = (gate_two * upstream).astype(bf16)
    act_grad = einsum("ld,tdf->tlf", branch_two_grad, down_full)
    pre_grad = jax.vjp(gelu_tanh, pre)[1](act_grad)[0].astype(bf16)
    hidden_two_grad = einsum("tlf,tdf->ld", pre_grad, up_full)
    factor_two = gain_two * (1.0 + scale_two)
    residual_grad = upstream + norm_back(hidden_two_grad * factor_two, normed_two, inverse_two)
    branch_one_grad = (gate_one * residual_grad).astype(bf16)
    attention_grad = einsum("ld,rdf->rfl", branch_one_grad, out_full).astype(bf16)

    up_grad = einsum("ld,tlf->tdf", hidden_two, pre_grad)
    down_grad = einsum("ld,tlf->tdf", branch_two_grad, activated)
    second_grad = jnp.concatenate([up_grad, down_grad], axis=2).astype(bf16)
    second_sum = reduce_weights(second_grad, dp_size, me, jnp.int32(0))
    up_out, down_out = second_sum[:, :hidden], second_sum[:, hidden:].T

    received = []
    for h in range(heads):
        pieces, lse = saved[h]
        grads = exchange(
            [attention_grad[r, h * HEAD_DIM : (h + 1) * HEAD_DIM] for r in range(GROUP)]
        )
        outs = attend_back(pieces, grads, lse, cosine, sine)
        received.append(exchange(outs))
    projected_grad = jnp.stack(
        [
            jnp.stack([received[h][r].reshape(3, HEAD_DIM, rows) for h in range(heads)], axis=1)
            for r in range(GROUP)
        ]
    ).reshape(GROUP, 3 * wide, rows)
    qkv_grad = einsum("ld,rcl->rdc", hidden_one, projected_grad)
    out_weight_grad = einsum("ld,rfl->rdf", branch_one_grad, attention)
    first_grad = jnp.concatenate([qkv_grad, out_weight_grad], axis=2).astype(bf16)
    first_sum = reduce_weights(first_grad, dp_size, me, position)
    qkv_out = jnp.stack(jnp.split(first_sum[:, : 3 * wide], 3, axis=1))
    out_out = first_sum[:, 3 * wide :].T

    hidden_one_grad = einsum("rcl,rdc->ld", projected_grad, qkv_full)
    input_grad = (
        residual_grad + norm_back(hidden_one_grad * factor_one, normed_one, inverse_one)
    ).astype(bf16)
    input_grad = from_group(input_grad, dp_size)

    def total(values):
        return jnp.sum(values, axis=0, keepdims=True)

    pull_one = total(hidden_one_grad * normed_one)
    pull_two = total(hidden_two_grad * normed_two)
    mine = jnp.concatenate(
        [
            total(hidden_one_grad),
            pull_one * gain_one,
            total(residual_grad * branch_one),
            total(hidden_two_grad),
            pull_two * gain_two,
            total(upstream * branch_two),
            pull_one * (1.0 + scale_one),
            pull_two * (1.0 + scale_two),
            total(branch_two_grad.astype(f32)),
            jnp.sum(pre_grad.astype(f32), axis=1).reshape(-1, width),
        ]
    )
    for_group = mine
    for r in range(1, GROUP):
        for_group = for_group + swap_dp(mine, dp_size, r)
    mod_grad = for_group[:6].astype(bf16).astype(f32)
    sums = for_group[6:9]
    bias_rows = for_group[9:].reshape(GROUP, -1, width)
    mods = [mod_grad]
    bias_sum = bias_rows[0]
    vector_sums = sums
    for t in range(1, GROUP):
        other = swap_z(jnp.concatenate([mod_grad, sums, bias_rows[t]]), dp_size, t)
        mods.append(other[:6])
        vector_sums = vector_sums + other[6:9]
        bias_sum = bias_sum + other[9:]
    mods = jnp.stack(mods)
    state = jnp.concatenate([mods.reshape(-1, width), vector_sums, bias_sum])
    quads = dp_size // GROUP
    if quads == 2:
        other = swap_dp(state, dp_size, GROUP)
        states = jnp.stack([state, other])
        quad_at = (me // GROUP) ^ jnp.arange(2)
    else:
        states = lax.all_gather(state, "dp", axis=0, tiled=False)
        states = states.reshape(quads, GROUP, *state.shape)
        states = lax.dynamic_index_in_dim(states, position, 1, keepdims=False)
        quad_at = jnp.arange(quads)
    tail = jnp.sum(states[:, 6 * GROUP :], axis=0)
    all_mods = states[:, : 6 * GROUP].reshape(quads * GROUP, 6 * width).astype(bf16)
    seq_at = seq_of(z ^ jnp.arange(GROUP))
    seq_at = (quad_at[:, None] * GROUP + seq_at[None, :]).reshape(-1)
    columns = ada_weight.shape[1]
    own_mods = lax.dynamic_slice_in_dim(all_mods, me * columns, columns, axis=1)
    pick = (seq_at[:, None] == jnp.arange(dp_size)[None, :]).astype(bf16)
    ada_out = einsum("sc,se->ce", jnp.dot(pick, embeds), own_mods)
    ada_bias_out = jnp.sum(own_mods.astype(f32), axis=0)
    mine_at = (seq_at == me).astype(f32)
    own_row = jnp.sum(all_mods.astype(f32) * mine_at[:, None], axis=0).astype(bf16)
    time_out = einsum("oe,oce->oc", own_row.reshape(dp_size, columns), ada_full)
    time_out = jnp.sum(time_out, axis=0, keepdims=True)

    def own_part(row):
        return lax.dynamic_slice_in_dim(row, me * per, per)

    bias_up_out = lax.dynamic_slice_in_dim(
        tail[3:].reshape(-1), me * up_bias.shape[0], up_bias.shape[0]
    )
    return (
        output,
        input_grad,
        time_out,
        ada_out,
        ada_bias_out,
        own_part(tail[0]),
        qkv_out,
        out_out,
        own_part(tail[1]),
        up_out,
        bias_up_out,
        down_out,
        own_part(tail[2]),
    )


def solution(mesh):
    placed = (
        P(("dp", "tensor"), None),
        P("dp", None),
        P(None, "dp"),
        P("dp"),
        P("dp"),
        P(None, "dp", "tensor"),
        P("tensor", "dp"),
        P("dp"),
        P("dp", "tensor"),
        P(("tensor", "dp")),
        P("tensor", "dp"),
        P("dp"),
        P(("dp", "tensor"), None),
    )
    return jax.shard_map(
        functools.partial(per_device, mesh.shape["dp"]),
        mesh=mesh,
        in_specs=placed,
        out_specs=(
            P(("dp", "tensor"), None),
            P(("dp", "tensor"), None),
            P("dp", None),
            P(None, "dp"),
            P("dp"),
            P("dp"),
            P(None, "dp", "tensor"),
            P("tensor", "dp"),
            P("dp"),
            P("dp", "tensor"),
            P(("tensor", "dp")),
            P("tensor", "dp"),
            P("dp"),
        ),
        check_vma=False,
    )
```

```python
import functools
import math

import jax
import jax.numpy as jnp
from jax import lax
from jax.experimental import pallas as pl
from jax.experimental.pallas import tpu as pltpu
from jax.sharding import PartitionSpec as P

HEAD_DIM = 64
EPSILON = 1e-05
ROPE_BASE = 10000.0
GROUP = 4
AXES = ("dp", "tensor")
f32 = jnp.float32
bf16 = jnp.bfloat16


def permute(array, dp_size, target):
    pairs = []
    for d in range(dp_size):
        for z in range(GROUP):
            to_d, to_z = target(d, z)
            pairs.append((d * GROUP + z, to_d * GROUP + to_z))
    return lax.ppermute(array, AXES, pairs)


def swap_dp(array, dp_size, mask):
    return permute(array, dp_size, lambda d, z: (d ^ mask, z))


def swap_z(array, dp_size, mask):
    return permute(array, dp_size, lambda d, z: (d, z ^ mask))


def swap_peer(array, dp_size, r):
    return permute(array, dp_size, lambda d, z: (d ^ (r >> 1), z ^ (r & 1)))


def regroup(array, dp_size):
    return permute(
        array, dp_size, lambda d, z: (d // 2 * 2 + z // 2, d % 2 * 2 + z % 2)
    )


def tie(arrays, *after):
    return lax.optimization_barrier((arrays, after))[0]


def reorder(array, index):
    count = array.shape[0]
    for k in range(count.bit_length() - 1):
        pairs = array.reshape(count >> (k + 1), 2, 1 << k, *array.shape[1:])
        pairs = jnp.concatenate([pairs[:, 1:], pairs[:, :1]], axis=1).reshape(array.shape)
        array = jnp.where((index >> k) % 2 == 1, pairs, array)
    return array


def gather_dp(array, dp_size):
    blocks = array[None]
    mask = 1
    while mask < dp_size:
        blocks = jnp.concatenate([blocks, swap_dp(blocks, dp_size, mask)])
        mask *= 2
    return blocks


PIECES = (
    (0, 0),
    (2, 0),
    (4, 0),
    (6, 0),
    (6, 2),
    (1, 0),
    (3, 0),
    (5, 0),
    (7, 0),
    (7, 2),
)


def stack_planes(shard, dp_size):
    return jnp.stack([shard] + [swap_z(shard, dp_size, t) for t in range(1, GROUP)])


def gather_weights(own, dp_size):
    if dp_size != 8:
        return (lax.all_gather(own, "dp", axis=1, tiled=True),)
    x = swap_dp(own, dp_size, 2)
    y = swap_dp(own, dp_size, 4)
    d0 = swap_dp(x[:2], dp_size, 4)
    d1 = swap_dp(y[2:], dp_size, 2)
    near = (own, x, y, d0, d1)
    return near + tuple(swap_dp(piece, dp_size, 1) for piece in near)


def load_weights(me, pieces, full, sems):
    if len(pieces) == 1:
        copies = [pltpu.make_async_copy(pieces[0], full, sems.at[0])]
    else:
        copies = []
        for i, (piece, (rel, first)) in enumerate(zip(pieces, PIECES)):
            count, rows = piece.shape[:2]
            start = pl.multiple_of((me ^ rel) * rows, rows)
            place = full.at[first : first + count, pl.ds(start, rows)]
            copies.append(pltpu.make_async_copy(piece, place, sems.at[i]))
    for copy in copies:
        copy.start()
    return copies


def store_blocks(me, outs, slot, value):
    if len(outs) == 1:
        outs[0][slot] = value
        return
    rows = outs[0].shape[2]
    for owner in range(2 * outs[0].shape[0]):
        rel = me ^ owner
        for parity, out in enumerate(outs):

            @pl.when((rel & 1) == parity)
            def _():
                out[rel >> 1, slot] = value[owner * rows : (owner + 1) * rows]


def grad_shapes(dp_size, width, columns):
    if dp_size != 8:
        return [jax.ShapeDtypeStruct((GROUP, width, columns), bf16)]
    return [jax.ShapeDtypeStruct((dp_size // 2, GROUP, width // dp_size, columns), bf16)] * 2


def plus(a, b):
    return (a.astype(f32) + b.astype(f32)).astype(bf16)


def reduce_cores(parts, dp_size):
    return swap_dp(parts[1], dp_size, 1) if dp_size == 8 else None


def reduce_first(parts, far, dp_size):
    if dp_size != 8:
        return None
    diagonal = plus(parts[0][3], far[3])
    return swap_dp(diagonal[:2], dp_size, 2), swap_dp(diagonal[2:], dp_size, 4)


def reduce_second(parts, far, half, dp_size):
    if dp_size != 8:
        total = lax.psum_scatter(parts[0], "dp", scatter_dimension=1, tiled=True)
        return total.astype(f32)
    near = parts[0]
    x = near[1].astype(f32) + far[1].astype(f32)
    y = near[2].astype(f32) + far[2].astype(f32)
    x = jnp.concatenate([x[:2], x[2:] + half[1].astype(f32)]).astype(bf16)
    y = jnp.concatenate([y[:2] + half[0].astype(f32), y[2:]]).astype(bf16)
    from_x = swap_dp(x, dp_size, 2)
    from_y = swap_dp(y, dp_size, 4)
    own = near[0].astype(f32) + far[0].astype(f32)
    return own + from_x.astype(f32) + from_y.astype(f32)


def reduce_planes(own, dp_size):
    total = own[0]
    for t in range(1, GROUP):
        total = total + swap_z(own[t].astype(bf16), dp_size, t).astype(f32)
    return total


def attend_kernel(a0, a1, a2, a3, o0, o1, o2, o3, lse, key_t, value_t, key):
    pieces = (a0, a1, a2, a3)
    block = a0.shape[1]
    for h in range(a0.shape[0] // (3 * HEAD_DIM)):
        at = 3 * HEAD_DIM * h
        for i, piece in enumerate(pieces):
            columns = slice(i * block, (i + 1) * block)
            key_t[:, columns] = piece[at + HEAD_DIM : at + 2 * HEAD_DIM]
            value_t[:, columns] = piece[at + 2 * HEAD_DIM : at + 3 * HEAD_DIM]
        key[...] = key_t[...].T
        for i, (piece, out) in enumerate(zip(pieces, (o0, o1, o2, o3))):
            query = piece[at : at + HEAD_DIM] * bf16(HEAD_DIM**-0.5)
            scores = jnp.dot(key[...], query, preferred_element_type=f32)
            highest = jnp.max(scores, axis=0, keepdims=True)
            exponent = jnp.exp(scores - highest)
            totals = jnp.sum(exponent, axis=0, keepdims=True)
            mixture = jnp.dot(value_t[...], exponent.astype(bf16), preferred_element_type=f32)
            out[h * HEAD_DIM : (h + 1) * HEAD_DIM] = (mixture / totals).astype(bf16)
            lse[h * GROUP + i : h * GROUP + i + 1, :] = highest + jnp.log(totals)


def attend(pieces):
    block = pieces[0].shape[1]
    heads = pieces[0].shape[0] // (3 * HEAD_DIM)
    length = GROUP * block
    vmem = pl.BlockSpec(memory_space=pltpu.VMEM)
    *outs, lse = pl.pallas_call(
        attend_kernel,
        out_shape=[jax.ShapeDtypeStruct((heads * HEAD_DIM, block), bf16)] * GROUP
        + [jax.ShapeDtypeStruct((heads * GROUP, block), f32)],
        in_specs=[vmem] * GROUP,
        out_specs=[vmem] * (GROUP + 1),
        scratch_shapes=[
            pltpu.VMEM((HEAD_DIM, length), bf16),
            pltpu.VMEM((HEAD_DIM, length), bf16),
            pltpu.VMEM((length, HEAD_DIM), bf16),
        ],
        compiler_params=pltpu.CompilerParams(vmem_limit_bytes=40 << 20),
        cost_estimate=pl.CostEstimate(
            flops=16 * heads * length * length * HEAD_DIM,
            bytes_accessed=8 * heads * length * HEAD_DIM,
            transcendentals=heads * length * length,
        ),
        name="attend",
    )(*pieces)
    return outs, lse


def attend_back_kernel(*refs):
    pieces, grads = refs[0:4], refs[4:8]
    lse, cosine, sine = refs[8:11]
    outs = refs[11:15]
    key_t, key, value_t, query_grad, key_grad, value_grad = refs[15:]
    block = pieces[0].shape[1]
    rows = min(256, block)
    half = HEAD_DIM // 2
    for h in range(grads[0].shape[0] // HEAD_DIM):
        at = 3 * HEAD_DIM * h
        for i, piece in enumerate(pieces):
            columns = slice(i * block, (i + 1) * block)
            key_t[:, columns] = piece[at + HEAD_DIM : at + 2 * HEAD_DIM]
            value_t[:, columns] = piece[at + 2 * HEAD_DIM : at + 3 * HEAD_DIM]
            key[columns, :] = piece[at + HEAD_DIM : at + 2 * HEAD_DIM].T
        for i, (piece, grad) in enumerate(zip(pieces, grads)):
            log_total = lse[h * GROUP + i : h * GROUP + i + 1, :].T
            for c in range(block // rows):
                own = slice(c * rows, (c + 1) * rows)
                query_t = piece[at : at + HEAD_DIM, own] * bf16(HEAD_DIM**-0.5)
                grad_t = grad[h * HEAD_DIM : (h + 1) * HEAD_DIM, own]
                scores = jnp.dot(query_t.T, key_t[...], preferred_element_type=f32)
                weights = jnp.exp(scores - log_total[own])
                pull = jnp.dot(grad_t.T, value_t[...], preferred_element_type=f32)
                centre = jnp.sum(weights * pull, axis=1, keepdims=True)
                score_grad = (weights * (pull - centre)).astype(bf16)
                value_term = jnp.dot(grad_t, weights.astype(bf16), preferred_element_type=f32)
                key_term = jnp.dot(query_t, score_grad, preferred_element_type=f32)
                if i == 0 and c == 0:
                    value_grad[...] = value_term
                    key_grad[...] = key_term
                else:
                    value_grad[...] += value_term
                    key_grad[...] += key_term
                query_grad[:, i * block + c * rows : i * block + (c + 1) * rows] = (
                    jnp.dot(score_grad, key[...], preferred_element_type=f32) * HEAD_DIM**-0.5
                ).T
        for i, out in enumerate(outs):
            columns = slice(i * block, (i + 1) * block)
            cos, sin = cosine[:, columns], sine[:, columns]
            for first, source in ((at, query_grad), (at + HEAD_DIM, key_grad)):
                upper, lower = source[:half, columns], source[half:, columns]
                out[first : first + half] = (upper * cos + lower * sin).astype(bf16)
                out[first + half : first + HEAD_DIM] = (lower * cos - upper * sin).astype(bf16)
            out[at + 2 * HEAD_DIM : at + 3 * HEAD_DIM] = value_grad[:, columns].astype(bf16)


def attend_back(pieces, grads, lse, cosine, sine):
    block = pieces[0].shape[1]
    heads = pieces[0].shape[0] // (3 * HEAD_DIM)
    length = GROUP * block
    vmem = pl.BlockSpec(memory_space=pltpu.VMEM)
    return pl.pallas_call(
        attend_back_kernel,
        out_shape=[jax.ShapeDtypeStruct((heads * 3 * HEAD_DIM, block), bf16)] * GROUP,
        in_specs=[vmem] * 11,
        out_specs=[vmem] * GROUP,
        scratch_shapes=[
            pltpu.VMEM((HEAD_DIM, length), bf16),
            pltpu.VMEM((length, HEAD_DIM), bf16),
            pltpu.VMEM((HEAD_DIM, length), bf16),
            pltpu.VMEM((HEAD_DIM, length), f32),
            pltpu.VMEM((HEAD_DIM, length), f32),
            pltpu.VMEM((HEAD_DIM, length), f32),
        ],
        compiler_params=pltpu.CompilerParams(vmem_limit_bytes=48 << 20),
        cost_estimate=pl.CostEstimate(
            flops=40 * heads * length * length * HEAD_DIM,
            bytes_accessed=16 * heads * length * HEAD_DIM,
            transcendentals=heads * length * length,
        ),
        name="attend_back",
    )(*pieces, *grads, lse, cosine, sine)


def normalize(rows):
    center = jnp.mean(rows, axis=1, keepdims=True)
    shifted = rows - center
    inverse = lax.rsqrt(jnp.mean(shifted * shifted, axis=1, keepdims=True) + EPSILON)
    return shifted * inverse, inverse


def norm_back(scaled, normed, inverse):
    return inverse * (
        scaled
        - jnp.mean(scaled, axis=1, keepdims=True)
        - normed * jnp.mean(scaled * normed, axis=1, keepdims=True)
    )


def dot(a, b):
    return jnp.dot(a, b, preferred_element_type=f32)


def dot_nt(a, b):
    return lax.dot_general(a, b, (((1,), (1,)), ((), ())), preferred_element_type=f32)


def total(values):
    return jnp.sum(values, axis=0, keepdims=True)


VMEM = pl.BlockSpec(memory_space=pltpu.VMEM)
SMEM = pl.BlockSpec(memory_space=pltpu.SMEM)
ANY = pl.BlockSpec(memory_space=pl.ANY)
HALF = HEAD_DIM // 2


def parts_of(heads):
    return (range(0, 1), range(1, heads)) if heads > 1 else (range(0, 1),)


def project_kernel(count, heads, *refs):
    where, tokens, vectors, cosine, sine = refs[:5]
    pieces, refs = refs[5 : 5 + count], refs[5 + count :]
    parts = parts_of(heads)
    hidden, packed = refs[0], refs[1 : 1 + GROUP * len(parts)]
    full, sems = refs[1 + GROUP * len(parts) :]
    me, base = where[0], where[1]
    wide = heads * HEAD_DIM
    copies = load_weights(me, pieces, full, sems)
    gain, scale, shift = vectors[0:1], vectors[1:2], vectors[2:3]
    normed, _ = normalize(tokens[...].astype(f32))
    hidden[...] = (normed * gain * (1.0 + scale) + shift).astype(bf16)
    cos, sin = cosine[...], sine[...]
    for copy in copies:
        copy.wait()
    for r in range(GROUP):
        projected = dot(hidden[...], full[base ^ r]).T
        for n, part in enumerate(parts):
            out = packed[r * len(parts) + n]
            for i, h in enumerate(part):
                at = 3 * HEAD_DIM * i
                for c in range(2):
                    first = c * wide + h * HEAD_DIM
                    upper = projected[first : first + HALF]
                    lower = projected[first + HALF : first + HEAD_DIM]
                    out[at : at + HALF] = (upper * cos - lower * sin).astype(bf16)
                    out[at + HALF : at + HEAD_DIM] = (lower * cos + upper * sin).astype(bf16)
                    at += HEAD_DIM
                first = 2 * wide + h * HEAD_DIM
                out[at : at + HEAD_DIM] = projected[first : first + HEAD_DIM].astype(bf16)


def project(where, tokens, vectors, cosine, sine, pieces, heads):
    rows, width = tokens.shape
    columns = pieces[0].shape[2]
    parts = parts_of(heads)
    outs = pl.pallas_call(
        functools.partial(project_kernel, len(pieces), heads),
        out_shape=[jax.ShapeDtypeStruct((rows, width), bf16)]
        + [jax.ShapeDtypeStruct((3 * HEAD_DIM * len(part), rows), bf16) for part in parts] * GROUP,
        in_specs=[SMEM] + [VMEM] * 4 + [ANY] * len(pieces),
        out_specs=[VMEM] * (1 + GROUP * len(parts)),
        scratch_shapes=[
            pltpu.VMEM((GROUP, width, columns), bf16),
            pltpu.SemaphoreType.DMA((len(pieces),)),
        ],
        compiler_params=pltpu.CompilerParams(vmem_limit_bytes=32 << 20),
        cost_estimate=pl.CostEstimate(
            flops=2 * rows * width * GROUP * columns,
            bytes_accessed=2 * GROUP * (width + rows) * columns,
            transcendentals=0,
        ),
        name="project",
    )(where, tokens, vectors, cosine, sine, *pieces)
    return outs[0], [outs[1 + n :: len(parts)] for n in range(len(parts))]


GELU_A = math.sqrt(2.0 / math.pi)
GELU_B = 0.044715


def feed_kernel(count, heads, *refs):
    where, tokens, upstream, vectors, bias_up = refs[:5]
    parts = parts_of(heads)
    used = GROUP * len(parts)
    mixtures, refs = refs[5 : 5 + used], refs[5 + used :]
    pieces, refs = refs[:count], refs[count:]
    output, residual_grad, out_hidden, out_branch_one, out_branch_two = refs[:5]
    activated, pre_grad, attention, sums, bias_sums = refs[5:10]
    mixture_grads = refs[10 : 10 + used]
    full, slope, keep_one, keep_two, sems = refs[10 + used :]
    me, base = where[0], where[1]
    wide = heads * HEAD_DIM
    hidden = bias_up.shape[1]
    of_out = slice(0, wide)
    of_up = slice(wide, wide + hidden)
    of_down = slice(wide + hidden, wide + 2 * hidden)
    copies = load_weights(me, pieces, full, sems)
    gain, scale, shift = vectors[0:1], vectors[1:2], vectors[2:3]
    gate_one, gate_two, bias_down = vectors[3:4], vectors[4:5], vectors[5:6]
    for r in range(GROUP):
        own = jnp.concatenate([mixtures[n * GROUP + r][...] for n in range(len(parts))])
        attention[r] = own.T
    for copy in copies:
        copy.wait()
    branch_one = dot_nt(attention[0], full[base, :, of_out])
    for r in range(1, GROUP):
        branch_one = branch_one + dot_nt(attention[r], full[base ^ r, :, of_out])
    keep_one[...] = branch_one
    residual = tokens[...].astype(f32) + gate_one * branch_one
    normed, _ = normalize(residual)
    out_hidden[...] = (normed * gain * (1.0 + scale) + shift).astype(bf16)

    keep_two[...] = jnp.broadcast_to(bias_down, keep_two.shape)

    def forward(t, carry):
        pre = dot(out_hidden[...], full[t, :, of_up]) + bias_up[pl.ds(t, 1)]
        inner = jnp.tanh(GELU_A * (pre + GELU_B * pre * pre * pre))
        activated[t] = (0.5 * pre * (1.0 + inner)).astype(bf16)
        slope[t] = 0.5 * (1.0 + inner) + (
            0.5 * GELU_A * pre * (1.0 - inner * inner) * (1.0 + 3.0 * GELU_B * pre * pre)
        )
        keep_two[...] += dot_nt(activated[t], full[t, :, of_down])
        return carry

    lax.fori_loop(0, GROUP, forward, 0)
    branch_two = keep_two[...]
    residual = tokens[...].astype(f32) + gate_one * keep_one[...]
    output[...] = (residual + gate_two * branch_two).astype(bf16)
    grad = upstream[...].astype(f32)
    branch_two_grad = gate_two * grad
    out_branch_two[...] = branch_two_grad.astype(bf16)
    sums[2:3] = total(grad * branch_two)
    sums[4:5] = total(out_branch_two[...].astype(f32))

    keep_two[...] = jnp.zeros_like(keep_two)

    def backward(t, carry):
        act_grad = dot(out_branch_two[...], full[t, :, of_down])
        pre_grad[t] = (act_grad * slope[t]).astype(bf16)
        bias_sums[pl.ds(t, 1)] = total(pre_grad[t].astype(f32))
        keep_two[...] += dot_nt(pre_grad[t], full[t, :, of_up])
        return carry

    lax.fori_loop(0, GROUP, backward, 0)
    hidden_grad = keep_two[...]
    residual = tokens[...].astype(f32) + gate_one * keep_one[...]
    normed, inverse = normalize(residual)
    sums[0:1] = total(hidden_grad)
    sums[1:2] = total(hidden_grad * normed)
    grad = upstream[...].astype(f32) + norm_back(
        hidden_grad * gain * (1.0 + scale), normed, inverse
    )
    residual_grad[...] = grad
    sums[3:4] = total(grad * keep_one[...])
    out_branch_one[...] = (gate_one * grad).astype(bf16)
    for r in range(GROUP):
        back = dot(out_branch_one[...], full[base ^ r, :, of_out]).astype(bf16).T
        for n, part in enumerate(parts):
            own = slice(part[0] * HEAD_DIM, (part[-1] + 1) * HEAD_DIM)
            mixture_grads[n * GROUP + r][...] = back[own]


def feed(where, tokens, upstream, vectors, bias_up, mixtures, pieces, heads):
    rows, width = tokens.shape
    wide = heads * HEAD_DIM
    hidden = bias_up.shape[1]
    columns = pieces[0].shape[2]
    parts = parts_of(heads)
    count = GROUP * len(parts)

    def shape(dtype, *lengths):
        return jax.ShapeDtypeStruct(lengths, dtype)

    outs = pl.pallas_call(
        functools.partial(feed_kernel, len(pieces), heads),
        out_shape=[
            shape(bf16, rows, width),
            shape(f32, rows, width),
            shape(bf16, rows, width),
            shape(bf16, rows, width),
            shape(bf16, rows, width),
            shape(bf16, GROUP, rows, hidden),
            shape(bf16, GROUP, rows, hidden),
            shape(bf16, GROUP, rows, wide),
            shape(f32, 5, width),
            shape(f32, GROUP, hidden),
        ]
        + [shape(bf16, len(part) * HEAD_DIM, rows) for part in parts for _ in range(GROUP)],
        in_specs=[SMEM] + [VMEM] * (4 + count) + [ANY] * len(pieces),
        out_specs=[VMEM] * (10 + count),
        scratch_shapes=[
            pltpu.VMEM((GROUP, width, columns), bf16),
            pltpu.VMEM((GROUP, rows, hidden), f32),
            pltpu.VMEM((rows, width), f32),
            pltpu.VMEM((rows, width), f32),
            pltpu.SemaphoreType.DMA((len(pieces),)),
        ],
        compiler_params=pltpu.CompilerParams(vmem_limit_bytes=56 << 20),
        cost_estimate=pl.CostEstimate(
            flops=4 * rows * width * GROUP * columns,
            bytes_accessed=2 * GROUP * (width + rows) * columns,
            transcendentals=GROUP * rows * hidden,
        ),
        name="feed",
    )(where, tokens, upstream, vectors, bias_up, *sum(mixtures, []), *pieces)
    grads = outs[10:]
    return outs[:10], [grads[n * GROUP : (n + 1) * GROUP] for n in range(len(parts))]


def feed_grads_kernel(where, hidden, branch_one, branch_two, act, pre, attention, *outs):
    me, base = where[0], where[1]
    t = pl.program_id(0)
    up = dot(hidden[...].T, pre[0]).astype(bf16)
    down = dot(branch_two[...].T, act[0]).astype(bf16)
    own = dot(branch_one[...].T, attention[base ^ t]).astype(bf16)
    store_blocks(me, outs, 0, jnp.concatenate([own, up, down], axis=1))


def feed_grads(dp_size, where, hidden, branch_one, branch_two, act, pre, attention):
    rows, width = hidden.shape
    wide, inner = attention.shape[2], act.shape[2]
    columns = wide + 2 * inner
    shapes = grad_shapes(dp_size, width, columns)
    if dp_size == 8:
        out_spec = pl.BlockSpec((4, 1, width // 8, columns), lambda t: (0, t, 0, 0))
    else:
        out_spec = pl.BlockSpec((1, width, columns), lambda t: (t, 0, 0))
    return pl.pallas_call(
        feed_grads_kernel,
        out_shape=shapes,
        grid=(GROUP,),
        in_specs=[SMEM]
        + [VMEM] * 3
        + [pl.BlockSpec((1, rows, inner), lambda t: (t, 0, 0))] * 2
        + [VMEM],
        out_specs=[out_spec] * len(shapes),
        compiler_params=pltpu.CompilerParams(vmem_limit_bytes=40 << 20),
        cost_estimate=pl.CostEstimate(
            flops=2 * rows * width * GROUP * columns,
            bytes_accessed=2 * GROUP * (width + rows) * columns,
            transcendentals=0,
        ),
        name="feed_grads",
    )(where, hidden, branch_one, branch_two, act, pre, attention)


def join_heads(pieces, heads, r):
    rows = []
    for c in range(3):
        for n, part in enumerate(parts_of(heads)):
            for i in range(len(part)):
                first = (3 * i + c) * HEAD_DIM
                rows.append(pieces[n * GROUP + r][first : first + HEAD_DIM])
    return jnp.concatenate(rows)


def project_grads_kernel(heads, used, where, hidden, *refs):
    pieces, outs = refs[:used], refs[used:]
    me, base = where[0], where[1]
    hidden_t = hidden[...].T
    for r in range(GROUP):
        value = dot_nt(hidden_t, join_heads(pieces, heads, r)).astype(bf16)
        store_blocks(me, outs, base ^ r, value)


def project_grads(dp_size, where, hidden, received, heads):
    rows, width = hidden.shape
    columns = 3 * heads * HEAD_DIM
    received = sum(received, [])
    shapes = grad_shapes(dp_size, width, columns)
    return pl.pallas_call(
        functools.partial(project_grads_kernel, heads, len(received)),
        out_shape=shapes,
        in_specs=[SMEM] + [VMEM] * (1 + len(received)),
        out_specs=[VMEM] * len(shapes),
        compiler_params=pltpu.CompilerParams(vmem_limit_bytes=32 << 20),
        cost_estimate=pl.CostEstimate(
            flops=2 * rows * width * GROUP * columns,
            bytes_accessed=2 * GROUP * (width + rows) * columns,
            transcendentals=0,
        ),
        name="project_grads",
    )(where, hidden, *received)


def project_back_kernel(count, heads, *refs):
    where, tokens, vectors, residual_grad = refs[:4]
    used = GROUP * len(parts_of(heads))
    received, refs = refs[4 : 4 + used], refs[4 + used :]
    pieces, (input_grad, sums, full, sems) = refs[:count], refs[count:]
    me, base = where[0], where[1]
    copies = load_weights(me, pieces, full, sems)
    gain, scale = vectors[0:1], vectors[1:2]
    normed, inverse = normalize(tokens[...].astype(f32))
    for copy in copies:
        copy.wait()
    hidden_grad = None
    for r in range(GROUP):
        term = dot_nt(join_heads(received, heads, r).T, full[base ^ r])
        hidden_grad = term if hidden_grad is None else hidden_grad + term
    sums[0:1] = total(hidden_grad)
    sums[1:2] = total(hidden_grad * normed)
    input_grad[...] = (
        residual_grad[...] + norm_back(hidden_grad * gain * (1.0 + scale), normed, inverse)
    ).astype(bf16)


def project_back(where, tokens, vectors, residual_grad, received, pieces, heads):
    rows, width = tokens.shape
    columns = pieces[0].shape[2]
    received = sum(received, [])
    return pl.pallas_call(
        functools.partial(project_back_kernel, len(pieces), heads),
        out_shape=[
            jax.ShapeDtypeStruct((rows, width), bf16),
            jax.ShapeDtypeStruct((2, width), f32),
        ],
        in_specs=[SMEM] + [VMEM] * (3 + len(received)) + [ANY] * len(pieces),
        out_specs=[VMEM] * 2,
        scratch_shapes=[
            pltpu.VMEM((GROUP, width, columns), bf16),
            pltpu.SemaphoreType.DMA((len(pieces),)),
        ],
        compiler_params=pltpu.CompilerParams(vmem_limit_bytes=32 << 20),
        cost_estimate=pl.CostEstimate(
            flops=2 * rows * width * GROUP * columns,
            bytes_accessed=2 * GROUP * (width + rows) * columns,
            transcendentals=0,
        ),
        name="project_back",
    )(where, tokens, vectors, residual_grad, *received, *pieces)


def einsum(spec, a, b):
    return jnp.einsum(spec, a, b, preferred_element_type=f32)


def per_device(
    dp_size,
    tokens,
    time_embed,
    ada_weight,
    ada_bias,
    norm1_gain,
    qkv_weight,
    out_weight,
    norm2_gain,
    up_weight,
    up_bias,
    down_weight,
    down_bias,
    out_grad,
):
    me = lax.axis_index("dp")
    z = lax.axis_index("tensor")
    position = me % 2 * 2 + z % 2
    base = z ^ position
    where = jnp.stack([me, base]).astype(jnp.int32)
    rows, width = tokens.shape
    heads = qkv_weight.shape[2] // HEAD_DIM
    wide = heads * HEAD_DIM
    hidden = up_weight.shape[1]
    cond = time_embed.shape[1]
    per = norm1_gain.shape[0]

    first_own = stack_planes(jnp.concatenate([*qkv_weight], axis=1), dp_size)
    first_pieces = gather_weights(first_own, dp_size)
    moved = regroup(tie(tokens, first_own), dp_size)
    second_shard = jnp.concatenate([out_weight.T, up_weight, down_weight.T], axis=1)
    second_own = stack_planes(tie(second_shard, moved), dp_size)
    second_pieces = gather_weights(second_own, dp_size)
    upstream = regroup(tie(out_grad, second_own), dp_size)

    lanes = max(per, cond, up_bias.shape[0])

    def fit(row):
        return jnp.pad(row, (0, lanes - row.shape[0]))

    small = jnp.stack(
        [fit(time_embed[0]), fit(norm1_gain), fit(norm2_gain), fit(down_bias), fit(up_bias)]
    )
    small = reorder(gather_dp(small, dp_size), me)
    embeds = small[:, 0, :cond]
    slices = einsum("sc,ce->se", embeds, ada_weight) + ada_bias.astype(f32)
    slices = gather_dp(slices, dp_size)
    sequence = me // 2 * 2 + z // 2
    modulation = reorder(lax.dynamic_index_in_dim(slices, sequence, 1), me).reshape(6, 1, width)
    shift_one, scale_one, gate_one, shift_two, scale_two, gate_two = modulation
    gain_one = small[:, 1, :per].reshape(1, width).astype(f32)
    gain_two = small[:, 2, :per].reshape(1, width).astype(f32)
    bias_down = small[:, 3, :per].reshape(1, width).astype(f32)
    bias_up = tie(small[:, 4, : up_bias.shape[0]].reshape(1, hidden), moved)
    bias_up = jnp.concatenate([bias_up, swap_z(bias_up, dp_size, 1)])
    bias_up = jnp.concatenate([bias_up, swap_z(bias_up, dp_size, 2)]).astype(f32)
    vectors_one = jnp.concatenate([gain_one, scale_one, shift_one])
    vectors_two = jnp.concatenate([gain_two, scale_two, shift_two, gate_one, gate_two, bias_down])
    ada_full = gather_dp(tie(ada_weight, second_pieces[1:3]), dp_size)

    frequency = jnp.exp(
        jnp.arange(HALF, dtype=f32) * (-2.0 * math.log(ROPE_BASE) / HEAD_DIM)
    )
    quarter = position ^ jnp.arange(GROUP, dtype=jnp.int32)
    places = (quarter[:, None] * rows + jnp.arange(rows, dtype=jnp.int32)[None, :]).reshape(-1)
    angles = frequency[:, None] * places.astype(f32)[None, :]
    cosine, sine = jnp.cos(angles), jnp.sin(angles)

    def exchange(blocks):
        return [blocks[0]] + [swap_peer(blocks[r], dp_size, r) for r in range(1, GROUP)]

    hidden_one, packed = project(
        where, moved, vectors_one, cosine[:, :rows], sine[:, :rows], first_pieces, heads
    )
    saved, mixtures = [], []
    for blocks in packed:
        pieces = exchange(blocks)
        outs, lse = attend(pieces)
        saved.append((pieces, lse))
        mixtures.append(exchange(outs))

    outs, mixture_grads = feed(
        where, moved, upstream, vectors_two, bias_up, mixtures, second_pieces, heads
    )
    output, residual_grad, hidden_two, branch_one_grad, branch_two_grad = outs[:5]
    activated, pre_grad, attention, feed_sums, bias_sums = outs[5:]
    second_grad = feed_grads(
        dp_size, where, hidden_two, branch_one_grad, branch_two_grad, activated, pre_grad, attention
    )
    second_far = reduce_cores(second_grad, dp_size)

    received = [None] * len(saved)
    order = list(reversed(range(len(saved))))
    incoming = {n: exchange(mixture_grads[n]) for n in order}
    output = regroup(tie(output, incoming[order[-1]]), dp_size)
    gates = [(second_grad,), (second_far,)]
    for n in order:
        pieces, lse = saved[n]
        grads = tie(incoming[n], *gates.pop(0))
        received[n] = exchange(attend_back(pieces, grads, lse, cosine, sine))
    second_half = reduce_first(second_grad, second_far, dp_size)
    first_grad = project_grads(dp_size, where, hidden_one, received, heads)
    first_far = reduce_cores(first_grad, dp_size)
    input_grad, project_sums = project_back(
        where, moved, vectors_one, residual_grad, received, first_pieces, heads
    )
    input_grad = regroup(input_grad, dp_size)
    second_sum = reduce_second(second_grad, second_far, second_half, dp_size)
    first_half = reduce_first(first_grad, first_far, dp_size)
    first_sum = reduce_second(first_grad, first_far, first_half, dp_size)
    second_sum = reduce_planes(second_sum, dp_size)
    first_sum = reduce_planes(first_sum, dp_size)
    out_out = second_sum[:, :wide].T
    up_out = second_sum[:, wide : wide + hidden]
    down_out = second_sum[:, wide + hidden :].T
    qkv_out = jnp.stack(jnp.split(first_sum, 3, axis=1))

    pull_one, pull_two = project_sums[1:2], feed_sums[1:2]
    mine = jnp.concatenate(
        [
            project_sums[:1],
            pull_one * gain_one,
            feed_sums[3:4],
            feed_sums[:1],
            pull_two * gain_two,
            feed_sums[2:3],
            pull_one * (1.0 + scale_one),
            pull_two * (1.0 + scale_two),
            feed_sums[4:5],
        ]
    )
    bias_sums = bias_sums.reshape(GROUP, hidden // width, width)
    other = swap_z(jnp.concatenate([mine, bias_sums.reshape(-1, width)]), dp_size, 1)
    other_bias = other[9:].reshape(bias_sums.shape)
    mine = jnp.concatenate(
        [mine + other[:9], bias_sums[0] + other_bias[1], bias_sums[2] + other_bias[3]]
    )
    mine = mine + swap_dp(mine, dp_size, 1)
    mods = mine[:6].astype(bf16).astype(f32)[None]
    other = swap_z(jnp.concatenate([mods[0], mine[6:]]), dp_size, 2)
    mods = jnp.concatenate([mods, other[None, :6]])
    flat = hidden // width
    tail = jnp.concatenate([mine[6:9] + other[6:9], mine[9 : 9 + flat] + other[9 + flat :]])
    mask = 2
    while mask < dp_size:
        other = swap_dp(jnp.concatenate([mods.reshape(-1, width), tail]), dp_size, mask)
        mods = jnp.concatenate([mods, other[: -tail.shape[0]].reshape(mods.shape)])
        tail = tail + other[-tail.shape[0] :]
        mask *= 2
    rel = jnp.arange(dp_size)
    seq_at = (me // 2 ^ rel // 2) * 2 + (z // 2 ^ rel % 2)
    mods = mods.reshape(dp_size, 6 * width).astype(bf16)
    columns = ada_weight.shape[1]
    own_mods = lax.dynamic_slice_in_dim(mods, me * columns, columns, axis=1)
    pick = (seq_at[:, None] == jnp.arange(dp_size)[None, :]).astype(bf16)
    ada_out = einsum("sc,se->ce", jnp.dot(pick, embeds), own_mods)
    ada_bias_out = jnp.sum(own_mods.astype(f32), axis=0)
    mine_at = (seq_at == me).astype(f32)
    own_row = jnp.sum(mods.astype(f32) * mine_at[:, None], axis=0).astype(bf16)
    own_row = reorder(own_row.reshape(dp_size, columns), me)
    time_out = jnp.sum(einsum("oe,oce->oc", own_row, ada_full), axis=0, keepdims=True)

    def own_part(row):
        return lax.dynamic_slice_in_dim(row, me * per, per)

    bias_up_out = lax.dynamic_slice_in_dim(
        tail[3:].reshape(-1), me * up_bias.shape[0], up_bias.shape[0]
    )
    return (
        output,
        input_grad,
        time_out,
        ada_out,
        ada_bias_out,
        own_part(tail[0]),
        qkv_out,
        out_out,
        own_part(tail[1]),
        up_out,
        bias_up_out,
        down_out,
        own_part(tail[2]),
    )


def solution(mesh):
    placed = (
        P(("dp", "tensor"), None),
        P("dp", None),
        P(None, "dp"),
        P("dp"),
        P("dp"),
        P(None, "dp", "tensor"),
        P("tensor", "dp"),
        P("dp"),
        P("dp", "tensor"),
        P(("tensor", "dp")),
        P("tensor", "dp"),
        P("dp"),
        P(("dp", "tensor"), None),
    )
    return jax.shard_map(
        functools.partial(per_device, mesh.shape["dp"]),
        mesh=mesh,
        in_specs=placed,
        out_specs=(
            P(("dp", "tensor"), None),
            P(("dp", "tensor"), None),
            P("dp", None),
            P(None, "dp"),
            P("dp"),
            P("dp"),
            P(None, "dp", "tensor"),
            P("tensor", "dp"),
            P("dp"),
            P("dp", "tensor"),
            P(("tensor", "dp")),
            P("tensor", "dp"),
            P("dp"),
        ),
        check_vma=False,
    )
```

```python
import functools
import math

import jax
import jax.numpy as jnp
from jax import lax
from jax.experimental import pallas as pl
from jax.experimental.pallas import tpu as pltpu
from jax.sharding import PartitionSpec as P

HEAD_DIM = 64
EPSILON = 1e-05
ROPE_BASE = 10000.0
GROUP = 4
AXES = ("dp", "tensor")
f32 = jnp.float32
bf16 = jnp.bfloat16


def permute(array, dp_size, target):
    pairs = []
    for d in range(dp_size):
        for z in range(GROUP):
            to_d, to_z = target(d, z)
            pairs.append((d * GROUP + z, to_d * GROUP + to_z))
    return lax.ppermute(array, AXES, pairs)


def swap_dp(array, dp_size, mask):
    return permute(array, dp_size, lambda d, z: (d ^ mask, z))


def swap_z(array, dp_size, mask):
    return permute(array, dp_size, lambda d, z: (d, z ^ mask))


def swap_peer(array, dp_size, r):
    return permute(array, dp_size, lambda d, z: (d ^ (r >> 1), z ^ (r & 1)))


def regroup(array, dp_size):
    return permute(
        array, dp_size, lambda d, z: (d // 2 * 2 + z // 2, d % 2 * 2 + z % 2)
    )


def tie(arrays, *after):
    return lax.optimization_barrier((arrays, after))[0]


def reorder(array, index):
    count = array.shape[0]
    for k in range(count.bit_length() - 1):
        pairs = array.reshape(count >> (k + 1), 2, 1 << k, *array.shape[1:])
        pairs = jnp.concatenate([pairs[:, 1:], pairs[:, :1]], axis=1).reshape(array.shape)
        array = jnp.where((index >> k) % 2 == 1, pairs, array)
    return array


def gather_dp(array, dp_size):
    blocks = array[None]
    mask = 2
    while mask < dp_size:
        blocks = jnp.concatenate([blocks, swap_dp(blocks, dp_size, mask)])
        mask *= 2
    blocks = jnp.stack([blocks, swap_dp(blocks, dp_size, 1)], axis=1)
    return blocks.reshape(dp_size, *array.shape)


WHOLE = ((0, 0), (2, 0), (4, 0), (6, 0), (1, 0), (3, 0), (5, 0), (7, 0))
HALVES = WHOLE[:4] + ((6, 2),) + WHOLE[4:] + ((7, 2),)


def stack_planes(shard, dp_size):
    return jnp.stack([shard] + [swap_z(shard, dp_size, t) for t in range(1, GROUP)])


def gather_weights(own, dp_size, way):
    if dp_size != 8:
        return (lax.all_gather(own, "dp", axis=1, tiled=True),)
    x = swap_dp(own, dp_size, 2)
    y = swap_dp(own, dp_size, 4)
    if way == 2:
        near = (own, x, y, swap_dp(x, dp_size, 4))
    elif way == 4:
        near = (own, x, y, swap_dp(y, dp_size, 2))
    else:
        near = (own, x, y, swap_dp(x[:2], dp_size, 4), swap_dp(y[2:], dp_size, 2))
    return near + tuple(swap_dp(piece, dp_size, 1) for piece in near)


def load_gathered(gathered, full, sems):
    if len(gathered.shape) == 3:
        copies = [pltpu.make_async_copy(gathered, full, sems.at[0])]
    else:
        count, _, rows, _ = gathered.shape
        copies = [
            pltpu.make_async_copy(
                gathered.at[i], full.at[:, i * rows : (i + 1) * rows], sems.at[i]
            )
            for i in range(count)
        ]
    for copy in copies:
        copy.start()
    return copies


def load_weights(me, pieces, full, sems):
    if len(pieces) == 1:
        copies = [pltpu.make_async_copy(pieces[0], full, sems.at[0])]
    else:
        copies = []
        for i, (piece, (rel, first)) in enumerate(
            zip(pieces, HALVES if len(pieces) == len(HALVES) else WHOLE)
        ):
            count, rows = piece.shape[:2]
            start = pl.multiple_of((me ^ rel) * rows, rows)
            place = full.at[first : first + count, pl.ds(start, rows)]
            copies.append(pltpu.make_async_copy(piece, place, sems.at[i]))
    for copy in copies:
        copy.start()
    return copies


def store_blocks(me, outs, slot, value):
    if len(outs) == 1:
        outs[0][slot] = value
        return
    rows = outs[0].shape[2]
    for owner in range(2 * outs[0].shape[0]):
        rel = me ^ owner
        for parity, out in enumerate(outs):

            @pl.when((rel & 1) == parity)
            def _():
                out[rel >> 1, slot] = value[owner * rows : (owner + 1) * rows]


def grad_shapes(dp_size, width, columns):
    if dp_size != 8:
        return [jax.ShapeDtypeStruct((GROUP, width, columns), bf16)]
    return [jax.ShapeDtypeStruct((dp_size // 2, GROUP, width // dp_size, columns), bf16)] * 2


def plus(a, b):
    return (a.astype(f32) + b.astype(f32)).astype(bf16)


def reduce_cores(parts, dp_size):
    return swap_dp(parts[1], dp_size, 1) if dp_size == 8 else None


def reduce_diagonal(parts, far, dp_size):
    return plus(parts[0][3], far[3]) if dp_size == 8 else None


def reduce_first(diagonal, dp_size):
    if dp_size != 8:
        return None
    return swap_dp(diagonal[:2], dp_size, 2), swap_dp(diagonal[2:], dp_size, 4)


def reduce_sides(parts, far, half, dp_size):
    if dp_size != 8:
        return None
    x = parts[0][1].astype(f32) + far[1].astype(f32)
    y = parts[0][2].astype(f32) + far[2].astype(f32)
    x = jnp.concatenate([x[:2], x[2:] + half[1].astype(f32)]).astype(bf16)
    y = jnp.concatenate([y[:2] + half[0].astype(f32), y[2:]]).astype(bf16)
    return x, y


def reduce_second(parts, far, sides, dp_size):
    if dp_size != 8:
        return lax.psum_scatter(parts[0], "dp", scatter_dimension=1, tiled=True).astype(f32)
    from_x = swap_dp(sides[0], dp_size, 2)
    from_y = swap_dp(sides[1], dp_size, 4)
    own = parts[0][0].astype(f32) + far[0].astype(f32)
    return own + from_x.astype(f32) + from_y.astype(f32)


def reduce_planes(own, dp_size):
    total = own[0]
    for t in range(1, GROUP):
        total = total + swap_z(own[t].astype(bf16), dp_size, t).astype(f32)
    return total


def attend_kernel(a0, a1, a2, a3, o0, o1, o2, o3, lse, key_t, value_t, key):
    pieces = (a0, a1, a2, a3)
    block = a0.shape[1]
    for h in range(a0.shape[0] // (3 * HEAD_DIM)):
        at = 3 * HEAD_DIM * h
        for i, piece in enumerate(pieces):
            columns = slice(i * block, (i + 1) * block)
            key_t[:, columns] = piece[at + HEAD_DIM : at + 2 * HEAD_DIM]
            value_t[:, columns] = piece[at + 2 * HEAD_DIM : at + 3 * HEAD_DIM]
        key[...] = key_t[...].T
        for i, (piece, out) in enumerate(zip(pieces, (o0, o1, o2, o3))):
            query = piece[at : at + HEAD_DIM] * bf16(HEAD_DIM**-0.5)
            scores = jnp.dot(key[...], query, preferred_element_type=f32)
            highest = jnp.max(scores, axis=0, keepdims=True)
            exponent = jnp.exp(scores - highest)
            totals = jnp.sum(exponent, axis=0, keepdims=True)
            mixture = jnp.dot(value_t[...], exponent.astype(bf16), preferred_element_type=f32)
            out[h * HEAD_DIM : (h + 1) * HEAD_DIM] = (mixture / totals).astype(bf16)
            lse[h * GROUP + i : h * GROUP + i + 1, :] = highest + jnp.log(totals)


def attend(pieces):
    block = pieces[0].shape[1]
    heads = pieces[0].shape[0] // (3 * HEAD_DIM)
    length = GROUP * block
    vmem = pl.BlockSpec(memory_space=pltpu.VMEM)
    *outs, lse = pl.pallas_call(
        attend_kernel,
        out_shape=[jax.ShapeDtypeStruct((heads * HEAD_DIM, block), bf16)] * GROUP
        + [jax.ShapeDtypeStruct((heads * GROUP, block), f32)],
        in_specs=[vmem] * GROUP,
        out_specs=[vmem] * (GROUP + 1),
        scratch_shapes=[
            pltpu.VMEM((HEAD_DIM, length), bf16),
            pltpu.VMEM((HEAD_DIM, length), bf16),
            pltpu.VMEM((length, HEAD_DIM), bf16),
        ],
        compiler_params=pltpu.CompilerParams(vmem_limit_bytes=40 << 20),
        cost_estimate=pl.CostEstimate(
            flops=16 * heads * length * length * HEAD_DIM,
            bytes_accessed=8 * heads * length * HEAD_DIM,
            transcendentals=heads * length * length,
        ),
        name="attend",
    )(*pieces)
    return outs, lse


def attend_back_kernel(first_head, *refs):
    pieces, grads = refs[0:4], refs[4:8]
    lse, cosine, sine = refs[8:11]
    outs = refs[11:15]
    key_t, key, value_t, query_grad, key_grad, value_grad = refs[15:]
    block = pieces[0].shape[1]
    rows = min(256, block)
    half = HEAD_DIM // 2
    for h in range(pieces[0].shape[0] // (3 * HEAD_DIM)):
        of_grad = slice((first_head + h) * HEAD_DIM, (first_head + h + 1) * HEAD_DIM)
        at = 3 * HEAD_DIM * h
        for i, piece in enumerate(pieces):
            columns = slice(i * block, (i + 1) * block)
            key_t[:, columns] = piece[at + HEAD_DIM : at + 2 * HEAD_DIM]
            value_t[:, columns] = piece[at + 2 * HEAD_DIM : at + 3 * HEAD_DIM]
            key[columns, :] = piece[at + HEAD_DIM : at + 2 * HEAD_DIM].T
        for i, (piece, grad) in enumerate(zip(pieces, grads)):
            log_total = lse[h * GROUP + i : h * GROUP + i + 1, :].T
            for c in range(block // rows):
                own = slice(c * rows, (c + 1) * rows)
                query_t = piece[at : at + HEAD_DIM, own] * bf16(HEAD_DIM**-0.5)
                grad_t = grad[of_grad, own]
                scores = jnp.dot(query_t.T, key_t[...], preferred_element_type=f32)
                weights = jnp.exp(scores - log_total[own])
                pull = jnp.dot(grad_t.T, value_t[...], preferred_element_type=f32)
                centre = jnp.sum(weights * pull, axis=1, keepdims=True)
                score_grad = (weights * (pull - centre)).astype(bf16)
                value_term = jnp.dot(grad_t, weights.astype(bf16), preferred_element_type=f32)
                key_term = jnp.dot(query_t, score_grad, preferred_element_type=f32)
                if i == 0 and c == 0:
                    value_grad[...] = value_term
                    key_grad[...] = key_term
                else:
                    value_grad[...] += value_term
                    key_grad[...] += key_term
                query_grad[:, i * block + c * rows : i * block + (c + 1) * rows] = (
                    jnp.dot(score_grad, key[...], preferred_element_type=f32) * HEAD_DIM**-0.5
                ).T
        for i, out in enumerate(outs):
            columns = slice(i * block, (i + 1) * block)
            cos, sin = cosine[:, columns], sine[:, columns]
            for first, source in ((at, query_grad), (at + HEAD_DIM, key_grad)):
                upper, lower = source[:half, columns], source[half:, columns]
                out[first : first + half] = (upper * cos + lower * sin).astype(bf16)
                out[first + half : first + HEAD_DIM] = (lower * cos - upper * sin).astype(bf16)
            out[at + 2 * HEAD_DIM : at + 3 * HEAD_DIM] = value_grad[:, columns].astype(bf16)


def attend_back(pieces, grads, first_head, lse, cosine, sine):
    block = pieces[0].shape[1]
    heads = pieces[0].shape[0] // (3 * HEAD_DIM)
    length = GROUP * block
    vmem = pl.BlockSpec(memory_space=pltpu.VMEM)
    return pl.pallas_call(
        functools.partial(attend_back_kernel, first_head),
        out_shape=[jax.ShapeDtypeStruct((heads * 3 * HEAD_DIM, block), bf16)] * GROUP,
        in_specs=[vmem] * 11,
        out_specs=[vmem] * GROUP,
        scratch_shapes=[
            pltpu.VMEM((HEAD_DIM, length), bf16),
            pltpu.VMEM((length, HEAD_DIM), bf16),
            pltpu.VMEM((HEAD_DIM, length), bf16),
            pltpu.VMEM((HEAD_DIM, length), f32),
            pltpu.VMEM((HEAD_DIM, length), f32),
            pltpu.VMEM((HEAD_DIM, length), f32),
        ],
        compiler_params=pltpu.CompilerParams(vmem_limit_bytes=48 << 20),
        cost_estimate=pl.CostEstimate(
            flops=40 * heads * length * length * HEAD_DIM,
            bytes_accessed=16 * heads * length * HEAD_DIM,
            transcendentals=heads * length * length,
        ),
        name="attend_back",
    )(*pieces, *grads, lse, cosine, sine)


def normalize(rows):
    center = jnp.mean(rows, axis=1, keepdims=True)
    shifted = rows - center
    inverse = lax.rsqrt(jnp.mean(shifted * shifted, axis=1, keepdims=True) + EPSILON)
    return shifted * inverse, inverse


def norm_back(scaled, normed, inverse):
    return inverse * (
        scaled
        - jnp.mean(scaled, axis=1, keepdims=True)
        - normed * jnp.mean(scaled * normed, axis=1, keepdims=True)
    )


def dot(a, b):
    return jnp.dot(a, b, preferred_element_type=f32)


def dot_nt(a, b):
    return lax.dot_general(a, b, (((1,), (1,)), ((), ())), preferred_element_type=f32)


def total(values):
    return jnp.sum(values, axis=0, keepdims=True)


VMEM = pl.BlockSpec(memory_space=pltpu.VMEM)
SMEM = pl.BlockSpec(memory_space=pltpu.SMEM)
ANY = pl.BlockSpec(memory_space=pl.ANY)
HALF = HEAD_DIM // 2


def parts_of(heads):
    return tuple(range(h, h + 1) for h in range(heads))


def project_kernel(count, heads, *refs):
    where, tokens, vectors, cosine, sine = refs[:5]
    pieces, refs = refs[5 : 5 + count], refs[5 + count :]
    parts = parts_of(heads)
    hidden, packed = refs[0], refs[1 : 1 + GROUP * len(parts)]
    full, sems = refs[1 + GROUP * len(parts) :]
    me, base = where[0], where[1]
    wide = heads * HEAD_DIM
    copies = load_weights(me, pieces, full, sems)
    gain, scale, shift = vectors[0:1], vectors[1:2], vectors[2:3]
    normed, _ = normalize(tokens[...].astype(f32))
    hidden[...] = (normed * gain * (1.0 + scale) + shift).astype(bf16)
    cos, sin = cosine[...], sine[...]
    for copy in copies:
        copy.wait()
    for r in range(GROUP):
        projected = dot(hidden[...], full[base ^ r]).T
        for n, part in enumerate(parts):
            out = packed[r * len(parts) + n]
            for i, h in enumerate(part):
                at = 3 * HEAD_DIM * i
                for c in range(2):
                    first = c * wide + h * HEAD_DIM
                    upper = projected[first : first + HALF]
                    lower = projected[first + HALF : first + HEAD_DIM]
                    out[at : at + HALF] = (upper * cos - lower * sin).astype(bf16)
                    out[at + HALF : at + HEAD_DIM] = (lower * cos + upper * sin).astype(bf16)
                    at += HEAD_DIM
                first = 2 * wide + h * HEAD_DIM
                out[at : at + HEAD_DIM] = projected[first : first + HEAD_DIM].astype(bf16)


def project(where, tokens, vectors, cosine, sine, pieces, heads):
    rows, width = tokens.shape
    columns = pieces[0].shape[2]
    parts = parts_of(heads)
    outs = pl.pallas_call(
        functools.partial(project_kernel, len(pieces), heads),
        out_shape=[jax.ShapeDtypeStruct((rows, width), bf16)]
        + [jax.ShapeDtypeStruct((3 * HEAD_DIM * len(part), rows), bf16) for part in parts] * GROUP,
        in_specs=[SMEM] + [VMEM] * 4 + [ANY] * len(pieces),
        out_specs=[VMEM] * (1 + GROUP * len(parts)),
        scratch_shapes=[
            pltpu.VMEM((GROUP, width, columns), bf16),
            pltpu.SemaphoreType.DMA((len(pieces),)),
        ],
        compiler_params=pltpu.CompilerParams(vmem_limit_bytes=32 << 20),
        cost_estimate=pl.CostEstimate(
            flops=2 * rows * width * GROUP * columns,
            bytes_accessed=2 * GROUP * (width + rows) * columns,
            transcendentals=0,
        ),
        name="project",
    )(where, tokens, vectors, cosine, sine, *pieces)
    return outs[0], [outs[1 + n :: len(parts)] for n in range(len(parts))]


GELU_A = math.sqrt(2.0 / math.pi)
GELU_B = 0.044715


def feed_kernel(heads, *refs):
    where, tokens, upstream, vectors, bias_up = refs[:5]
    parts = parts_of(heads)
    used = GROUP * len(parts)
    mixtures, refs = refs[5 : 5 + used], refs[5 + used :]
    gathered, refs = refs[0], refs[1:]
    output, residual_grad, out_hidden, out_branch_one, out_branch_two = refs[:5]
    activated, pre_grad, attention, sums, bias_sums = refs[5:10]
    mixture_grads = refs[10 : 10 + GROUP]
    full, slope, keep_one, keep_two, sems = refs[10 + GROUP :]
    me, own_block = where[0], where[1]
    wide = heads * HEAD_DIM
    hidden = bias_up.shape[1]
    of_out = slice(0, wide)
    of_up = slice(wide, wide + hidden)
    of_down = slice(wide + hidden, wide + 2 * hidden)
    copies = load_gathered(gathered, full, sems)
    gain, scale, shift = vectors[0:1], vectors[1:2], vectors[2:3]
    gate_one, gate_two, bias_down = vectors[3:4], vectors[4:5], vectors[5:6]
    for r in range(GROUP):
        own = jnp.concatenate([mixtures[n * GROUP + r][...] for n in range(len(parts))])
        attention[r] = own.T
    for copy in copies:
        copy.wait()
    branch_one = dot_nt(attention[0], full[own_block, :, of_out])
    for r in range(1, GROUP):
        branch_one = branch_one + dot_nt(attention[r], full[own_block ^ r, :, of_out])
    keep_one[...] = branch_one
    residual = tokens[...].astype(f32) + gate_one * branch_one
    normed, _ = normalize(residual)
    out_hidden[...] = (normed * gain * (1.0 + scale) + shift).astype(bf16)

    keep_two[...] = jnp.broadcast_to(bias_down, keep_two.shape)

    def forward(t, carry):
        pre = dot(out_hidden[...], full[t, :, of_up]) + bias_up[pl.ds(t, 1)]
        inner = jnp.tanh(GELU_A * (pre + GELU_B * pre * pre * pre))
        activated[t] = (0.5 * pre * (1.0 + inner)).astype(bf16)
        slope[t] = 0.5 * (1.0 + inner) + (
            0.5 * GELU_A * pre * (1.0 - inner * inner) * (1.0 + 3.0 * GELU_B * pre * pre)
        )
        keep_two[...] += dot_nt(activated[t], full[t, :, of_down])
        return carry

    lax.fori_loop(0, GROUP, forward, 0)
    branch_two = keep_two[...]
    residual = tokens[...].astype(f32) + gate_one * keep_one[...]
    output[...] = (residual + gate_two * branch_two).astype(bf16)
    grad = upstream[...].astype(f32)
    branch_two_grad = gate_two * grad
    out_branch_two[...] = branch_two_grad.astype(bf16)
    sums[2:3] = total(grad * branch_two)
    sums[4:5] = total(out_branch_two[...].astype(f32))

    keep_two[...] = jnp.zeros_like(keep_two)

    def backward(t, carry):
        act_grad = dot(out_branch_two[...], full[t, :, of_down])
        pre_grad[t] = (act_grad * slope[t]).astype(bf16)
        bias_sums[pl.ds(t, 1)] = total(pre_grad[t].astype(f32))
        keep_two[...] += dot_nt(pre_grad[t], full[t, :, of_up])
        return carry

    lax.fori_loop(0, GROUP, backward, 0)
    hidden_grad = keep_two[...]
    residual = tokens[...].astype(f32) + gate_one * keep_one[...]
    normed, inverse = normalize(residual)
    sums[0:1] = total(hidden_grad)
    sums[1:2] = total(hidden_grad * normed)
    grad = upstream[...].astype(f32) + norm_back(
        hidden_grad * gain * (1.0 + scale), normed, inverse
    )
    residual_grad[...] = grad
    sums[3:4] = total(grad * keep_one[...])
    out_branch_one[...] = (gate_one * grad).astype(bf16)
    for r in range(GROUP):
        back = dot(out_branch_one[...], full[own_block ^ r, :, of_out])
        mixture_grads[r][...] = back.astype(bf16).T


def feed(where, tokens, upstream, vectors, bias_up, mixtures, gathered, heads):
    rows, width = tokens.shape
    wide = heads * HEAD_DIM
    hidden = bias_up.shape[1]
    columns = gathered.shape[-1]
    parts = parts_of(heads)
    count = GROUP * len(parts)

    def shape(dtype, *lengths):
        return jax.ShapeDtypeStruct(lengths, dtype)

    outs = pl.pallas_call(
        functools.partial(feed_kernel, heads),
        out_shape=[
            shape(bf16, rows, width),
            shape(f32, rows, width),
            shape(bf16, rows, width),
            shape(bf16, rows, width),
            shape(bf16, rows, width),
            shape(bf16, GROUP, rows, hidden),
            shape(bf16, GROUP, rows, hidden),
            shape(bf16, GROUP, rows, wide),
            shape(f32, 5, width),
            shape(f32, GROUP, hidden),
        ]
        + [shape(bf16, wide, rows)] * GROUP,
        in_specs=[SMEM] + [VMEM] * (4 + count) + [ANY],
        out_specs=[VMEM] * (10 + GROUP),
        scratch_shapes=[
            pltpu.VMEM((GROUP, width, columns), bf16),
            pltpu.VMEM((GROUP, rows, hidden), f32),
            pltpu.VMEM((rows, width), f32),
            pltpu.VMEM((rows, width), f32),
            pltpu.SemaphoreType.DMA((gathered.shape[0],)),
        ],
        compiler_params=pltpu.CompilerParams(vmem_limit_bytes=56 << 20),
        cost_estimate=pl.CostEstimate(
            flops=4 * rows * width * GROUP * columns,
            bytes_accessed=2 * GROUP * (width + rows) * columns,
            transcendentals=GROUP * rows * hidden,
        ),
        name="feed",
    )(where, tokens, upstream, vectors, bias_up, *sum(mixtures, []), gathered)
    return outs[:10], outs[10:]


def feed_grads_kernel(where, hidden, branch_one, branch_two, act, pre, attention, out):
    own_block = where[1]
    t = pl.program_id(0)
    up = dot(hidden[...].T, pre[0]).astype(bf16)
    down = dot(branch_two[...].T, act[0]).astype(bf16)
    own = dot(branch_one[...].T, attention[own_block ^ t]).astype(bf16)
    value = jnp.concatenate([own, up, down], axis=1)
    if len(out.shape) == 3:
        out[0] = value
    else:
        out[...] = value.reshape(out.shape)


def feed_grads(dp_size, where, hidden, branch_one, branch_two, act, pre, attention):
    rows, width = hidden.shape
    wide, inner = attention.shape[2], act.shape[2]
    columns = wide + 2 * inner
    if dp_size == 8:
        shape = (dp_size, GROUP, width // dp_size, columns)
        out_spec = pl.BlockSpec((dp_size, 1, width // dp_size, columns), lambda t: (0, t, 0, 0))
    else:
        shape = (GROUP, width, columns)
        out_spec = pl.BlockSpec((1, width, columns), lambda t: (t, 0, 0))
    return pl.pallas_call(
        feed_grads_kernel,
        out_shape=jax.ShapeDtypeStruct(shape, bf16),
        grid=(GROUP,),
        in_specs=[SMEM]
        + [VMEM] * 3
        + [pl.BlockSpec((1, rows, inner), lambda t: (t, 0, 0))] * 2
        + [VMEM],
        out_specs=out_spec,
        compiler_params=pltpu.CompilerParams(vmem_limit_bytes=40 << 20),
        cost_estimate=pl.CostEstimate(
            flops=2 * rows * width * GROUP * columns,
            bytes_accessed=2 * GROUP * (width + rows) * columns,
            transcendentals=0,
        ),
        name="feed_grads",
    )(where, hidden, branch_one, branch_two, act, pre, attention)


def join_heads(pieces, heads, r):
    rows = []
    for c in range(3):
        for n, part in enumerate(parts_of(heads)):
            for i in range(len(part)):
                first = (3 * i + c) * HEAD_DIM
                rows.append(pieces[n * GROUP + r][first : first + HEAD_DIM])
    return jnp.concatenate(rows)


def project_grads_kernel(heads, used, where, hidden, *refs):
    pieces, outs = refs[:used], refs[used:]
    me, base = where[0], where[1]
    hidden_t = hidden[...].T
    for r in range(GROUP):
        value = dot_nt(hidden_t, join_heads(pieces, heads, r)).astype(bf16)
        store_blocks(me, outs, base ^ r, value)


def project_grads(dp_size, where, hidden, received, heads):
    rows, width = hidden.shape
    columns = 3 * heads * HEAD_DIM
    received = sum(received, [])
    shapes = grad_shapes(dp_size, width, columns)
    return pl.pallas_call(
        functools.partial(project_grads_kernel, heads, len(received)),
        out_shape=shapes,
        in_specs=[SMEM] + [VMEM] * (1 + len(received)),
        out_specs=[VMEM] * len(shapes),
        compiler_params=pltpu.CompilerParams(vmem_limit_bytes=32 << 20),
        cost_estimate=pl.CostEstimate(
            flops=2 * rows * width * GROUP * columns,
            bytes_accessed=2 * GROUP * (width + rows) * columns,
            transcendentals=0,
        ),
        name="project_grads",
    )(where, hidden, *received)


def project_back_kernel(count, heads, *refs):
    where, tokens, vectors, residual_grad = refs[:4]
    used = GROUP * len(parts_of(heads))
    received, refs = refs[4 : 4 + used], refs[4 + used :]
    pieces, (input_grad, sums, full, sems) = refs[:count], refs[count:]
    me, base = where[0], where[1]
    copies = load_weights(me, pieces, full, sems)
    gain, scale = vectors[0:1], vectors[1:2]
    normed, inverse = normalize(tokens[...].astype(f32))
    for copy in copies:
        copy.wait()
    hidden_grad = None
    for r in range(GROUP):
        term = dot_nt(join_heads(received, heads, r).T, full[base ^ r])
        hidden_grad = term if hidden_grad is None else hidden_grad + term
    sums[0:1] = total(hidden_grad)
    sums[1:2] = total(hidden_grad * normed)
    input_grad[...] = (
        residual_grad[...] + norm_back(hidden_grad * gain * (1.0 + scale), normed, inverse)
    ).astype(bf16)


def project_back(where, tokens, vectors, residual_grad, received, pieces, heads):
    rows, width = tokens.shape
    columns = pieces[0].shape[2]
    received = sum(received, [])
    return pl.pallas_call(
        functools.partial(project_back_kernel, len(pieces), heads),
        out_shape=[
            jax.ShapeDtypeStruct((rows, width), bf16),
            jax.ShapeDtypeStruct((2, width), f32),
        ],
        in_specs=[SMEM] + [VMEM] * (3 + len(received)) + [ANY] * len(pieces),
        out_specs=[VMEM] * 2,
        scratch_shapes=[
            pltpu.VMEM((GROUP, width, columns), bf16),
            pltpu.SemaphoreType.DMA((len(pieces),)),
        ],
        compiler_params=pltpu.CompilerParams(vmem_limit_bytes=32 << 20),
        cost_estimate=pl.CostEstimate(
            flops=2 * rows * width * GROUP * columns,
            bytes_accessed=2 * GROUP * (width + rows) * columns,
            transcendentals=0,
        ),
        name="project_back",
    )(where, tokens, vectors, residual_grad, *received, *pieces)


def einsum(spec, a, b):
    return jnp.einsum(spec, a, b, preferred_element_type=f32)


def per_device(
    dp_size,
    tokens,
    time_embed,
    ada_weight,
    ada_bias,
    norm1_gain,
    qkv_weight,
    out_weight,
    norm2_gain,
    up_weight,
    up_bias,
    down_weight,
    down_bias,
    out_grad,
):
    me = lax.axis_index("dp")
    z = lax.axis_index("tensor")
    position = me % 2 * 2 + z % 2
    base = z ^ position
    where = jnp.stack([me, base]).astype(jnp.int32)
    where_whole = jnp.stack([me, position]).astype(jnp.int32)
    rows, width = tokens.shape
    heads = qkv_weight.shape[2] // HEAD_DIM
    wide = heads * HEAD_DIM
    hidden = up_weight.shape[1]
    cond = time_embed.shape[1]
    per = norm1_gain.shape[0]

    columns = ada_weight.shape[1]
    small = jnp.concatenate([time_embed[0], norm1_gain, norm2_gain, down_bias, up_bias])
    lines = -(-small.shape[0] // columns)
    small = jnp.pad(small, (0, lines * columns - small.shape[0])).reshape(lines, columns)
    pack = jnp.concatenate([ada_weight, ada_bias[None], small])
    pack = jnp.pad(pack, ((0, -pack.shape[0] % 16), (0, 0)))
    pack = gather_dp(pack, dp_size)
    ada_full = pack[:, :cond]

    first_own = stack_planes(jnp.concatenate([*qkv_weight], axis=1), dp_size)
    first_pieces = gather_weights(first_own, dp_size, 0)
    moved = regroup(tie(tokens, first_own), dp_size)
    second_shard = jnp.concatenate([out_weight.T, up_weight, down_weight.T], axis=1)
    if dp_size == 8:
        gathered = lax.all_gather(second_shard, AXES, axis=0, tiled=False)
        gathered = gathered.reshape(dp_size, GROUP, *second_shard.shape)
    else:
        gathered = lax.all_gather(second_shard, "tensor", axis=0, tiled=False)
        gathered = lax.all_gather(gathered, "dp", axis=1, tiled=True)
    upstream = regroup(tie(out_grad, moved), dp_size)

    small = reorder(pack[:, cond + 1 : cond + 1 + lines], me).reshape(dp_size, lines * columns)
    embeds = small[:, :cond]
    sequence = me // 2 * 2 + z // 2
    embed = lax.dynamic_slice_in_dim(embeds, sequence, 1)
    modulation = einsum("sc,oce->soe", embed, ada_full)[0] + pack[:, cond].astype(f32)
    modulation = reorder(modulation, me).reshape(6, 1, width)
    shift_one, scale_one, gate_one, shift_two, scale_two, gate_two = modulation

    def vector(n):
        return small[:, cond + n * per : cond + (n + 1) * per].reshape(1, width).astype(f32)

    gain_one, gain_two, bias_down = vector(0), vector(1), vector(2)
    bias_up = small[:, cond + 3 * per : cond + 3 * per + up_bias.shape[0]].reshape(1, hidden)
    bias_up = tie(bias_up, moved)
    bias_up = jnp.concatenate([bias_up, swap_z(bias_up, dp_size, 1)])
    bias_up = jnp.concatenate([bias_up, swap_z(bias_up, dp_size, 2)]).astype(f32)
    bias_up = reorder(bias_up, z)
    vectors_one = jnp.concatenate([gain_one, scale_one, shift_one])
    vectors_two = jnp.concatenate([gain_two, scale_two, shift_two, gate_one, gate_two, bias_down])

    frequency = jnp.exp(
        jnp.arange(HALF, dtype=f32) * (-2.0 * math.log(ROPE_BASE) / HEAD_DIM)
    )
    quarter = position ^ jnp.arange(GROUP, dtype=jnp.int32)
    places = (quarter[:, None] * rows + jnp.arange(rows, dtype=jnp.int32)[None, :]).reshape(-1)
    angles = frequency[:, None] * places.astype(f32)[None, :]
    cosine, sine = jnp.cos(angles), jnp.sin(angles)

    def exchange(blocks):
        return [blocks[0]] + [swap_peer(blocks[r], dp_size, r) for r in range(1, GROUP)]

    hidden_one, packed = project(
        where, moved, vectors_one, cosine[:, :rows], sine[:, :rows], first_pieces, heads
    )
    saved, mixtures = [], []
    for blocks in packed:
        pieces = exchange(blocks)
        outs, lse = attend(pieces)
        saved.append((pieces, lse))
        mixtures.append(exchange(outs))

    outs, mixture_grads = feed(
        where_whole, moved, upstream, vectors_two, bias_up, mixtures, gathered, heads
    )
    output, residual_grad, hidden_two, branch_one_grad, branch_two_grad = outs[:5]
    activated, pre_grad, attention, feed_sums, bias_sums = outs[5:]
    incoming = exchange(mixture_grads)
    second_grad = feed_grads(
        dp_size,
        where_whole,
        hidden_two,
        branch_one_grad,
        branch_two_grad,
        activated,
        pre_grad,
        attention,
    )
    if dp_size == 8:
        second_sum = lax.psum_scatter(second_grad, "dp", scatter_dimension=0, tiled=False)
    else:
        second_sum = lax.psum_scatter(second_grad, "dp", scatter_dimension=1, tiled=True)
    second_sum = lax.psum_scatter(second_sum, "tensor", scatter_dimension=0, tiled=False)
    second_sum = second_sum.astype(f32)
    output = regroup(tie(output, incoming), dp_size)

    received = []
    gates = [second_grad]
    for n, (pieces, lse) in enumerate(saved):
        grads = tie(incoming, gates[n]) if n < len(gates) else incoming
        received.append(exchange(attend_back(pieces, grads, n, lse, cosine, sine)))
    first_grad = project_grads(dp_size, where, hidden_one, received, heads)
    first_far = reduce_cores(first_grad, dp_size)
    input_grad, project_sums = project_back(
        where, moved, vectors_one, residual_grad, tie(received, first_grad), first_pieces, heads
    )
    first_diagonal = reduce_diagonal(first_grad, first_far, dp_size)
    first_half = reduce_first(first_diagonal, dp_size)
    input_grad = regroup(input_grad, dp_size)
    first_sides = reduce_sides(first_grad, first_far, first_half, dp_size)
    first_sum = reduce_second(first_grad, first_far, first_sides, dp_size)
    first_sum = reduce_planes(first_sum, dp_size)
    out_out = second_sum[:, :wide].T
    up_out = second_sum[:, wide : wide + hidden]
    down_out = second_sum[:, wide + hidden :].T
    qkv_out = jnp.stack(jnp.split(first_sum, 3, axis=1))

    pull_one, pull_two = project_sums[1:2], feed_sums[1:2]
    mine = jnp.concatenate(
        [
            project_sums[:1],
            pull_one * gain_one,
            feed_sums[3:4],
            feed_sums[:1],
            pull_two * gain_two,
            feed_sums[2:3],
            pull_one * (1.0 + scale_one),
            pull_two * (1.0 + scale_two),
            feed_sums[4:5],
        ]
    )
    bias_sums = reorder(bias_sums, z).reshape(GROUP, hidden // width, width)
    other = swap_z(jnp.concatenate([mine, bias_sums.reshape(-1, width)]), dp_size, 1)
    other_bias = other[9:].reshape(bias_sums.shape)
    mine = jnp.concatenate(
        [mine + other[:9], bias_sums[0] + other_bias[1], bias_sums[2] + other_bias[3]]
    )
    mine = mine + swap_dp(mine, dp_size, 1)
    mods = mine[:6].astype(bf16).astype(f32)[None]
    other = swap_z(jnp.concatenate([mods[0], mine[6:]]), dp_size, 2)
    mods = jnp.concatenate([mods, other[None, :6]])
    flat = hidden // width
    tail = jnp.concatenate([mine[6:9] + other[6:9], mine[9 : 9 + flat] + other[9 + flat :]])
    mask = 2
    while mask < dp_size:
        other = swap_dp(jnp.concatenate([mods.reshape(-1, width), tail]), dp_size, mask)
        mods = jnp.concatenate([mods, other[: -tail.shape[0]].reshape(mods.shape)])
        tail = tail + other[-tail.shape[0] :]
        mask *= 2
    rel = jnp.arange(dp_size)
    seq_at = (me // 2 ^ rel // 2) * 2 + (z // 2 ^ rel % 2)
    mods = mods.reshape(dp_size, 6 * width).astype(bf16)
    own_mods = lax.dynamic_slice_in_dim(mods, me * columns, columns, axis=1)
    pick = (seq_at[:, None] == jnp.arange(dp_size)[None, :]).astype(bf16)
    ada_out = einsum("sc,se->ce", jnp.dot(pick, embeds), own_mods)
    ada_bias_out = jnp.sum(own_mods.astype(f32), axis=0)
    mine_at = (seq_at == me).astype(f32)
    own_row = jnp.sum(mods.astype(f32) * mine_at[:, None], axis=0).astype(bf16)
    own_row = reorder(own_row.reshape(dp_size, columns), me)
    time_out = jnp.sum(einsum("oe,oce->oc", own_row, ada_full), axis=0, keepdims=True)

    def own_part(row):
        return lax.dynamic_slice_in_dim(row, me * per, per)

    bias_up_out = lax.dynamic_slice_in_dim(
        tail[3:].reshape(-1), me * up_bias.shape[0], up_bias.shape[0]
    )
    return (
        output,
        input_grad,
        time_out,
        ada_out,
        ada_bias_out,
        own_part(tail[0]),
        qkv_out,
        out_out,
        own_part(tail[1]),
        up_out,
        bias_up_out,
        down_out,
        own_part(tail[2]),
    )


def solution(mesh):
    placed = (
        P(("dp", "tensor"), None),
        P("dp", None),
        P(None, "dp"),
        P("dp"),
        P("dp"),
        P(None, "dp", "tensor"),
        P("tensor", "dp"),
        P("dp"),
        P("dp", "tensor"),
        P(("tensor", "dp")),
        P("tensor", "dp"),
        P("dp"),
        P(("dp", "tensor"), None),
    )
    return jax.shard_map(
        functools.partial(per_device, mesh.shape["dp"]),
        mesh=mesh,
        in_specs=placed,
        out_specs=(
            P(("dp", "tensor"), None),
            P(("dp", "tensor"), None),
            P("dp", None),
            P(None, "dp"),
            P("dp"),
            P("dp"),
            P(None, "dp", "tensor"),
            P("tensor", "dp"),
            P("dp"),
            P("dp", "tensor"),
            P(("tensor", "dp")),
            P("tensor", "dp"),
            P("dp"),
        ),
        check_vma=False,
    )
```

```python
import functools
import math

import jax
import jax.numpy as jnp
from jax import lax
from jax.experimental import pallas as pl
from jax.experimental.pallas import tpu as pltpu
from jax.sharding import PartitionSpec as P

HEAD_DIM = 64
EPSILON = 1e-05
ROPE_BASE = 10000.0
GROUP = 4
DP = ("quad", "core")
TENSOR = ("high", "low")
AXES = DP + TENSOR
TEAM = ("core", "low")
f32 = jnp.float32
bf16 = jnp.bfloat16
VMEM = pl.BlockSpec(memory_space=pltpu.VMEM)
SMEM = pl.BlockSpec(memory_space=pltpu.SMEM)
ANY = pl.BlockSpec(memory_space=pl.ANY)
HALF = HEAD_DIM // 2


def whole(array):
    return pl.BlockSpec(
        array.shape, lambda *at: (0,) * len(array.shape), pipeline_mode=pl.Buffered(1)
    )


def permute(array, dp_size, target):
    pairs = []
    for d in range(dp_size):
        for z in range(GROUP):
            to_d, to_z = target(d, z)
            if (d, z) != (to_d, to_z):
                pairs.append((d * GROUP + z, to_d * GROUP + to_z))
    return lax.ppermute(array, AXES, pairs)


def swap_dp(array, dp_size, mask):
    return permute(array, dp_size, lambda d, z: (d ^ mask, z))


def swap_z(array, dp_size, mask):
    return permute(array, dp_size, lambda d, z: (d, z ^ mask))


def send_tokens(array, dp_size):
    return permute(array, dp_size, lambda d, z: (d // 2 * 2 + z // 2, d % 2 * 2 + z % 2))


def settle(array, moved):
    stay = lax.axis_index("core") == lax.axis_index("high")
    return jnp.where(stay, array, moved)


def regroup(array, dp_size):
    return settle(array, send_tokens(array, dp_size))


def meet(*arrays):
    return lax.optimization_barrier(arrays)


def exchange(blocks):
    return lax.all_to_all(blocks, TEAM, 0, 0, tiled=True)


def reorder(array, index):
    count = array.shape[0]
    for k in range(count.bit_length() - 1):
        pairs = array.reshape(count >> (k + 1), 2, 1 << k, *array.shape[1:])
        pairs = jnp.concatenate([pairs[:, 1:], pairs[:, :1]], axis=1).reshape(array.shape)
        array = jnp.where((index >> k) % 2 == 1, pairs, array)
    return array


def first_step(array, dp_size):
    return jnp.stack([array, swap_dp(array, dp_size, 2)])


def spread_dp(blocks, dp_size):
    array = blocks[0]
    mask = 4
    while mask < dp_size:
        blocks = jnp.concatenate([blocks, swap_dp(blocks, dp_size, mask)])
        mask *= 2
    blocks = jnp.stack([blocks, swap_dp(blocks, dp_size, 1)], axis=1)
    return blocks.reshape(dp_size, *array.shape)


WHOLE = ((0, 0), (2, 0), (4, 0), (6, 0), (1, 0), (3, 0), (5, 0), (7, 0))
HALVES = WHOLE[:4] + ((6, 2),) + WHOLE[4:] + ((7, 2),)


def send_planes(shard, dp_size):
    return [swap_z(shard, dp_size, t) for t in range(1, GROUP)]


def gather_sides(own, dp_size):
    if dp_size != 8:
        return ()
    return swap_dp(own, dp_size, 2), swap_dp(own, dp_size, 4)


def gather_weights(own, sides, dp_size):
    if dp_size != 8:
        return (lax.all_gather(own, DP, axis=1, tiled=True),)
    x, y = sides
    near = (own, x, y, swap_dp(x[:2], dp_size, 4), swap_dp(y[2:], dp_size, 2))
    return near + tuple(swap_dp(piece, dp_size, 1) for piece in near)


def load_weights(me, pieces, full, sems, flip=None):
    if len(pieces) == 1:
        flips = [t if flip is None else t ^ flip for t in range(GROUP)]
        copies = [
            pltpu.make_async_copy(pieces[0].at[t], full.at[flips[t]], sems.at[t])
            for t in range(GROUP)
        ]
    else:
        copies = []
        for i, (piece, (rel, first)) in enumerate(
            zip(pieces, HALVES if len(pieces) == len(HALVES) else WHOLE)
        ):
            count, rows = piece.shape[:2]
            start = pl.multiple_of((me ^ rel) * rows, rows)
            if flip is None:
                place = full.at[first : first + count, pl.ds(start, rows)]
                copies.append(pltpu.make_async_copy(piece, place, sems.at[i]))
                continue
            for t in range(count):
                place = full.at[(first + t) ^ flip, pl.ds(start, rows)]
                sem = sems.at[GROUP * i + t]
                copies.append(pltpu.make_async_copy(piece.at[t], place, sem))
    for copy in copies:
        copy.start()
    return copies


def store_blocks(me, parity, outs, slot, value):
    if len(outs) == 1:
        outs[0][slot] = value
        return
    rows = outs[0].shape[2]
    for owner in range(2 * outs[0].shape[0]):
        out = outs[(owner + parity) % 2]
        out[(me ^ owner) >> 1, slot] = value[owner * rows : (owner + 1) * rows]


def grad_shapes(dp_size, width, columns):
    if dp_size != 8:
        return [jax.ShapeDtypeStruct((GROUP, width, columns), bf16)]
    return [jax.ShapeDtypeStruct((dp_size // 2, GROUP, width // dp_size, columns), bf16)] * 2


def plus(a, b):
    return (a.astype(f32) + b.astype(f32)).astype(bf16)


def reduce_cores(parts, dp_size):
    return swap_dp(parts[1], dp_size, 1) if dp_size == 8 else None


def reduce_diagonal(parts, far, dp_size):
    return plus(parts[0][3], far[3]) if dp_size == 8 else None


def reduce_first(diagonal, dp_size):
    if dp_size != 8:
        return None
    return swap_dp(diagonal[:2], dp_size, 2), swap_dp(diagonal[2:], dp_size, 4)


def reduce_sides(parts, far, half, dp_size):
    if dp_size != 8:
        return None
    x = parts[0][1].astype(f32) + far[1].astype(f32)
    y = parts[0][2].astype(f32) + far[2].astype(f32)
    x = jnp.concatenate([x[:2], x[2:] + half[1].astype(f32)]).astype(bf16)
    y = jnp.concatenate([y[:2] + half[0].astype(f32), y[2:]]).astype(bf16)
    return x, y


def reduce_second(parts, far, sides, dp_size):
    if dp_size != 8:
        return lax.psum_scatter(parts[0], DP, scatter_dimension=1, tiled=True).astype(f32)
    from_x = swap_dp(sides[0], dp_size, 2)
    from_y = swap_dp(sides[1], dp_size, 4)
    own = parts[0][0].astype(f32) + far[0].astype(f32)
    return own + from_x.astype(f32) + from_y.astype(f32)


def reduce_planes(own):
    terms = lax.all_to_all(own.astype(bf16), TENSOR, 0, 0, tiled=True)
    return jnp.sum(terms.astype(f32), axis=0)


def attend_kernel(packed, out, lse, key_t, value_t, key):
    count, _, block = packed.shape
    for i in range(count):
        columns = slice(i * block, (i + 1) * block)
        key_t[:, columns] = packed[i, HEAD_DIM : 2 * HEAD_DIM]
        value_t[:, columns] = packed[i, 2 * HEAD_DIM :]
    key[...] = key_t[...].T
    for i in range(count):
        query = packed[i, :HEAD_DIM] * bf16(HEAD_DIM**-0.5)
        scores = jnp.dot(key[...], query, preferred_element_type=f32)
        highest = jnp.max(scores, axis=0, keepdims=True)
        exponent = jnp.exp(scores - highest)
        totals = jnp.sum(exponent, axis=0, keepdims=True)
        mixture = jnp.dot(value_t[...], exponent.astype(bf16), preferred_element_type=f32)
        out[i] = (mixture / totals).astype(bf16)
        lse[0, i : i + 1, :] = highest + jnp.log(totals)


def attend(packed):
    count, lines, block = packed.shape
    heads = lines // (3 * HEAD_DIM)
    length = count * block
    return pl.pallas_call(
        attend_kernel,
        out_shape=[
            jax.ShapeDtypeStruct((count, heads * HEAD_DIM, block), bf16),
            jax.ShapeDtypeStruct((heads, count, block), f32),
        ],
        grid=(heads,),
        in_specs=[pl.BlockSpec((count, 3 * HEAD_DIM, block), lambda h: (0, h, 0))],
        out_specs=[
            pl.BlockSpec((count, HEAD_DIM, block), lambda h: (0, h, 0)),
            pl.BlockSpec((1, count, block), lambda h: (h, 0, 0)),
        ],
        scratch_shapes=[
            pltpu.VMEM((HEAD_DIM, length), bf16),
            pltpu.VMEM((HEAD_DIM, length), bf16),
            pltpu.VMEM((length, HEAD_DIM), bf16),
        ],
        compiler_params=pltpu.CompilerParams(vmem_limit_bytes=32 << 20),
        cost_estimate=pl.CostEstimate(
            flops=16 * heads * length * length * HEAD_DIM,
            bytes_accessed=8 * heads * length * HEAD_DIM,
            transcendentals=heads * length * length,
        ),
        name="attend",
    )(packed)


def attend_back_kernel(packed, grads, lse, cosine, sine, out, *scratch):
    key_t, key, value_t, query_grad, key_grad, value_grad = scratch
    count, _, block = packed.shape
    rows = min(256, block)
    half = HEAD_DIM // 2
    for i in range(count):
        columns = slice(i * block, (i + 1) * block)
        key_t[:, columns] = packed[i, HEAD_DIM : 2 * HEAD_DIM]
        value_t[:, columns] = packed[i, 2 * HEAD_DIM :]
        key[columns, :] = packed[i, HEAD_DIM : 2 * HEAD_DIM].T
    for i in range(count):
        log_total = lse[0, i : i + 1, :].T
        for c in range(block // rows):
            own = slice(c * rows, (c + 1) * rows)
            query_t = packed[i, :HEAD_DIM, own] * bf16(HEAD_DIM**-0.5)
            grad_t = grads[i, :, own]
            scores = jnp.dot(query_t.T, key_t[...], preferred_element_type=f32)
            weights = jnp.exp(scores - log_total[own])
            pull = jnp.dot(grad_t.T, value_t[...], preferred_element_type=f32)
            centre = jnp.sum(weights * pull, axis=1, keepdims=True)
            score_grad = (weights * (pull - centre)).astype(bf16)
            value_term = jnp.dot(grad_t, weights.astype(bf16), preferred_element_type=f32)
            key_term = jnp.dot(query_t, score_grad, preferred_element_type=f32)
            if i == 0 and c == 0:
                value_grad[...] = value_term
                key_grad[...] = key_term
            else:
                value_grad[...] += value_term
                key_grad[...] += key_term
            query_grad[:, i * block + c * rows : i * block + (c + 1) * rows] = (
                jnp.dot(score_grad, key[...], preferred_element_type=f32) * HEAD_DIM**-0.5
            ).T
    for i in range(count):
        columns = slice(i * block, (i + 1) * block)
        cos, sin = cosine[:, columns], sine[:, columns]
        for first, source in ((0, query_grad), (HEAD_DIM, key_grad)):
            upper, lower = source[:half, columns], source[half:, columns]
            out[i, first : first + half] = (upper * cos + lower * sin).astype(bf16)
            out[i, first + half : first + HEAD_DIM] = (lower * cos - upper * sin).astype(bf16)
        out[i, 2 * HEAD_DIM :] = value_grad[:, columns].astype(bf16)


def attend_back(head, packed, grads, lse, cosine, sine):
    count, _, block = packed.shape
    length = count * block
    lines = 3 * HEAD_DIM
    return pl.pallas_call(
        attend_back_kernel,
        out_shape=jax.ShapeDtypeStruct((count, lines, block), bf16),
        grid=(1,),
        in_specs=[
            pl.BlockSpec((count, lines, block), lambda i: (0, head, 0)),
            pl.BlockSpec((count, HEAD_DIM, block), lambda i: (0, head, 0)),
            pl.BlockSpec((1, count, block), lambda i: (head, 0, 0)),
            whole(cosine),
            whole(sine),
        ],
        out_specs=pl.BlockSpec((count, lines, block), lambda i: (0, 0, 0)),
        scratch_shapes=[
            pltpu.VMEM((HEAD_DIM, length), bf16),
            pltpu.VMEM((length, HEAD_DIM), bf16),
            pltpu.VMEM((HEAD_DIM, length), bf16),
            pltpu.VMEM((HEAD_DIM, length), f32),
            pltpu.VMEM((HEAD_DIM, length), f32),
            pltpu.VMEM((HEAD_DIM, length), f32),
        ],
        compiler_params=pltpu.CompilerParams(vmem_limit_bytes=60 << 20),
        cost_estimate=pl.CostEstimate(
            flops=40 * length * length * HEAD_DIM,
            bytes_accessed=16 * length * HEAD_DIM,
            transcendentals=length * length,
        ),
        name="attend_back",
    )(packed, grads, lse, cosine, sine)


def normalize(rows):
    center = jnp.mean(rows, axis=1, keepdims=True)
    shifted = rows - center
    inverse = lax.rsqrt(jnp.mean(shifted * shifted, axis=1, keepdims=True) + EPSILON)
    return shifted * inverse, inverse


def norm_back(scaled, normed, inverse):
    return inverse * (
        scaled
        - jnp.mean(scaled, axis=1, keepdims=True)
        - normed * jnp.mean(scaled * normed, axis=1, keepdims=True)
    )


def dot(a, b):
    return jnp.dot(a, b, preferred_element_type=f32)


def dot_nt(a, b):
    return lax.dot_general(a, b, (((1,), (1,)), ((), ())), preferred_element_type=f32)


def total(values):
    return jnp.sum(values, axis=0, keepdims=True)


def pack_kernel(ada, ada_bias, embed, gain_one, gain_two, bias_down, out, rows):
    lines = ada.shape[0]
    rows[...] = jnp.zeros_like(rows)
    for n, ref in enumerate((ada_bias, embed, gain_one, gain_two, bias_down)):
        rows[n : n + 1, : ref.shape[1]] = ref[...].astype(f32)
    out[:lines, : ada.shape[1]] = ada[...]
    out[lines:] = rows[...].astype(bf16)


def pack(ada, ada_bias, embed, gain_one, gain_two, bias_down):
    lines, columns = ada.shape
    columns = max(columns, embed.shape[1])
    rows = [x.reshape(1, -1) for x in (ada_bias, embed, gain_one, gain_two, bias_down)]
    return pl.pallas_call(
        pack_kernel,
        out_shape=jax.ShapeDtypeStruct((lines + 16, columns), bf16),
        in_specs=[VMEM] * 6,
        out_specs=VMEM,
        scratch_shapes=[pltpu.VMEM((16, columns), f32)],
        name="pack",
    )(ada, *rows)


def prepare_kernel(columns, per, where, packs, vectors, embeds, mods, wide):
    me, z = where[0], where[1]
    count = packs.shape[0]
    cond = embeds.shape[1]
    rel = jnp.where(me % 2 == z // 2, 0, 1)
    embed = jnp.broadcast_to(packs[rel, cond : cond + 16][1:2, :cond], (8, cond))
    mods[...] = jnp.zeros_like(mods)
    wide[...] = jnp.zeros_like(wide)
    vectors[...] = jnp.zeros_like(vectors)

    def add(r, total_mods):
        owner = me ^ r
        rows = packs[r, cond : cond + 16].astype(f32)
        part = dot(embed, packs[r, :cond, :columns]) + rows[0:1, :columns]
        mods[:, :columns] = part
        wide[:, :per] = rows[0:8, :per]
        embeds[pl.ds(owner, 1)] = rows[1:2, :cond]
        vectors[0:8] += pltpu.roll(wide[...], owner * per, 1)
        return total_mods + pltpu.roll(mods[...], owner * columns, 1)

    flat = lax.fori_loop(0, count, add, jnp.zeros(mods.shape, f32))
    width = vectors.shape[1]
    for n in range(6):
        vectors[8 + n : 9 + n] = flat[0:1, n * width : (n + 1) * width]


def prepare(where, packs, width, per, cond):
    dp_size = packs.shape[0]
    columns = 6 * width // dp_size
    return pl.pallas_call(
        functools.partial(prepare_kernel, columns, per),
        out_shape=[
            jax.ShapeDtypeStruct((16, width), f32),
            jax.ShapeDtypeStruct((dp_size, cond), f32),
        ],
        in_specs=[SMEM, VMEM],
        out_specs=[VMEM] * 2,
        scratch_shapes=[pltpu.VMEM((8, 6 * width), f32), pltpu.VMEM((8, width), f32)],
        compiler_params=pltpu.CompilerParams(vmem_limit_bytes=16 << 20),
        name="prepare",
    )(where, packs)


GAIN_ONE, GAIN_TWO, BIAS_DOWN, SHIFT_ONE, SCALE_ONE, GATE_ONE, SHIFT_TWO, SCALE_TWO, GATE_TWO = (
    slice(n, n + 1) for n in (2, 3, 4, 8, 9, 10, 11, 12, 13)
)


def project_kernel(count, *refs):
    where, tokens, vectors, cosine, sine = refs[:5]
    pieces, (hidden, packed, full, sems) = refs[5 : 5 + count], refs[5 + count :]
    me, z = where[0], where[1]
    wide = full.shape[2] // 3
    copies = load_weights(me, pieces, full, sems)
    gain, scale, shift = vectors[GAIN_ONE], vectors[SCALE_ONE], vectors[SHIFT_ONE]
    normed, _ = normalize(tokens[...].astype(f32))
    hidden[...] = (normed * gain * (1.0 + scale) + shift).astype(bf16)
    cos, sin = cosine[...], sine[...]
    for copy in copies:
        copy.wait()
    for i in range(GROUP):
        projected = dot(hidden[...], full[z ^ i]).T
        for h in range(wide // HEAD_DIM):
            at = 3 * HEAD_DIM * h
            for c in range(2):
                first = c * wide + h * HEAD_DIM
                upper = projected[first : first + HALF]
                lower = projected[first + HALF : first + HEAD_DIM]
                packed[i, at : at + HALF] = (upper * cos - lower * sin).astype(bf16)
                packed[i, at + HALF : at + HEAD_DIM] = (lower * cos + upper * sin).astype(bf16)
                at += HEAD_DIM
            first = 2 * wide + h * HEAD_DIM
            packed[i, at : at + HEAD_DIM] = projected[first : first + HEAD_DIM].astype(bf16)


def project(where, tokens, vectors, cosine, sine, pieces):
    rows, width = tokens.shape
    columns = pieces[0].shape[2]
    shapes = [
        jax.ShapeDtypeStruct((rows, width), bf16),
        jax.ShapeDtypeStruct((GROUP, columns, rows), bf16),
    ]
    return pl.pallas_call(
        functools.partial(project_kernel, len(pieces)),
        out_shape=shapes,
        grid=(1,),
        in_specs=[SMEM]
        + [whole(x) for x in (tokens, vectors, cosine, sine)]
        + [ANY] * len(pieces),
        out_specs=[whole(x) for x in shapes],
        scratch_shapes=[
            pltpu.VMEM((GROUP, width, columns), bf16),
            pltpu.SemaphoreType.DMA((GROUP * len(pieces),)),
        ],
        compiler_params=pltpu.CompilerParams(vmem_limit_bytes=32 << 20),
        cost_estimate=pl.CostEstimate(
            flops=2 * rows * width * GROUP * columns,
            bytes_accessed=2 * GROUP * (width + rows) * columns,
            transcendentals=0,
        ),
        name="project",
    )(where, tokens, vectors, cosine, sine, *pieces)


GELU_A = math.sqrt(2.0 / math.pi)
GELU_B = 0.044715


def feed_kernel(count, *refs):
    where, tokens, upstream, vectors, mixtures = refs[:5]
    pieces, refs = refs[5 : 5 + count], refs[5 + count :]
    output, residual_grad, out_hidden, out_branch_one, out_branch_two = refs[:5]
    activated, pre_grad, attention, sums, bias_sums = refs[5:10]
    mixture_grads, full, bias_up, slope, keep_one, keep_two, sems = refs[10:]
    wide = mixtures.shape[1]
    hidden = bias_up.shape[1]
    of_out = slice(0, wide)
    of_up = slice(wide, wide + hidden)
    of_down = slice(wide + hidden, wide + 2 * hidden)
    of_bias = slice(wide + 2 * hidden, wide + 2 * hidden + 64)
    copies = load_weights(where[0], pieces, full, sems)
    gain, scale, shift = vectors[GAIN_TWO], vectors[SCALE_TWO], vectors[SHIFT_TWO]
    gate_one, gate_two, bias_down = vectors[GATE_ONE], vectors[GATE_TWO], vectors[BIAS_DOWN]
    for r in range(GROUP):
        attention[r] = mixtures[r].T
    for copy in copies:
        copy.wait()
    for t in range(GROUP):
        bias_up[t : t + 1] = full[t, :, of_bias].T[0:1].astype(f32)
    branch_one = dot_nt(attention[0], full[0, :, of_out])
    for r in range(1, GROUP):
        branch_one = branch_one + dot_nt(attention[r], full[r, :, of_out])
    keep_one[...] = branch_one
    residual = tokens[...].astype(f32) + gate_one * branch_one
    normed, _ = normalize(residual)
    out_hidden[...] = (normed * gain * (1.0 + scale) + shift).astype(bf16)

    keep_two[...] = jnp.broadcast_to(bias_down, keep_two.shape)

    def forward(t, carry):
        pre = dot(out_hidden[...], full[t, :, of_up]) + bias_up[pl.ds(t, 1)]
        inner = jnp.tanh(GELU_A * (pre + GELU_B * pre * pre * pre))
        activated[t] = (0.5 * pre * (1.0 + inner)).astype(bf16)
        slope[t] = 0.5 * (1.0 + inner) + (
            0.5 * GELU_A * pre * (1.0 - inner * inner) * (1.0 + 3.0 * GELU_B * pre * pre)
        )
        keep_two[...] += dot_nt(activated[t], full[t, :, of_down])
        return carry

    lax.fori_loop(0, GROUP, forward, 0)
    branch_two = keep_two[...]
    residual = tokens[...].astype(f32) + gate_one * keep_one[...]
    output[...] = (residual + gate_two * branch_two).astype(bf16)
    grad = upstream[...].astype(f32)
    branch_two_grad = gate_two * grad
    out_branch_two[...] = branch_two_grad.astype(bf16)
    sums[2:3] = total(grad * branch_two)
    sums[4:5] = total(out_branch_two[...].astype(f32))

    keep_two[...] = jnp.zeros_like(keep_two)

    def backward(t, carry):
        act_grad = dot(out_branch_two[...], full[t, :, of_down])
        pre_grad[t] = (act_grad * slope[t]).astype(bf16)
        bias_sums[pl.ds(t, 1)] = total(pre_grad[t].astype(f32))
        keep_two[...] += dot_nt(pre_grad[t], full[t, :, of_up])
        return carry

    lax.fori_loop(0, GROUP, backward, 0)
    hidden_grad = keep_two[...]
    residual = tokens[...].astype(f32) + gate_one * keep_one[...]
    normed, inverse = normalize(residual)
    sums[0:1] = total(hidden_grad)
    sums[1:2] = total(hidden_grad * normed)
    grad = upstream[...].astype(f32) + norm_back(
        hidden_grad * gain * (1.0 + scale), normed, inverse
    )
    residual_grad[...] = grad
    sums[3:4] = total(grad * keep_one[...])
    out_branch_one[...] = (gate_one * grad).astype(bf16)
    for r in range(GROUP):
        back = dot(out_branch_one[...], full[r, :, of_out])
        mixture_grads[r] = back.astype(bf16).T


def feed(where, tokens, upstream, vectors, mixtures, pieces):
    rows, width = tokens.shape
    wide = mixtures.shape[1]
    columns = pieces[0].shape[2]
    hidden = width

    def shape(dtype, *lengths):
        return jax.ShapeDtypeStruct(lengths, dtype)

    shapes = [
        shape(bf16, rows, width),
        shape(f32, rows, width),
        shape(bf16, rows, width),
        shape(bf16, rows, width),
        shape(bf16, rows, width),
        shape(bf16, GROUP, rows, hidden),
        shape(bf16, GROUP, rows, hidden),
        shape(bf16, GROUP, rows, wide),
        shape(f32, 5, width),
        shape(f32, GROUP, hidden),
        shape(bf16, GROUP, wide, rows),
    ]
    return pl.pallas_call(
        functools.partial(feed_kernel, len(pieces)),
        out_shape=shapes,
        grid=(1,),
        in_specs=[SMEM]
        + [whole(x) for x in (tokens, upstream, vectors, mixtures)]
        + [ANY] * len(pieces),
        out_specs=[whole(x) for x in shapes],
        scratch_shapes=[
            pltpu.VMEM((GROUP, width, columns), bf16),
            pltpu.VMEM((GROUP, hidden), f32),
            pltpu.VMEM((GROUP, rows, hidden), f32),
            pltpu.VMEM((rows, width), f32),
            pltpu.VMEM((rows, width), f32),
            pltpu.SemaphoreType.DMA((GROUP * len(pieces),)),
        ],
        compiler_params=pltpu.CompilerParams(vmem_limit_bytes=60 << 20),
        cost_estimate=pl.CostEstimate(
            flops=4 * rows * width * GROUP * columns,
            bytes_accessed=2 * GROUP * (width + rows) * columns,
            transcendentals=GROUP * rows * hidden,
        ),
        name="feed",
    )(where, tokens, upstream, vectors, mixtures, *pieces)


def feed_grads_kernel(hidden, branch_one, branch_two, act, pre, attention, sums, out):
    t = pl.program_id(0)
    up = dot(hidden[...].T, pre[0]).astype(bf16)
    down = dot(branch_two[...].T, act[0]).astype(bf16)
    own = dot(branch_one[...].T, attention[0]).astype(bf16)
    line = lax.broadcasted_iota(jnp.int32, (8, 1), 0)
    lines = jnp.where(line == 0, sums[pl.ds(t, 1)], 0.0)
    for n in (1, 2):
        lines = jnp.where(line == n, sums[3 + n : 4 + n], lines)
    lines = jnp.concatenate([lines, jnp.zeros((120, lines.shape[1]), f32)])
    extra = lines.T[:, :64].astype(bf16)
    value = jnp.concatenate([own, up, down, extra], axis=1)
    if len(out.shape) == 3:
        out[0] = value
    else:
        out[...] = value.reshape(out.shape)


def feed_grads(dp_size, hidden, branch_one, branch_two, act, pre, attention, sums):
    rows, width = hidden.shape
    wide, inner = attention.shape[2], act.shape[2]
    columns = wide + 2 * inner + 64
    if dp_size == 8:
        shape = (dp_size, GROUP, width // dp_size, columns)
        out_spec = pl.BlockSpec((dp_size, 1, width // dp_size, columns), lambda t: (0, t, 0, 0))
    else:
        shape = (GROUP, width, columns)
        out_spec = pl.BlockSpec((1, width, columns), lambda t: (t, 0, 0))
    return pl.pallas_call(
        feed_grads_kernel,
        out_shape=jax.ShapeDtypeStruct(shape, bf16),
        grid=(GROUP,),
        in_specs=[whole(hidden)] * 3
        + [pl.BlockSpec((1, rows, inner), lambda t: (t, 0, 0))] * 2
        + [pl.BlockSpec((1, rows, wide), lambda t: (t, 0, 0)), whole(sums)],
        out_specs=out_spec,
        compiler_params=pltpu.CompilerParams(vmem_limit_bytes=60 << 20),
        cost_estimate=pl.CostEstimate(
            flops=2 * rows * width * GROUP * columns,
            bytes_accessed=2 * GROUP * (width + rows) * columns,
            transcendentals=0,
        ),
        name="feed_grads",
    )(hidden, branch_one, branch_two, act, pre, attention, sums)


def join_heads(received, i):
    return jnp.concatenate(
        [ref[i, c * HEAD_DIM : (c + 1) * HEAD_DIM] for c in range(3) for ref in received]
    )


def project_grads_kernel(heads, where, hidden, *refs):
    received, outs = refs[:heads], refs[heads:]
    me = where[0]
    for parity in range(2):

        @pl.when(me % 2 == parity)
        def _():
            hidden_t = hidden[...].T
            for i in range(GROUP):
                value = dot_nt(hidden_t, join_heads(received, i)).astype(bf16)
                store_blocks(me, parity, outs, i, value)


def project_grads(dp_size, where, hidden, received):
    rows, width = hidden.shape
    heads = len(received)
    columns = 3 * heads * HEAD_DIM
    shapes = grad_shapes(dp_size, width, columns)
    return pl.pallas_call(
        functools.partial(project_grads_kernel, heads),
        out_shape=shapes,
        grid=(1,),
        in_specs=[SMEM] + [whole(x) for x in (hidden, *received)],
        out_specs=[whole(x) for x in shapes],
        compiler_params=pltpu.CompilerParams(vmem_limit_bytes=32 << 20),
        cost_estimate=pl.CostEstimate(
            flops=2 * rows * width * GROUP * columns,
            bytes_accessed=2 * GROUP * (width + rows) * columns,
            transcendentals=0,
        ),
        name="project_grads",
    )(where, hidden, *received)


def project_back_kernel(count, heads, *refs):
    where, tokens, vectors, residual_grad = refs[:4]
    received, refs = refs[4 : 4 + heads], refs[4 + heads :]
    pieces, (input_grad, sums, full, sems) = refs[:count], refs[count:]
    me, z = where[0], where[1]
    copies = load_weights(me, pieces, full, sems)
    gain, scale = vectors[GAIN_ONE], vectors[SCALE_ONE]
    normed, inverse = normalize(tokens[...].astype(f32))
    for copy in copies:
        copy.wait()
    hidden_grad = None
    for i in range(GROUP):
        term = dot_nt(join_heads(received, i).T, full[z ^ i])
        hidden_grad = term if hidden_grad is None else hidden_grad + term
    sums[0:1] = total(hidden_grad)
    sums[1:2] = total(hidden_grad * normed)
    input_grad[...] = (
        residual_grad[...] + norm_back(hidden_grad * gain * (1.0 + scale), normed, inverse)
    ).astype(bf16)


def project_back(where, tokens, vectors, residual_grad, received, pieces):
    rows, width = tokens.shape
    columns = pieces[0].shape[2]
    shapes = [
        jax.ShapeDtypeStruct((rows, width), bf16),
        jax.ShapeDtypeStruct((2, width), f32),
    ]
    return pl.pallas_call(
        functools.partial(project_back_kernel, len(pieces), len(received)),
        out_shape=shapes,
        grid=(1,),
        in_specs=[SMEM]
        + [whole(x) for x in (tokens, vectors, residual_grad, *received)]
        + [ANY] * len(pieces),
        out_specs=[whole(x) for x in shapes],
        scratch_shapes=[
            pltpu.VMEM((GROUP, width, columns), bf16),
            pltpu.SemaphoreType.DMA((GROUP * len(pieces),)),
        ],
        compiler_params=pltpu.CompilerParams(vmem_limit_bytes=32 << 20),
        cost_estimate=pl.CostEstimate(
            flops=2 * rows * width * GROUP * columns,
            bytes_accessed=2 * GROUP * (width + rows) * columns,
            transcendentals=0,
        ),
        name="project_back",
    )(where, tokens, vectors, residual_grad, *received, *pieces)


def einsum(spec, a, b):
    return jnp.einsum(spec, a, b, preferred_element_type=f32)


def per_device(
    dp_size,
    tokens,
    time_embed,
    ada_weight,
    ada_bias,
    norm1_gain,
    qkv_weight,
    out_weight,
    norm2_gain,
    up_weight,
    up_bias,
    down_weight,
    down_bias,
    out_grad,
):
    me = lax.axis_index(DP)
    z = lax.axis_index(TENSOR)
    position = lax.axis_index(TEAM)
    where = jnp.stack([me, z]).astype(jnp.int32)
    rows, width = tokens.shape
    heads = qkv_weight.shape[2] // HEAD_DIM
    wide = heads * HEAD_DIM
    hidden = up_weight.shape[1]
    cond = time_embed.shape[1]
    per = norm1_gain.shape[0]

    first_shard = jnp.concatenate([*qkv_weight], axis=1)
    packs = pack(ada_weight, ada_bias, time_embed, norm1_gain, norm2_gain, down_bias)
    packs, *others = meet(first_step(packs, dp_size), *send_planes(first_shard, dp_size))
    packs = spread_dp(packs, dp_size)
    first_own = jnp.stack([first_shard, *others])
    extra = jnp.pad(up_bias[:, None], ((0, 0), (0, 63)))
    second_shard = jnp.concatenate([out_weight.T, up_weight, down_weight.T, extra], axis=1)
    tokens, first_own = meet(tokens, first_own)
    sent = send_tokens(tokens, dp_size)
    first_pieces = gather_weights(first_own, gather_sides(first_own, dp_size), dp_size)
    moved = settle(tokens, sent)
    second_own = lax.all_gather(second_shard, TENSOR, axis=0, tiled=False)

    columns = ada_weight.shape[1]
    vectors, embeds = prepare(where, packs, width, per, cond)
    ada_full = packs[:, :cond, :columns]
    gain_one, gain_two = vectors[GAIN_ONE], vectors[GAIN_TWO]
    scale_one, scale_two = vectors[SCALE_ONE], vectors[SCALE_TWO]

    frequency = jnp.exp(
        jnp.arange(HALF, dtype=f32) * (-2.0 * math.log(ROPE_BASE) / HEAD_DIM)
    )
    angles = frequency[:, None] * jnp.arange(GROUP * rows, dtype=jnp.int32).astype(f32)[None, :]
    cosine, sine = jnp.cos(angles), jnp.sin(angles)
    cosine_own = lax.dynamic_slice_in_dim(cosine, position * rows, rows, axis=1)
    sine_own = lax.dynamic_slice_in_dim(sine, position * rows, rows, axis=1)

    cosine_own, second_own = meet(cosine_own, second_own)
    second_sides = gather_sides(second_own, dp_size)
    hidden_one, packed = project(where, moved, vectors, cosine_own, sine_own, first_pieces)
    packed = exchange(packed)
    out_grad, packed = meet(out_grad, packed)
    upstream = send_tokens(out_grad, dp_size)
    mixtures, lse = attend(packed)
    lse, *second_sides = meet(lse, *second_sides)
    second_pieces = gather_weights(second_own, second_sides, dp_size)
    mixtures, upstream = meet(mixtures, upstream)
    upstream = settle(out_grad, upstream)
    mixtures = exchange(mixtures)

    outs = feed(where, moved, upstream, vectors, mixtures, second_pieces)
    output, residual_grad, hidden_two, branch_one_grad, branch_two_grad = outs[:5]
    activated, pre_grad, attention, feed_sums, bias_sums, mixture_grads = outs[5:]
    incoming = exchange(mixture_grads)
    sums_two = jnp.concatenate(
        [bias_sums, feed_sums[1:2] * (1.0 + scale_two), feed_sums[4:5]]
    )
    second_grad = feed_grads(
        dp_size,
        hidden_two,
        branch_one_grad,
        branch_two_grad,
        activated,
        pre_grad,
        attention,
        jnp.pad(sums_two, ((0, 2), (0, 0))),
    )
    incoming, second_grad, output = meet(incoming, second_grad, output)
    output = regroup(output, dp_size)
    if dp_size == 8:
        second_sum = lax.psum_scatter(second_grad, DP, scatter_dimension=0, tiled=False)
    else:
        second_sum = lax.psum_scatter(second_grad, DP, scatter_dimension=1, tiled=True)

    received = []
    for h in range(heads):
        received.append(exchange(attend_back(h, packed, incoming, lse, cosine, sine)))
        if h == 0:
            incoming, output = meet(incoming, output)
    first_grad = list(project_grads(dp_size, where, hidden_one, received))
    first_far = reduce_cores(first_grad, dp_size)
    if dp_size == 8:
        first_diagonal = reduce_diagonal(first_grad, first_far, dp_size)
        *received, first_diagonal, second_sum = meet(*received, first_diagonal, second_sum)
        first_half = reduce_first(first_diagonal, dp_size)
    input_grad, project_sums = project_back(
        where, moved, vectors, residual_grad, received, first_pieces
    )
    sent = send_tokens(input_grad, dp_size)
    pull_one, pull_two = project_sums[1:2], feed_sums[1:2]
    mine = jnp.concatenate(
        [
            project_sums[:1],
            pull_one * gain_one,
            feed_sums[3:4],
            feed_sums[:1],
            pull_two * gain_two,
            feed_sums[2:3],
            pull_one * (1.0 + scale_one),
        ]
    )
    second_sum = lax.psum_scatter(second_sum, TENSOR, scatter_dimension=0, tiled=False)
    second_sum = second_sum.astype(f32)

    def widen(mods, swap, mask):
        return jnp.concatenate([mods, swap(mods, dp_size, mask)])

    mods = mine[None]
    mask = 2
    while mask < dp_size:
        mods = widen(mods, swap_dp, mask)
        mask *= 2
    mods = mods + swap_dp(mods, dp_size, 1)
    first_sides = None
    if dp_size == 8:
        first_sides = reduce_sides(first_grad, first_far, first_half, dp_size)
    first_sum = reduce_second(first_grad, first_far, first_sides, dp_size)
    mods, first_sum, second_sum = meet(mods, first_sum, second_sum)
    first_sum = reduce_planes(first_sum)
    mods = mods + swap_z(mods, dp_size, 1)
    mods = mods.at[:, :6].set(mods[:, :6].astype(bf16).astype(f32))
    mods = widen(mods, swap_z, 2)
    tail = jnp.sum(mods[:, 6:], axis=0)
    mods = mods[:, :6]
    input_grad = settle(input_grad, sent)
    out_out = second_sum[:, :wide].T
    up_out = second_sum[:, wide : wide + hidden]
    down_out = second_sum[:, wide + hidden : wide + 2 * hidden].T
    bias_up_out, gain_two_out, bias_down_out = second_sum[:, wide + 2 * hidden :].T[:3]
    qkv_out = jnp.stack(jnp.split(first_sum, 3, axis=1))

    rel = jnp.arange(dp_size)
    quads = dp_size // 2
    seq_at = (me // 2 ^ rel % quads) * 2 + (z // 2 ^ rel // quads)
    mods = mods.reshape(dp_size, 6 * width).astype(bf16)
    own_mods = lax.dynamic_slice_in_dim(mods, me * columns, columns, axis=1)
    pick = (seq_at[:, None] == jnp.arange(dp_size)[None, :]).astype(bf16)
    ada_out = einsum("sc,se->ce", jnp.dot(pick, embeds.astype(bf16)), own_mods)
    ada_bias_out = jnp.sum(own_mods.astype(f32), axis=0)
    mine_at = (seq_at == me).astype(f32)
    own_row = jnp.sum(mods.astype(f32) * mine_at[:, None], axis=0).astype(bf16)
    own_row = reorder(own_row.reshape(dp_size, columns), me)
    time_out = jnp.sum(einsum("oe,oce->oc", own_row, ada_full), axis=0, keepdims=True)

    def own_part(row):
        return lax.dynamic_slice_in_dim(row, me * per, per)

    return (
        output,
        input_grad,
        time_out,
        ada_out,
        ada_bias_out,
        own_part(tail[0]),
        qkv_out,
        out_out,
        gain_two_out,
        up_out,
        bias_up_out,
        down_out,
        bias_down_out,
    )


def solution(mesh):
    dp_size, tensor_size = mesh.shape["dp"], mesh.shape["tensor"]
    parts = jax.sharding.Mesh(
        mesh.devices.reshape(dp_size // 2, 2, tensor_size // 2, 2), AXES
    )
    in_specs = (
        P(AXES, None),
        P(DP, None),
        P(None, DP),
        P(DP),
        P(DP),
        P(None, DP, TENSOR),
        P(TENSOR, DP),
        P(DP),
        P(DP, TENSOR),
        P(TENSOR + DP),
        P(TENSOR, DP),
        P(DP),
        P(AXES, None),
    )
    out_specs = (
        P(AXES, None),
        P(AXES, None),
        P(DP, None),
        P(None, DP),
        P(DP),
        P(DP),
        P(None, DP, TENSOR),
        P(TENSOR, DP),
        P(DP),
        P(DP, TENSOR),
        P(TENSOR + DP),
        P(TENSOR, DP),
        P(DP),
    )
    return jax.shard_map(
        functools.partial(per_device, dp_size),
        mesh=parts,
        in_specs=in_specs,
        out_specs=out_specs,
        check_vma=False,
    )
```

```python
import functools
import math

import jax
import jax.numpy as jnp
from jax import lax
from jax.experimental import pallas as pl
from jax.experimental.pallas import tpu as pltpu
from jax.sharding import PartitionSpec as P

HEAD_DIM = 64
EPSILON = 1e-05
ROPE_BASE = 10000.0
GROUP = 4
DP = ("quad", "core")
TENSOR = ("high", "low")
AXES = DP + TENSOR
TEAM = ("core", "low")
f32 = jnp.float32
bf16 = jnp.bfloat16
VMEM = pl.BlockSpec(memory_space=pltpu.VMEM)
SMEM = pl.BlockSpec(memory_space=pltpu.SMEM)
ANY = pl.BlockSpec(memory_space=pl.ANY)
HALF = HEAD_DIM // 2


def whole(array):
    return pl.BlockSpec(
        array.shape, lambda *at: (0,) * len(array.shape), pipeline_mode=pl.Buffered(1)
    )


def permute(array, dp_size, target):
    pairs = []
    for d in range(dp_size):
        for z in range(GROUP):
            to_d, to_z = target(d, z)
            if (d, z) != (to_d, to_z):
                pairs.append((d * GROUP + z, to_d * GROUP + to_z))
    return lax.ppermute(array, AXES, pairs)


def swap_dp(array, dp_size, mask):
    return permute(array, dp_size, lambda d, z: (d ^ mask, z))


def swap_z(array, dp_size, mask):
    return permute(array, dp_size, lambda d, z: (d, z ^ mask))


def send_tokens(array, dp_size):
    return permute(array, dp_size, lambda d, z: (d // 2 * 2 + z // 2, d % 2 * 2 + z % 2))


def settle(array, moved):
    stay = lax.axis_index("core") == lax.axis_index("high")
    return jnp.where(stay, array, moved)


def regroup(array, dp_size):
    return settle(array, send_tokens(array, dp_size))


def meet(*arrays):
    return lax.optimization_barrier(arrays)


def exchange(blocks):
    return lax.all_to_all(blocks, TEAM, 0, 0, tiled=True)


def reorder(array, index):
    count = array.shape[0]
    for k in range(count.bit_length() - 1):
        pairs = array.reshape(count >> (k + 1), 2, 1 << k, *array.shape[1:])
        pairs = jnp.concatenate([pairs[:, 1:], pairs[:, :1]], axis=1).reshape(array.shape)
        array = jnp.where((index >> k) % 2 == 1, pairs, array)
    return array


def first_step(array, dp_size):
    return jnp.stack([array, swap_dp(array, dp_size, 2)])


def spread_dp(blocks, dp_size):
    array = blocks[0]
    mask = 4
    while mask < dp_size:
        blocks = jnp.concatenate([blocks, swap_dp(blocks, dp_size, mask)])
        mask *= 2
    blocks = jnp.stack([blocks, swap_dp(blocks, dp_size, 1)], axis=1)
    return blocks.reshape(dp_size, *array.shape)


WHOLE = ((0, 0), (2, 0), (4, 0), (6, 0), (1, 0), (3, 0), (5, 0), (7, 0))
HALVES = WHOLE[:4] + ((6, 2),) + WHOLE[4:] + ((7, 2),)


def send_planes(shard, dp_size):
    return [swap_z(shard, dp_size, t) for t in range(1, GROUP)]


def gather_sides(own, dp_size):
    if dp_size != 8:
        return ()
    return swap_dp(own, dp_size, 2), swap_dp(own, dp_size, 4)


def gather_weights(own, sides, dp_size):
    if dp_size != 8:
        return (lax.all_gather(own, DP, axis=1, tiled=True),)
    x, y = sides
    near = (own, x, y, swap_dp(x[:2], dp_size, 4), swap_dp(y[2:], dp_size, 2))
    return near + tuple(swap_dp(piece, dp_size, 1) for piece in near)


def load_weights(me, pieces, full, sems, flip=None):
    if len(pieces) == 1:
        flips = [t if flip is None else t ^ flip for t in range(GROUP)]
        copies = [
            pltpu.make_async_copy(pieces[0].at[t], full.at[flips[t]], sems.at[t])
            for t in range(GROUP)
        ]
    else:
        copies = []
        for i, (piece, (rel, first)) in enumerate(
            zip(pieces, HALVES if len(pieces) == len(HALVES) else WHOLE)
        ):
            count, rows = piece.shape[:2]
            start = pl.multiple_of((me ^ rel) * rows, rows)
            if flip is None:
                place = full.at[first : first + count, pl.ds(start, rows)]
                copies.append(pltpu.make_async_copy(piece, place, sems.at[i]))
                continue
            for t in range(count):
                place = full.at[(first + t) ^ flip, pl.ds(start, rows)]
                sem = sems.at[GROUP * i + t]
                copies.append(pltpu.make_async_copy(piece.at[t], place, sem))
    for copy in copies:
        copy.start()
    return copies


def store_blocks(me, parity, outs, slot, value):
    if len(outs) == 1:
        outs[0][slot] = value
        return
    rows = outs[0].shape[2]
    for owner in range(2 * outs[0].shape[0]):
        out = outs[(owner + parity) % 2]
        out[(me ^ owner) >> 1, slot] = value[owner * rows : (owner + 1) * rows]


def grad_shapes(dp_size, width, columns):
    if dp_size != 8:
        return [jax.ShapeDtypeStruct((GROUP, width, columns), bf16)]
    return [jax.ShapeDtypeStruct((dp_size // 2, GROUP, width // dp_size, columns), bf16)] * 2


def plus(a, b):
    return (a.astype(f32) + b.astype(f32)).astype(bf16)


def reduce_cores(parts, dp_size):
    return swap_dp(parts[1], dp_size, 1) if dp_size == 8 else None


def reduce_diagonal(parts, far, dp_size):
    return plus(parts[0][3], far[3]) if dp_size == 8 else None


def reduce_first(diagonal, dp_size):
    if dp_size != 8:
        return None
    return swap_dp(diagonal[:2], dp_size, 2), swap_dp(diagonal[2:], dp_size, 4)


def reduce_sides(parts, far, half, dp_size):
    if dp_size != 8:
        return None
    x = parts[0][1].astype(f32) + far[1].astype(f32)
    y = parts[0][2].astype(f32) + far[2].astype(f32)
    x = jnp.concatenate([x[:2], x[2:] + half[1].astype(f32)]).astype(bf16)
    y = jnp.concatenate([y[:2] + half[0].astype(f32), y[2:]]).astype(bf16)
    return x, y


def reduce_second(parts, far, sides, dp_size):
    if dp_size != 8:
        return lax.psum_scatter(parts[0], DP, scatter_dimension=1, tiled=True).astype(f32)
    from_x = swap_dp(sides[0], dp_size, 2)
    from_y = swap_dp(sides[1], dp_size, 4)
    own = parts[0][0].astype(f32) + far[0].astype(f32)
    return own + from_x.astype(f32) + from_y.astype(f32)


def reduce_planes(own):
    terms = lax.all_to_all(own.astype(bf16), TENSOR, 0, 0, tiled=True)
    return jnp.sum(terms.astype(f32), axis=0)


def attend_kernel(packed, out, lse, key_t, value_t, key):
    count, _, block = packed.shape
    for i in range(count):
        columns = slice(i * block, (i + 1) * block)
        key_t[:, columns] = packed[i, HEAD_DIM : 2 * HEAD_DIM]
        value_t[:, columns] = packed[i, 2 * HEAD_DIM :]
    key[...] = key_t[...].T
    for i in range(count):
        query = packed[i, :HEAD_DIM] * bf16(HEAD_DIM**-0.5)
        scores = jnp.dot(key[...], query, preferred_element_type=f32)
        highest = jnp.max(scores, axis=0, keepdims=True)
        exponent = jnp.exp(scores - highest)
        totals = jnp.sum(exponent, axis=0, keepdims=True)
        mixture = jnp.dot(value_t[...], exponent.astype(bf16), preferred_element_type=f32)
        out[i] = (mixture / totals).astype(bf16)
        lse[0, i : i + 1, :] = highest + jnp.log(totals)


def attend(packed):
    count, lines, block = packed.shape
    heads = lines // (3 * HEAD_DIM)
    length = count * block
    return pl.pallas_call(
        attend_kernel,
        out_shape=[
            jax.ShapeDtypeStruct((count, heads * HEAD_DIM, block), bf16),
            jax.ShapeDtypeStruct((heads, count, block), f32),
        ],
        grid=(heads,),
        in_specs=[pl.BlockSpec((count, 3 * HEAD_DIM, block), lambda h: (0, h, 0))],
        out_specs=[
            pl.BlockSpec((count, HEAD_DIM, block), lambda h: (0, h, 0)),
            pl.BlockSpec((1, count, block), lambda h: (h, 0, 0)),
        ],
        scratch_shapes=[
            pltpu.VMEM((HEAD_DIM, length), bf16),
            pltpu.VMEM((HEAD_DIM, length), bf16),
            pltpu.VMEM((length, HEAD_DIM), bf16),
        ],
        compiler_params=pltpu.CompilerParams(vmem_limit_bytes=32 << 20),
        cost_estimate=pl.CostEstimate(
            flops=16 * heads * length * length * HEAD_DIM,
            bytes_accessed=8 * heads * length * HEAD_DIM,
            transcendentals=heads * length * length,
        ),
        name="attend",
    )(packed)


def attend_back_kernel(packed, grads, lse, cosine, sine, out, *scratch):
    key_t, key, value_t, query_grad, key_grad, value_grad = scratch
    count, _, block = packed.shape
    rows = min(256, block)
    half = HEAD_DIM // 2
    for i in range(count):
        columns = slice(i * block, (i + 1) * block)
        key_t[:, columns] = packed[i, HEAD_DIM : 2 * HEAD_DIM]
        value_t[:, columns] = packed[i, 2 * HEAD_DIM :]
        key[columns, :] = packed[i, HEAD_DIM : 2 * HEAD_DIM].T
    for i in range(count):
        log_total = lse[0, i : i + 1, :].T
        for c in range(block // rows):
            own = slice(c * rows, (c + 1) * rows)
            query_t = packed[i, :HEAD_DIM, own] * bf16(HEAD_DIM**-0.5)
            grad_t = grads[i, :, own]
            scores = jnp.dot(query_t.T, key_t[...], preferred_element_type=f32)
            weights = jnp.exp(scores - log_total[own])
            pull = jnp.dot(grad_t.T, value_t[...], preferred_element_type=f32)
            centre = jnp.sum(weights * pull, axis=1, keepdims=True)
            score_grad = (weights * (pull - centre)).astype(bf16)
            value_term = jnp.dot(grad_t, weights.astype(bf16), preferred_element_type=f32)
            key_term = jnp.dot(query_t, score_grad, preferred_element_type=f32)
            if i == 0 and c == 0:
                value_grad[...] = value_term
                key_grad[...] = key_term
            else:
                value_grad[...] += value_term
                key_grad[...] += key_term
            query_grad[:, i * block + c * rows : i * block + (c + 1) * rows] = (
                jnp.dot(score_grad, key[...], preferred_element_type=f32) * HEAD_DIM**-0.5
            ).T
    for i in range(count):
        columns = slice(i * block, (i + 1) * block)
        cos, sin = cosine[:, columns], sine[:, columns]
        for first, source in ((0, query_grad), (HEAD_DIM, key_grad)):
            upper, lower = source[:half, columns], source[half:, columns]
            out[i, first : first + half] = (upper * cos + lower * sin).astype(bf16)
            out[i, first + half : first + HEAD_DIM] = (lower * cos - upper * sin).astype(bf16)
        out[i, 2 * HEAD_DIM :] = value_grad[:, columns].astype(bf16)


def attend_back(head, packed, grads, lse, cosine, sine):
    count, _, block = packed.shape
    length = count * block
    lines = 3 * HEAD_DIM
    return pl.pallas_call(
        attend_back_kernel,
        out_shape=jax.ShapeDtypeStruct((count, lines, block), bf16),
        grid=(1,),
        in_specs=[
            pl.BlockSpec((count, lines, block), lambda i: (0, head, 0)),
            pl.BlockSpec((count, HEAD_DIM, block), lambda i: (0, head, 0)),
            pl.BlockSpec((1, count, block), lambda i: (head, 0, 0)),
            whole(cosine),
            whole(sine),
        ],
        out_specs=pl.BlockSpec((count, lines, block), lambda i: (0, 0, 0)),
        scratch_shapes=[
            pltpu.VMEM((HEAD_DIM, length), bf16),
            pltpu.VMEM((length, HEAD_DIM), bf16),
            pltpu.VMEM((HEAD_DIM, length), bf16),
            pltpu.VMEM((HEAD_DIM, length), f32),
            pltpu.VMEM((HEAD_DIM, length), f32),
            pltpu.VMEM((HEAD_DIM, length), f32),
        ],
        compiler_params=pltpu.CompilerParams(vmem_limit_bytes=60 << 20),
        cost_estimate=pl.CostEstimate(
            flops=40 * length * length * HEAD_DIM,
            bytes_accessed=16 * length * HEAD_DIM,
            transcendentals=length * length,
        ),
        name="attend_back",
    )(packed, grads, lse, cosine, sine)


def normalize(rows):
    center = jnp.mean(rows, axis=1, keepdims=True)
    shifted = rows - center
    inverse = lax.rsqrt(jnp.mean(shifted * shifted, axis=1, keepdims=True) + EPSILON)
    return shifted * inverse, inverse


def norm_back(scaled, normed, inverse):
    return inverse * (
        scaled
        - jnp.mean(scaled, axis=1, keepdims=True)
        - normed * jnp.mean(scaled * normed, axis=1, keepdims=True)
    )


def dot(a, b):
    return jnp.dot(a, b, preferred_element_type=f32)


def dot_nt(a, b):
    return lax.dot_general(a, b, (((1,), (1,)), ((), ())), preferred_element_type=f32)


def total(values):
    return jnp.sum(values, axis=0, keepdims=True)


def pack_kernel(ada, ada_bias, embed, gain_one, gain_two, bias_down, out, rows):
    lines = ada.shape[0]
    rows[...] = jnp.zeros_like(rows)
    for n, ref in enumerate((ada_bias, embed, gain_one, gain_two, bias_down)):
        rows[n : n + 1, : ref.shape[1]] = ref[...].astype(f32)
    out[:lines, : ada.shape[1]] = ada[...]
    out[lines:] = rows[...].astype(bf16)


def pack(ada, ada_bias, embed, gain_one, gain_two, bias_down):
    lines, columns = ada.shape
    columns = max(columns, embed.shape[1])
    rows = [x.reshape(1, -1) for x in (ada_bias, embed, gain_one, gain_two, bias_down)]
    return pl.pallas_call(
        pack_kernel,
        out_shape=jax.ShapeDtypeStruct((lines + 16, columns), bf16),
        in_specs=[VMEM] * 6,
        out_specs=VMEM,
        scratch_shapes=[pltpu.VMEM((16, columns), f32)],
        name="pack",
    )(ada, *rows)


def prepare_kernel(columns, per, where, packs, vectors, embeds, mods, wide):
    me, z = where[0], where[1]
    count = packs.shape[0]
    cond = embeds.shape[1]
    rel = jnp.where(me % 2 == z // 2, 0, 1)
    embed = jnp.broadcast_to(packs[rel, cond : cond + 16][1:2, :cond], (8, cond))
    mods[...] = jnp.zeros_like(mods)
    wide[...] = jnp.zeros_like(wide)
    vectors[...] = jnp.zeros_like(vectors)

    def add(r, total_mods):
        owner = me ^ r
        rows = packs[r, cond : cond + 16].astype(f32)
        part = dot(embed, packs[r, :cond, :columns]) + rows[0:1, :columns]
        mods[:, :columns] = part
        wide[:, :per] = rows[0:8, :per]
        embeds[pl.ds(owner, 1)] = rows[1:2, :cond]
        vectors[0:8] += pltpu.roll(wide[...], owner * per, 1)
        return total_mods + pltpu.roll(mods[...], owner * columns, 1)

    flat = lax.fori_loop(0, count, add, jnp.zeros(mods.shape, f32))
    width = vectors.shape[1]
    for n in range(6):
        vectors[8 + n : 9 + n] = flat[0:1, n * width : (n + 1) * width]


def prepare(where, packs, width, per, cond):
    dp_size = packs.shape[0]
    columns = 6 * width // dp_size
    return pl.pallas_call(
        functools.partial(prepare_kernel, columns, per),
        out_shape=[
            jax.ShapeDtypeStruct((16, width), f32),
            jax.ShapeDtypeStruct((dp_size, cond), f32),
        ],
        in_specs=[SMEM, VMEM],
        out_specs=[VMEM] * 2,
        scratch_shapes=[pltpu.VMEM((8, 6 * width), f32), pltpu.VMEM((8, width), f32)],
        compiler_params=pltpu.CompilerParams(vmem_limit_bytes=16 << 20),
        name="prepare",
    )(where, packs)


GAIN_ONE, GAIN_TWO, BIAS_DOWN, SHIFT_ONE, SCALE_ONE, GATE_ONE, SHIFT_TWO, SCALE_TWO, GATE_TWO = (
    slice(n, n + 1) for n in (2, 3, 4, 8, 9, 10, 11, 12, 13)
)


def project_kernel(count, *refs):
    where, tokens, vectors, cosine, sine = refs[:5]
    pieces, (hidden, packed, full, sems) = refs[5 : 5 + count], refs[5 + count :]
    me, z = where[0], where[1]
    wide = full.shape[2] // 3
    copies = load_weights(me, pieces, full, sems)
    gain, scale, shift = vectors[GAIN_ONE], vectors[SCALE_ONE], vectors[SHIFT_ONE]
    normed, _ = normalize(tokens[...].astype(f32))
    hidden[...] = (normed * gain * (1.0 + scale) + shift).astype(bf16)
    cos, sin = cosine[...], sine[...]
    for copy in copies:
        copy.wait()
    for i in range(GROUP):
        projected = dot(hidden[...], full[z ^ i]).T
        for h in range(wide // HEAD_DIM):
            at = 3 * HEAD_DIM * h
            for c in range(2):
                first = c * wide + h * HEAD_DIM
                upper = projected[first : first + HALF]
                lower = projected[first + HALF : first + HEAD_DIM]
                packed[i, at : at + HALF] = (upper * cos - lower * sin).astype(bf16)
                packed[i, at + HALF : at + HEAD_DIM] = (lower * cos + upper * sin).astype(bf16)
                at += HEAD_DIM
            first = 2 * wide + h * HEAD_DIM
            packed[i, at : at + HEAD_DIM] = projected[first : first + HEAD_DIM].astype(bf16)


def project(where, tokens, vectors, cosine, sine, pieces):
    rows, width = tokens.shape
    columns = pieces[0].shape[2]
    shapes = [
        jax.ShapeDtypeStruct((rows, width), bf16),
        jax.ShapeDtypeStruct((GROUP, columns, rows), bf16),
    ]
    return pl.pallas_call(
        functools.partial(project_kernel, len(pieces)),
        out_shape=shapes,
        grid=(1,),
        in_specs=[SMEM]
        + [whole(x) for x in (tokens, vectors, cosine, sine)]
        + [ANY] * len(pieces),
        out_specs=[whole(x) for x in shapes],
        scratch_shapes=[
            pltpu.VMEM((GROUP, width, columns), bf16),
            pltpu.SemaphoreType.DMA((GROUP * len(pieces),)),
        ],
        compiler_params=pltpu.CompilerParams(vmem_limit_bytes=32 << 20),
        cost_estimate=pl.CostEstimate(
            flops=2 * rows * width * GROUP * columns,
            bytes_accessed=2 * GROUP * (width + rows) * columns,
            transcendentals=0,
        ),
        name="project",
    )(where, tokens, vectors, cosine, sine, *pieces)


GELU_A = math.sqrt(2.0 / math.pi)
GELU_B = 0.044715


def feed_kernel(count, *refs):
    where, tokens, upstream, vectors, mixtures = refs[:5]
    pieces, refs = refs[5 : 5 + count], refs[5 + count :]
    output, residual_grad, out_hidden, out_branch_one, out_branch_two = refs[:5]
    activated, pre_grad, attention, sums, bias_sums = refs[5:10]
    mixture_grads, full, bias_up, slope, keep_one, keep_two, sems = refs[10:]
    wide = mixtures.shape[1]
    hidden = bias_up.shape[1]
    of_up = slice(0, hidden)
    of_down = slice(hidden, 2 * hidden)
    of_out = slice(2 * hidden, 2 * hidden + wide)
    of_bias = slice(2 * hidden + wide, 2 * hidden + wide + 64)
    copies = load_weights(where[0], pieces, full, sems)
    gain, scale, shift = vectors[GAIN_TWO], vectors[SCALE_TWO], vectors[SHIFT_TWO]
    gate_one, gate_two, bias_down = vectors[GATE_ONE], vectors[GATE_TWO], vectors[BIAS_DOWN]
    for r in range(GROUP):
        attention[r] = mixtures[r].T
    for copy in copies:
        copy.wait()
    for t in range(GROUP):
        bias_up[t : t + 1] = full[t, :, of_bias].T[0:1].astype(f32)
    branch_one = dot_nt(attention[0], full[0, :, of_out])
    for r in range(1, GROUP):
        branch_one = branch_one + dot_nt(attention[r], full[r, :, of_out])
    keep_one[...] = branch_one
    residual = tokens[...].astype(f32) + gate_one * branch_one
    normed, _ = normalize(residual)
    out_hidden[...] = (normed * gain * (1.0 + scale) + shift).astype(bf16)

    keep_two[...] = jnp.broadcast_to(bias_down, keep_two.shape)

    def forward(t, carry):
        pre = dot(out_hidden[...], full[t, :, of_up]) + bias_up[pl.ds(t, 1)]
        inner = jnp.tanh(GELU_A * (pre + GELU_B * pre * pre * pre))
        activated[t] = (0.5 * pre * (1.0 + inner)).astype(bf16)
        slope[t] = 0.5 * (1.0 + inner) + (
            0.5 * GELU_A * pre * (1.0 - inner * inner) * (1.0 + 3.0 * GELU_B * pre * pre)
        )
        keep_two[...] += dot_nt(activated[t], full[t, :, of_down])
        return carry

    lax.fori_loop(0, GROUP, forward, 0)
    branch_two = keep_two[...]
    residual = tokens[...].astype(f32) + gate_one * keep_one[...]
    output[...] = (residual + gate_two * branch_two).astype(bf16)
    grad = upstream[...].astype(f32)
    branch_two_grad = gate_two * grad
    out_branch_two[...] = branch_two_grad.astype(bf16)
    sums[2:3] = total(grad * branch_two)
    sums[4:5] = total(out_branch_two[...].astype(f32))

    keep_two[...] = jnp.zeros_like(keep_two)

    def backward(t, carry):
        act_grad = dot(out_branch_two[...], full[t, :, of_down])
        pre_grad[t] = (act_grad * slope[t]).astype(bf16)
        bias_sums[pl.ds(t, 1)] = total(pre_grad[t].astype(f32))
        keep_two[...] += dot_nt(pre_grad[t], full[t, :, of_up])
        return carry

    lax.fori_loop(0, GROUP, backward, 0)
    hidden_grad = keep_two[...]
    residual = tokens[...].astype(f32) + gate_one * keep_one[...]
    normed, inverse = normalize(residual)
    sums[0:1] = total(hidden_grad)
    sums[1:2] = total(hidden_grad * normed)
    grad = upstream[...].astype(f32) + norm_back(
        hidden_grad * gain * (1.0 + scale), normed, inverse
    )
    residual_grad[...] = grad
    sums[3:4] = total(grad * keep_one[...])
    out_branch_one[...] = (gate_one * grad).astype(bf16)
    for r in range(GROUP):
        back = dot(out_branch_one[...], full[r, :, of_out])
        mixture_grads[r] = back.astype(bf16).T


def feed(where, tokens, upstream, vectors, mixtures, pieces):
    rows, width = tokens.shape
    wide = mixtures.shape[1]
    columns = pieces[0].shape[2]
    hidden = width

    def shape(dtype, *lengths):
        return jax.ShapeDtypeStruct(lengths, dtype)

    shapes = [
        shape(bf16, rows, width),
        shape(f32, rows, width),
        shape(bf16, rows, width),
        shape(bf16, rows, width),
        shape(bf16, rows, width),
        shape(bf16, GROUP, rows, hidden),
        shape(bf16, GROUP, rows, hidden),
        shape(bf16, GROUP, rows, wide),
        shape(f32, 5, width),
        shape(f32, GROUP, hidden),
        shape(bf16, GROUP, wide, rows),
    ]
    return pl.pallas_call(
        functools.partial(feed_kernel, len(pieces)),
        out_shape=shapes,
        grid=(1,),
        in_specs=[SMEM]
        + [whole(x) for x in (tokens, upstream, vectors, mixtures)]
        + [ANY] * len(pieces),
        out_specs=[whole(x) for x in shapes],
        scratch_shapes=[
            pltpu.VMEM((GROUP, width, columns), bf16),
            pltpu.VMEM((GROUP, hidden), f32),
            pltpu.VMEM((GROUP, rows, hidden), f32),
            pltpu.VMEM((rows, width), f32),
            pltpu.VMEM((rows, width), f32),
            pltpu.SemaphoreType.DMA((GROUP * len(pieces),)),
        ],
        compiler_params=pltpu.CompilerParams(vmem_limit_bytes=60 << 20),
        cost_estimate=pl.CostEstimate(
            flops=4 * rows * width * GROUP * columns,
            bytes_accessed=2 * GROUP * (width + rows) * columns,
            transcendentals=GROUP * rows * hidden,
        ),
        name="feed",
    )(where, tokens, upstream, vectors, mixtures, *pieces)


def feed_grads_kernel(hidden, branch_one, branch_two, act, pre, attention, sums, out):
    t = pl.program_id(0)
    up = dot(hidden[...].T, pre[0]).astype(bf16)
    down = dot(branch_two[...].T, act[0]).astype(bf16)
    own = dot(branch_one[...].T, attention[0]).astype(bf16)
    line = lax.broadcasted_iota(jnp.int32, (8, 1), 0)
    lines = jnp.where(line == 0, sums[pl.ds(t, 1)], 0.0)
    for n in (1, 2):
        lines = jnp.where(line == n, sums[3 + n : 4 + n], lines)
    lines = jnp.concatenate([lines, jnp.zeros((120, lines.shape[1]), f32)])
    extra = lines.T[:, :64].astype(bf16)
    at = 0
    for value in (up, down, jnp.concatenate([own, extra], axis=1)):
        columns = slice(at, at + value.shape[1])
        at += value.shape[1]
        if len(out.shape) == 3:
            out[0, :, columns] = value
        else:
            out[:, 0, :, columns] = value.reshape(out.shape[0], out.shape[2], -1)


def feed_grads(dp_size, hidden, branch_one, branch_two, act, pre, attention, sums):
    rows, width = hidden.shape
    wide, inner = attention.shape[2], act.shape[2]
    columns = wide + 2 * inner + 64
    if dp_size == 8:
        shape = (dp_size, GROUP, width // dp_size, columns)
        out_spec = pl.BlockSpec((dp_size, 1, width // dp_size, columns), lambda t: (0, t, 0, 0))
    else:
        shape = (GROUP, width, columns)
        out_spec = pl.BlockSpec((1, width, columns), lambda t: (t, 0, 0))
    return pl.pallas_call(
        feed_grads_kernel,
        out_shape=jax.ShapeDtypeStruct(shape, bf16),
        grid=(GROUP,),
        in_specs=[whole(hidden)] * 3
        + [pl.BlockSpec((1, rows, inner), lambda t: (t, 0, 0))] * 2
        + [pl.BlockSpec((1, rows, wide), lambda t: (t, 0, 0)), whole(sums)],
        out_specs=out_spec,
        compiler_params=pltpu.CompilerParams(vmem_limit_bytes=60 << 20),
        cost_estimate=pl.CostEstimate(
            flops=2 * rows * width * GROUP * columns,
            bytes_accessed=2 * GROUP * (width + rows) * columns,
            transcendentals=0,
        ),
        name="feed_grads",
    )(hidden, branch_one, branch_two, act, pre, attention, sums)


def join_heads(received, i):
    return jnp.concatenate(
        [ref[i, c * HEAD_DIM : (c + 1) * HEAD_DIM] for c in range(3) for ref in received]
    )


def project_grads_kernel(heads, where, hidden, *refs):
    received, outs = refs[:heads], refs[heads:]
    me = where[0]
    for parity in range(2):

        @pl.when(me % 2 == parity)
        def _():
            hidden_t = hidden[...].T
            for i in range(GROUP):
                value = dot_nt(hidden_t, join_heads(received, i)).astype(bf16)
                store_blocks(me, parity, outs, i, value)


def project_grads(dp_size, where, hidden, received):
    rows, width = hidden.shape
    heads = len(received)
    columns = 3 * heads * HEAD_DIM
    shapes = grad_shapes(dp_size, width, columns)
    return pl.pallas_call(
        functools.partial(project_grads_kernel, heads),
        out_shape=shapes,
        grid=(1,),
        in_specs=[SMEM] + [whole(x) for x in (hidden, *received)],
        out_specs=[whole(x) for x in shapes],
        compiler_params=pltpu.CompilerParams(vmem_limit_bytes=32 << 20),
        cost_estimate=pl.CostEstimate(
            flops=2 * rows * width * GROUP * columns,
            bytes_accessed=2 * GROUP * (width + rows) * columns,
            transcendentals=0,
        ),
        name="project_grads",
    )(where, hidden, *received)


def project_back_kernel(count, heads, *refs):
    where, tokens, vectors, residual_grad = refs[:4]
    received, refs = refs[4 : 4 + heads], refs[4 + heads :]
    pieces, (input_grad, sums, full, sems) = refs[:count], refs[count:]
    me, z = where[0], where[1]
    copies = load_weights(me, pieces, full, sems)
    gain, scale = vectors[GAIN_ONE], vectors[SCALE_ONE]
    normed, inverse = normalize(tokens[...].astype(f32))
    for copy in copies:
        copy.wait()
    hidden_grad = None
    for i in range(GROUP):
        term = dot_nt(join_heads(received, i).T, full[z ^ i])
        hidden_grad = term if hidden_grad is None else hidden_grad + term
    sums[0:1] = total(hidden_grad)
    sums[1:2] = total(hidden_grad * normed)
    input_grad[...] = (
        residual_grad[...] + norm_back(hidden_grad * gain * (1.0 + scale), normed, inverse)
    ).astype(bf16)


def project_back(where, tokens, vectors, residual_grad, received, pieces):
    rows, width = tokens.shape
    columns = pieces[0].shape[2]
    shapes = [
        jax.ShapeDtypeStruct((rows, width), bf16),
        jax.ShapeDtypeStruct((2, width), f32),
    ]
    return pl.pallas_call(
        functools.partial(project_back_kernel, len(pieces), len(received)),
        out_shape=shapes,
        grid=(1,),
        in_specs=[SMEM]
        + [whole(x) for x in (tokens, vectors, residual_grad, *received)]
        + [ANY] * len(pieces),
        out_specs=[whole(x) for x in shapes],
        scratch_shapes=[
            pltpu.VMEM((GROUP, width, columns), bf16),
            pltpu.SemaphoreType.DMA((GROUP * len(pieces),)),
        ],
        compiler_params=pltpu.CompilerParams(vmem_limit_bytes=32 << 20),
        cost_estimate=pl.CostEstimate(
            flops=2 * rows * width * GROUP * columns,
            bytes_accessed=2 * GROUP * (width + rows) * columns,
            transcendentals=0,
        ),
        name="project_back",
    )(where, tokens, vectors, residual_grad, *received, *pieces)


def einsum(spec, a, b):
    return jnp.einsum(spec, a, b, preferred_element_type=f32)


def per_device(
    dp_size,
    tokens,
    time_embed,
    ada_weight,
    ada_bias,
    norm1_gain,
    qkv_weight,
    out_weight,
    norm2_gain,
    up_weight,
    up_bias,
    down_weight,
    down_bias,
    out_grad,
):
    me = lax.axis_index(DP)
    z = lax.axis_index(TENSOR)
    position = lax.axis_index(TEAM)
    where = jnp.stack([me, z]).astype(jnp.int32)
    rows, width = tokens.shape
    heads = qkv_weight.shape[2] // HEAD_DIM
    wide = heads * HEAD_DIM
    hidden = up_weight.shape[1]
    cond = time_embed.shape[1]
    per = norm1_gain.shape[0]

    first_shard = jnp.concatenate([*qkv_weight], axis=1)
    packs = pack(ada_weight, ada_bias, time_embed, norm1_gain, norm2_gain, down_bias)
    packs, *others = meet(first_step(packs, dp_size), *send_planes(first_shard, dp_size))
    packs = spread_dp(packs, dp_size)
    first_own = jnp.stack([first_shard, *others])
    extra = jnp.pad(up_bias[:, None], ((0, 0), (0, 63)))
    second_shard = jnp.concatenate([up_weight, down_weight.T, out_weight.T, extra], axis=1)
    tokens, first_own = meet(tokens, first_own)
    sent = send_tokens(tokens, dp_size)
    first_pieces = gather_weights(first_own, gather_sides(first_own, dp_size), dp_size)
    moved = settle(tokens, sent)
    second_own = lax.all_gather(second_shard, TENSOR, axis=0, tiled=False)

    columns = ada_weight.shape[1]
    vectors, embeds = prepare(where, packs, width, per, cond)
    ada_full = packs[:, :cond, :columns]
    gain_one, gain_two = vectors[GAIN_ONE], vectors[GAIN_TWO]
    scale_one, scale_two = vectors[SCALE_ONE], vectors[SCALE_TWO]

    frequency = jnp.exp(
        jnp.arange(HALF, dtype=f32) * (-2.0 * math.log(ROPE_BASE) / HEAD_DIM)
    )
    angles = frequency[:, None] * jnp.arange(GROUP * rows, dtype=jnp.int32).astype(f32)[None, :]
    cosine, sine = jnp.cos(angles), jnp.sin(angles)
    cosine_own = lax.dynamic_slice_in_dim(cosine, position * rows, rows, axis=1)
    sine_own = lax.dynamic_slice_in_dim(sine, position * rows, rows, axis=1)

    cosine_own, second_own = meet(cosine_own, second_own)
    second_sides = gather_sides(second_own, dp_size)
    hidden_one, packed = project(where, moved, vectors, cosine_own, sine_own, first_pieces)
    packed = exchange(packed)
    out_grad, packed = meet(out_grad, packed)
    upstream = send_tokens(out_grad, dp_size)
    mixtures, lse = attend(packed)
    lse, *second_sides = meet(lse, *second_sides)
    second_pieces = gather_weights(second_own, second_sides, dp_size)
    mixtures, upstream = meet(mixtures, upstream)
    upstream = settle(out_grad, upstream)
    mixtures = exchange(mixtures)

    outs = feed(where, moved, upstream, vectors, mixtures, second_pieces)
    output, residual_grad, hidden_two, branch_one_grad, branch_two_grad = outs[:5]
    activated, pre_grad, attention, feed_sums, bias_sums, mixture_grads = outs[5:]
    incoming = exchange(mixture_grads)
    sums_two = jnp.concatenate(
        [bias_sums, feed_sums[1:2] * (1.0 + scale_two), feed_sums[4:5]]
    )
    second_grad = feed_grads(
        dp_size,
        hidden_two,
        branch_one_grad,
        branch_two_grad,
        activated,
        pre_grad,
        attention,
        jnp.pad(sums_two, ((0, 2), (0, 0))),
    )
    incoming, second_grad, output = meet(incoming, second_grad, output)
    output = regroup(output, dp_size)
    if dp_size == 8:
        second_sum = lax.psum_scatter(second_grad, DP, scatter_dimension=0, tiled=False)
    else:
        second_sum = lax.psum_scatter(second_grad, DP, scatter_dimension=1, tiled=True)

    received = []
    for h in range(heads):
        received.append(exchange(attend_back(h, packed, incoming, lse, cosine, sine)))
        if h == 0:
            incoming, output = meet(incoming, output)
    first_grad = list(project_grads(dp_size, where, hidden_one, received))
    first_far = reduce_cores(first_grad, dp_size)
    if dp_size == 8:
        first_diagonal = reduce_diagonal(first_grad, first_far, dp_size)
        *received, first_diagonal, second_sum = meet(*received, first_diagonal, second_sum)
        first_half = reduce_first(first_diagonal, dp_size)
    input_grad, project_sums = project_back(
        where, moved, vectors, residual_grad, received, first_pieces
    )
    sent = send_tokens(input_grad, dp_size)
    pull_one, pull_two = project_sums[1:2], feed_sums[1:2]
    mine = jnp.concatenate(
        [
            project_sums[:1],
            pull_one * gain_one,
            feed_sums[3:4],
            feed_sums[:1],
            pull_two * gain_two,
            feed_sums[2:3],
            pull_one * (1.0 + scale_one),
        ]
    )
    second_sum = lax.psum_scatter(second_sum, TENSOR, scatter_dimension=0, tiled=False)
    second_sum = second_sum.astype(f32)

    def widen(mods, swap, mask):
        return jnp.concatenate([mods, swap(mods, dp_size, mask)])

    mods = mine[None]
    mask = 2
    while mask < dp_size:
        mods = widen(mods, swap_dp, mask)
        mask *= 2
    mods = mods + swap_dp(mods, dp_size, 1)
    first_sides = None
    if dp_size == 8:
        first_sides = reduce_sides(first_grad, first_far, first_half, dp_size)
    first_sum = reduce_second(first_grad, first_far, first_sides, dp_size)
    mods, first_sum, second_sum = meet(mods, first_sum, second_sum)
    first_sum = [
        lax.dynamic_index_in_dim(first_sum.astype(bf16), z ^ t, 0, keepdims=False)
        for t in range(GROUP)
    ]
    first_sum = first_sum[:1] + [swap_z(first_sum[t], dp_size, t) for t in range(1, GROUP)]
    first_sum = sum(term.astype(f32) for term in first_sum)
    mods = mods + swap_z(mods, dp_size, 1)
    mods = mods.at[:, :6].set(mods[:, :6].astype(bf16).astype(f32))
    mods = widen(mods, swap_z, 2)
    tail = jnp.sum(mods[:, 6:], axis=0)
    mods = mods[:, :6]
    input_grad = settle(input_grad, sent)
    up_out = second_sum[:, :hidden]
    down_out = second_sum[:, hidden : 2 * hidden].T
    out_out = second_sum[:, 2 * hidden : 2 * hidden + wide].T
    bias_up_out, gain_two_out, bias_down_out = second_sum[:, wide + 2 * hidden :].T[:3]
    qkv_out = jnp.stack(jnp.split(first_sum, 3, axis=1))

    rel = jnp.arange(dp_size)
    quads = dp_size // 2
    seq_at = (me // 2 ^ rel % quads) * 2 + (z // 2 ^ rel // quads)
    mods = mods.reshape(dp_size, 6 * width).astype(bf16)
    own_mods = lax.dynamic_slice_in_dim(mods, me * columns, columns, axis=1)
    pick = (seq_at[:, None] == jnp.arange(dp_size)[None, :]).astype(bf16)
    ada_out = einsum("sc,se->ce", jnp.dot(pick, embeds.astype(bf16)), own_mods)
    ada_bias_out = jnp.sum(own_mods.astype(f32), axis=0)
    mine_at = (seq_at == me).astype(f32)
    own_row = jnp.sum(mods.astype(f32) * mine_at[:, None], axis=0).astype(bf16)
    own_row = reorder(own_row.reshape(dp_size, columns), me)
    time_out = jnp.sum(einsum("oe,oce->oc", own_row, ada_full), axis=0, keepdims=True)

    def own_part(row):
        return lax.dynamic_slice_in_dim(row, me * per, per)

    return (
        output,
        input_grad,
        time_out,
        ada_out,
        ada_bias_out,
        own_part(tail[0]),
        qkv_out,
        out_out,
        gain_two_out,
        up_out,
        bias_up_out,
        down_out,
        bias_down_out,
    )


def solution(mesh):
    dp_size, tensor_size = mesh.shape["dp"], mesh.shape["tensor"]
    parts = jax.sharding.Mesh(
        mesh.devices.reshape(dp_size // 2, 2, tensor_size // 2, 2), AXES
    )
    in_specs = (
        P(AXES, None),
        P(DP, None),
        P(None, DP),
        P(DP),
        P(DP),
        P(None, DP, TENSOR),
        P(TENSOR, DP),
        P(DP),
        P(DP, TENSOR),
        P(TENSOR + DP),
        P(TENSOR, DP),
        P(DP),
        P(AXES, None),
    )
    out_specs = (
        P(AXES, None),
        P(AXES, None),
        P(DP, None),
        P(None, DP),
        P(DP),
        P(DP),
        P(None, DP, TENSOR),
        P(TENSOR, DP),
        P(DP),
        P(DP, TENSOR),
        P(TENSOR + DP),
        P(TENSOR, DP),
        P(DP),
    )
    return jax.shard_map(
        functools.partial(per_device, dp_size),
        mesh=parts,
        in_specs=in_specs,
        out_specs=out_specs,
        check_vma=False,
    )
```

```python
import functools
import math

import jax
import jax.numpy as jnp
from jax import lax
from jax.experimental import pallas as pl
from jax.experimental.pallas import tpu as pltpu
from jax.sharding import PartitionSpec as P

HEAD_DIM = 64
EPSILON = 1e-05
ROPE_BASE = 10000.0
GROUP = 4
DP = ("quad", "core")
TENSOR = ("high", "low")
AXES = DP + TENSOR
TEAM = ("core", "low")
f32 = jnp.float32
bf16 = jnp.bfloat16
VMEM = pl.BlockSpec(memory_space=pltpu.VMEM)
SMEM = pl.BlockSpec(memory_space=pltpu.SMEM)
ANY = pl.BlockSpec(memory_space=pl.ANY)
HALF = HEAD_DIM // 2


def whole(array):
    return pl.BlockSpec(
        array.shape, lambda *at: (0,) * len(array.shape), pipeline_mode=pl.Buffered(1)
    )


def permute(array, dp_size, target):
    pairs = []
    for d in range(dp_size):
        for z in range(GROUP):
            to_d, to_z = target(d, z)
            if (d, z) != (to_d, to_z):
                pairs.append((d * GROUP + z, to_d * GROUP + to_z))
    return lax.ppermute(array, AXES, pairs)


def swap_dp(array, dp_size, mask):
    return permute(array, dp_size, lambda d, z: (d ^ mask, z))


def swap_z(array, dp_size, mask):
    return permute(array, dp_size, lambda d, z: (d, z ^ mask))


def send_tokens(array, dp_size):
    return permute(array, dp_size, lambda d, z: (d // 2 * 2 + z // 2, d % 2 * 2 + z % 2))


def settle(array, moved):
    stay = lax.axis_index("core") == lax.axis_index("high")
    return jnp.where(stay, array, moved)


def regroup(array, dp_size):
    return settle(array, send_tokens(array, dp_size))


def meet(*arrays):
    return lax.optimization_barrier(arrays)


def exchange(blocks):
    return lax.all_to_all(blocks, TEAM, 0, 0, tiled=True)


def reorder(array, index):
    count = array.shape[0]
    for k in range(count.bit_length() - 1):
        pairs = array.reshape(count >> (k + 1), 2, 1 << k, *array.shape[1:])
        pairs = jnp.concatenate([pairs[:, 1:], pairs[:, :1]], axis=1).reshape(array.shape)
        array = jnp.where((index >> k) % 2 == 1, pairs, array)
    return array


def first_step(array, dp_size):
    return jnp.stack([array, swap_dp(array, dp_size, 2)])


def spread_dp(blocks, dp_size):
    array = blocks[0]
    mask = 4
    while mask < dp_size:
        blocks = jnp.concatenate([blocks, swap_dp(blocks, dp_size, mask)])
        mask *= 2
    blocks = jnp.stack([blocks, swap_dp(blocks, dp_size, 1)], axis=1)
    return blocks.reshape(dp_size, *array.shape)


WHOLE = ((0, 0), (2, 0), (4, 0), (6, 0), (1, 0), (3, 0), (5, 0), (7, 0))
HALVES = WHOLE[:4] + ((6, 2),) + WHOLE[4:] + ((7, 2),)


def send_planes(shard, dp_size):
    return [swap_z(shard, dp_size, t) for t in range(1, GROUP)]


def gather_sides(own, dp_size):
    if dp_size != 8:
        return ()
    return swap_dp(own, dp_size, 2), swap_dp(own, dp_size, 4)


def gather_weights(own, sides, dp_size):
    if dp_size != 8:
        return (lax.all_gather(own, DP, axis=1, tiled=True),)
    x, y = sides
    near = (own, x, y, swap_dp(x[:2], dp_size, 4), swap_dp(y[2:], dp_size, 2))
    return near + tuple(swap_dp(piece, dp_size, 1) for piece in near)


def load_weights(me, pieces, full, sems, flip=None):
    if len(pieces) == 1:
        flips = [t if flip is None else t ^ flip for t in range(GROUP)]
        copies = [
            pltpu.make_async_copy(pieces[0].at[t], full.at[flips[t]], sems.at[t])
            for t in range(GROUP)
        ]
    else:
        copies = []
        for i, (piece, (rel, first)) in enumerate(
            zip(pieces, HALVES if len(pieces) == len(HALVES) else WHOLE)
        ):
            count, rows = piece.shape[:2]
            start = pl.multiple_of((me ^ rel) * rows, rows)
            if flip is None:
                place = full.at[first : first + count, pl.ds(start, rows)]
                copies.append(pltpu.make_async_copy(piece, place, sems.at[i]))
                continue
            for t in range(count):
                place = full.at[(first + t) ^ flip, pl.ds(start, rows)]
                sem = sems.at[GROUP * i + t]
                copies.append(pltpu.make_async_copy(piece.at[t], place, sem))
    for copy in copies:
        copy.start()
    return copies


def store_blocks(me, parity, outs, slot, value):
    if len(outs) == 1:
        outs[0][slot] = value
        return
    rows = outs[0].shape[2]
    for owner in range(2 * outs[0].shape[0]):
        out = outs[(owner + parity) % 2]
        out[(me ^ owner) >> 1, slot] = value[owner * rows : (owner + 1) * rows]


def grad_shapes(dp_size, width, columns):
    if dp_size != 8:
        return [jax.ShapeDtypeStruct((GROUP, width, columns), bf16)]
    return [jax.ShapeDtypeStruct((dp_size // 2, GROUP, width // dp_size, columns), bf16)] * 2


def plus(a, b):
    return (a.astype(f32) + b.astype(f32)).astype(bf16)


def reduce_cores(parts, dp_size):
    return swap_dp(parts[1], dp_size, 1) if dp_size == 8 else None


def reduce_diagonal(parts, far, dp_size):
    return plus(parts[0][3], far[3]) if dp_size == 8 else None


def reduce_first(diagonal, dp_size):
    if dp_size != 8:
        return None
    return swap_dp(diagonal[:2], dp_size, 2), swap_dp(diagonal[2:], dp_size, 4)


def reduce_sides(parts, far, half, dp_size):
    if dp_size != 8:
        return None
    x = parts[0][1].astype(f32) + far[1].astype(f32)
    y = parts[0][2].astype(f32) + far[2].astype(f32)
    x = jnp.concatenate([x[:2], x[2:] + half[1].astype(f32)]).astype(bf16)
    y = jnp.concatenate([y[:2] + half[0].astype(f32), y[2:]]).astype(bf16)
    return x, y


def reduce_second(parts, far, sides, dp_size):
    if dp_size != 8:
        return lax.psum_scatter(parts[0], DP, scatter_dimension=1, tiled=True).astype(f32)
    from_x = swap_dp(sides[0], dp_size, 2)
    from_y = swap_dp(sides[1], dp_size, 4)
    own = parts[0][0].astype(f32) + far[0].astype(f32)
    return own + from_x.astype(f32) + from_y.astype(f32)


def reduce_planes(own):
    terms = lax.all_to_all(own.astype(bf16), TENSOR, 0, 0, tiled=True)
    return jnp.sum(terms.astype(f32), axis=0)


def attend_kernel(packed, out, lse, key_t, value_t, key):
    count, _, block = packed.shape
    for i in range(count):
        columns = slice(i * block, (i + 1) * block)
        key_t[:, columns] = packed[i, HEAD_DIM : 2 * HEAD_DIM]
        value_t[:, columns] = packed[i, 2 * HEAD_DIM :]
    key[...] = key_t[...].T
    for i in range(count):
        query = packed[i, :HEAD_DIM] * bf16(HEAD_DIM**-0.5)
        scores = jnp.dot(key[...], query, preferred_element_type=f32)
        highest = jnp.max(scores, axis=0, keepdims=True)
        exponent = jnp.exp(scores - highest)
        totals = jnp.sum(exponent, axis=0, keepdims=True)
        mixture = jnp.dot(value_t[...], exponent.astype(bf16), preferred_element_type=f32)
        out[i] = (mixture / totals).astype(bf16)
        lse[0, i : i + 1, :] = highest + jnp.log(totals)


def attend(packed):
    count, lines, block = packed.shape
    heads = lines // (3 * HEAD_DIM)
    length = count * block
    return pl.pallas_call(
        attend_kernel,
        out_shape=[
            jax.ShapeDtypeStruct((count, heads * HEAD_DIM, block), bf16),
            jax.ShapeDtypeStruct((heads, count, block), f32),
        ],
        grid=(heads,),
        in_specs=[pl.BlockSpec((count, 3 * HEAD_DIM, block), lambda h: (0, h, 0))],
        out_specs=[
            pl.BlockSpec((count, HEAD_DIM, block), lambda h: (0, h, 0)),
            pl.BlockSpec((1, count, block), lambda h: (h, 0, 0)),
        ],
        scratch_shapes=[
            pltpu.VMEM((HEAD_DIM, length), bf16),
            pltpu.VMEM((HEAD_DIM, length), bf16),
            pltpu.VMEM((length, HEAD_DIM), bf16),
        ],
        compiler_params=pltpu.CompilerParams(vmem_limit_bytes=32 << 20),
        cost_estimate=pl.CostEstimate(
            flops=16 * heads * length * length * HEAD_DIM,
            bytes_accessed=8 * heads * length * HEAD_DIM,
            transcendentals=heads * length * length,
        ),
        name="attend",
    )(packed)


def attend_back_kernel(packed, grads, lse, cosine, sine, out, *scratch):
    key_t, key, value_t, query_grad, key_grad, value_grad = scratch
    count, _, block = packed.shape
    rows = min(256, block)
    half = HEAD_DIM // 2
    for i in range(count):
        columns = slice(i * block, (i + 1) * block)
        key_t[:, columns] = packed[i, HEAD_DIM : 2 * HEAD_DIM]
        value_t[:, columns] = packed[i, 2 * HEAD_DIM :]
        key[columns, :] = packed[i, HEAD_DIM : 2 * HEAD_DIM].T
    for i in range(count):
        log_total = lse[0, i : i + 1, :].T
        for c in range(block // rows):
            own = slice(c * rows, (c + 1) * rows)
            query_t = packed[i, :HEAD_DIM, own] * bf16(HEAD_DIM**-0.5)
            grad_t = grads[i, :, own]
            scores = jnp.dot(query_t.T, key_t[...], preferred_element_type=f32)
            weights = jnp.exp(scores - log_total[own])
            pull = jnp.dot(grad_t.T, value_t[...], preferred_element_type=f32)
            centre = jnp.sum(weights * pull, axis=1, keepdims=True)
            score_grad = (weights * (pull - centre)).astype(bf16)
            value_term = jnp.dot(grad_t, weights.astype(bf16), preferred_element_type=f32)
            key_term = jnp.dot(query_t, score_grad, preferred_element_type=f32)
            if i == 0 and c == 0:
                value_grad[...] = value_term
                key_grad[...] = key_term
            else:
                value_grad[...] += value_term
                key_grad[...] += key_term
            query_grad[:, i * block + c * rows : i * block + (c + 1) * rows] = (
                jnp.dot(score_grad, key[...], preferred_element_type=f32) * HEAD_DIM**-0.5
            ).T
    for i in range(count):
        columns = slice(i * block, (i + 1) * block)
        cos, sin = cosine[:, columns], sine[:, columns]
        for first, source in ((0, query_grad), (HEAD_DIM, key_grad)):
            upper, lower = source[:half, columns], source[half:, columns]
            out[i, first : first + half] = (upper * cos + lower * sin).astype(bf16)
            out[i, first + half : first + HEAD_DIM] = (lower * cos - upper * sin).astype(bf16)
        out[i, 2 * HEAD_DIM :] = value_grad[:, columns].astype(bf16)


def attend_back(head, packed, grads, lse, cosine, sine):
    count, _, block = packed.shape
    length = count * block
    lines = 3 * HEAD_DIM
    return pl.pallas_call(
        attend_back_kernel,
        out_shape=jax.ShapeDtypeStruct((count, lines, block), bf16),
        grid=(1,),
        in_specs=[
            pl.BlockSpec((count, lines, block), lambda i: (0, head, 0)),
            pl.BlockSpec((count, HEAD_DIM, block), lambda i: (0, head, 0)),
            pl.BlockSpec((1, count, block), lambda i: (head, 0, 0)),
            whole(cosine),
            whole(sine),
        ],
        out_specs=pl.BlockSpec((count, lines, block), lambda i: (0, 0, 0)),
        scratch_shapes=[
            pltpu.VMEM((HEAD_DIM, length), bf16),
            pltpu.VMEM((length, HEAD_DIM), bf16),
            pltpu.VMEM((HEAD_DIM, length), bf16),
            pltpu.VMEM((HEAD_DIM, length), f32),
            pltpu.VMEM((HEAD_DIM, length), f32),
            pltpu.VMEM((HEAD_DIM, length), f32),
        ],
        compiler_params=pltpu.CompilerParams(vmem_limit_bytes=60 << 20),
        cost_estimate=pl.CostEstimate(
            flops=40 * length * length * HEAD_DIM,
            bytes_accessed=16 * length * HEAD_DIM,
            transcendentals=length * length,
        ),
        name="attend_back",
    )(packed, grads, lse, cosine, sine)


def normalize(rows):
    center = jnp.mean(rows, axis=1, keepdims=True)
    shifted = rows - center
    inverse = lax.rsqrt(jnp.mean(shifted * shifted, axis=1, keepdims=True) + EPSILON)
    return shifted * inverse, inverse


def norm_back(scaled, normed, inverse):
    return inverse * (
        scaled
        - jnp.mean(scaled, axis=1, keepdims=True)
        - normed * jnp.mean(scaled * normed, axis=1, keepdims=True)
    )


def dot(a, b):
    return jnp.dot(a, b, preferred_element_type=f32)


def dot_nt(a, b):
    return lax.dot_general(a, b, (((1,), (1,)), ((), ())), preferred_element_type=f32)


def total(values):
    return jnp.sum(values, axis=0, keepdims=True)


def pack_kernel(ada, ada_bias, embed, gain_one, gain_two, bias_down, out, rows):
    lines = ada.shape[0]
    rows[...] = jnp.zeros_like(rows)
    for n, ref in enumerate((ada_bias, embed, gain_one, gain_two, bias_down)):
        rows[n : n + 1, : ref.shape[1]] = ref[...].astype(f32)
    out[:lines, : ada.shape[1]] = ada[...]
    out[lines:] = rows[...].astype(bf16)


def pack(ada, ada_bias, embed, gain_one, gain_two, bias_down):
    lines, columns = ada.shape
    columns = max(columns, embed.shape[1])
    rows = [x.reshape(1, -1) for x in (ada_bias, embed, gain_one, gain_two, bias_down)]
    return pl.pallas_call(
        pack_kernel,
        out_shape=jax.ShapeDtypeStruct((lines + 16, columns), bf16),
        in_specs=[VMEM] * 6,
        out_specs=VMEM,
        scratch_shapes=[pltpu.VMEM((16, columns), f32)],
        name="pack",
    )(ada, *rows)


def prepare_kernel(columns, per, where, packs, vectors, embeds, mods, wide):
    me, z = where[0], where[1]
    count = packs.shape[0]
    cond = embeds.shape[1]
    rel = jnp.where(me % 2 == z // 2, 0, 1)
    embed = jnp.broadcast_to(packs[rel, cond : cond + 16][1:2, :cond], (8, cond))
    mods[...] = jnp.zeros_like(mods)
    wide[...] = jnp.zeros_like(wide)
    vectors[...] = jnp.zeros_like(vectors)

    def add(r, total_mods):
        owner = me ^ r
        rows = packs[r, cond : cond + 16].astype(f32)
        part = dot(embed, packs[r, :cond, :columns]) + rows[0:1, :columns]
        mods[:, :columns] = part
        wide[:, :per] = rows[0:8, :per]
        embeds[pl.ds(owner, 1)] = rows[1:2, :cond]
        vectors[0:8] += pltpu.roll(wide[...], owner * per, 1)
        return total_mods + pltpu.roll(mods[...], owner * columns, 1)

    flat = lax.fori_loop(0, count, add, jnp.zeros(mods.shape, f32))
    width = vectors.shape[1]
    for n in range(6):
        vectors[8 + n : 9 + n] = flat[0:1, n * width : (n + 1) * width]


def prepare(where, packs, width, per, cond):
    dp_size = packs.shape[0]
    columns = 6 * width // dp_size
    return pl.pallas_call(
        functools.partial(prepare_kernel, columns, per),
        out_shape=[
            jax.ShapeDtypeStruct((16, width), f32),
            jax.ShapeDtypeStruct((dp_size, cond), f32),
        ],
        in_specs=[SMEM, VMEM],
        out_specs=[VMEM] * 2,
        scratch_shapes=[pltpu.VMEM((8, 6 * width), f32), pltpu.VMEM((8, width), f32)],
        compiler_params=pltpu.CompilerParams(vmem_limit_bytes=16 << 20),
        name="prepare",
    )(where, packs)


GAIN_ONE, GAIN_TWO, BIAS_DOWN, SHIFT_ONE, SCALE_ONE, GATE_ONE, SHIFT_TWO, SCALE_TWO, GATE_TWO = (
    slice(n, n + 1) for n in (2, 3, 4, 8, 9, 10, 11, 12, 13)
)


def project_kernel(count, *refs):
    where, tokens, vectors, cosine, sine = refs[:5]
    pieces, (hidden, packed, full, sems) = refs[5 : 5 + count], refs[5 + count :]
    me, z = where[0], where[1]
    wide = full.shape[2] // 3
    copies = load_weights(me, pieces, full, sems)
    gain, scale, shift = vectors[GAIN_ONE], vectors[SCALE_ONE], vectors[SHIFT_ONE]
    normed, _ = normalize(tokens[...].astype(f32))
    hidden[...] = (normed * gain * (1.0 + scale) + shift).astype(bf16)
    cos, sin = cosine[...], sine[...]
    for copy in copies:
        copy.wait()
    for i in range(GROUP):
        projected = dot(hidden[...], full[z ^ i]).T
        for h in range(wide // HEAD_DIM):
            at = 3 * HEAD_DIM * h
            for c in range(2):
                first = c * wide + h * HEAD_DIM
                upper = projected[first : first + HALF]
                lower = projected[first + HALF : first + HEAD_DIM]
                packed[i, at : at + HALF] = (upper * cos - lower * sin).astype(bf16)
                packed[i, at + HALF : at + HEAD_DIM] = (lower * cos + upper * sin).astype(bf16)
                at += HEAD_DIM
            first = 2 * wide + h * HEAD_DIM
            packed[i, at : at + HEAD_DIM] = projected[first : first + HEAD_DIM].astype(bf16)


def project(where, tokens, vectors, cosine, sine, pieces):
    rows, width = tokens.shape
    columns = pieces[0].shape[2]
    shapes = [
        jax.ShapeDtypeStruct((rows, width), bf16),
        jax.ShapeDtypeStruct((GROUP, columns, rows), bf16),
    ]
    return pl.pallas_call(
        functools.partial(project_kernel, len(pieces)),
        out_shape=shapes,
        grid=(1,),
        in_specs=[SMEM]
        + [whole(x) for x in (tokens, vectors, cosine, sine)]
        + [ANY] * len(pieces),
        out_specs=[whole(x) for x in shapes],
        scratch_shapes=[
            pltpu.VMEM((GROUP, width, columns), bf16),
            pltpu.SemaphoreType.DMA((GROUP * len(pieces),)),
        ],
        compiler_params=pltpu.CompilerParams(vmem_limit_bytes=32 << 20),
        cost_estimate=pl.CostEstimate(
            flops=2 * rows * width * GROUP * columns,
            bytes_accessed=2 * GROUP * (width + rows) * columns,
            transcendentals=0,
        ),
        name="project",
    )(where, tokens, vectors, cosine, sine, *pieces)


GELU_A = math.sqrt(2.0 / math.pi)
GELU_B = 0.044715


def feed_kernel(count, *refs):
    where, tokens, upstream, vectors, mixtures = refs[:5]
    pieces, refs = refs[5 : 5 + count], refs[5 + count :]
    output, residual_grad, out_hidden, out_branch_one, out_branch_two = refs[:5]
    activated, pre_grad, attention, sums, bias_sums = refs[5:10]
    mixture_grads, full, bias_up, slope, keep_one, keep_two, sems = refs[10:]
    wide = mixtures.shape[1]
    hidden = bias_up.shape[1]
    of_up = slice(0, hidden)
    of_down = slice(hidden, 2 * hidden)
    of_out = slice(2 * hidden, 2 * hidden + wide)
    of_bias = slice(2 * hidden + wide, 2 * hidden + wide + 64)
    copies = load_weights(where[0], pieces, full, sems)
    gain, scale, shift = vectors[GAIN_TWO], vectors[SCALE_TWO], vectors[SHIFT_TWO]
    gate_one, gate_two, bias_down = vectors[GATE_ONE], vectors[GATE_TWO], vectors[BIAS_DOWN]
    for r in range(GROUP):
        attention[r] = mixtures[r].T
    for copy in copies:
        copy.wait()
    for t in range(GROUP):
        bias_up[t : t + 1] = full[t, :, of_bias].T[0:1].astype(f32)
    branch_one = dot_nt(attention[0], full[0, :, of_out])
    for r in range(1, GROUP):
        branch_one = branch_one + dot_nt(attention[r], full[r, :, of_out])
    keep_one[...] = branch_one
    residual = tokens[...].astype(f32) + gate_one * branch_one
    normed, _ = normalize(residual)
    out_hidden[...] = (normed * gain * (1.0 + scale) + shift).astype(bf16)

    keep_two[...] = jnp.broadcast_to(bias_down, keep_two.shape)

    def forward(t, carry):
        pre = dot(out_hidden[...], full[t, :, of_up]) + bias_up[pl.ds(t, 1)]
        inner = jnp.tanh(GELU_A * (pre + GELU_B * pre * pre * pre))
        activated[t] = (0.5 * pre * (1.0 + inner)).astype(bf16)
        slope[t] = 0.5 * (1.0 + inner) + (
            0.5 * GELU_A * pre * (1.0 - inner * inner) * (1.0 + 3.0 * GELU_B * pre * pre)
        )
        keep_two[...] += dot_nt(activated[t], full[t, :, of_down])
        return carry

    lax.fori_loop(0, GROUP, forward, 0)
    branch_two = keep_two[...]
    residual = tokens[...].astype(f32) + gate_one * keep_one[...]
    output[...] = (residual + gate_two * branch_two).astype(bf16)
    grad = upstream[...].astype(f32)
    branch_two_grad = gate_two * grad
    out_branch_two[...] = branch_two_grad.astype(bf16)
    sums[2:3] = total(grad * branch_two)
    sums[4:5] = total(out_branch_two[...].astype(f32))

    keep_two[...] = jnp.zeros_like(keep_two)

    def backward(t, carry):
        act_grad = dot(out_branch_two[...], full[t, :, of_down])
        pre_grad[t] = (act_grad * slope[t]).astype(bf16)
        bias_sums[pl.ds(t, 1)] = total(pre_grad[t].astype(f32))
        keep_two[...] += dot_nt(pre_grad[t], full[t, :, of_up])
        return carry

    lax.fori_loop(0, GROUP, backward, 0)
    hidden_grad = keep_two[...]
    residual = tokens[...].astype(f32) + gate_one * keep_one[...]
    normed, inverse = normalize(residual)
    sums[0:1] = total(hidden_grad)
    sums[1:2] = total(hidden_grad * normed)
    grad = upstream[...].astype(f32) + norm_back(
        hidden_grad * gain * (1.0 + scale), normed, inverse
    )
    residual_grad[...] = grad
    sums[3:4] = total(grad * keep_one[...])
    out_branch_one[...] = (gate_one * grad).astype(bf16)
    for r in range(GROUP):
        back = dot(out_branch_one[...], full[r, :, of_out])
        mixture_grads[r] = back.astype(bf16).T


def feed(where, tokens, upstream, vectors, mixtures, pieces):
    rows, width = tokens.shape
    wide = mixtures.shape[1]
    columns = pieces[0].shape[2]
    hidden = width

    def shape(dtype, *lengths):
        return jax.ShapeDtypeStruct(lengths, dtype)

    shapes = [
        shape(bf16, rows, width),
        shape(f32, rows, width),
        shape(bf16, rows, width),
        shape(bf16, rows, width),
        shape(bf16, rows, width),
        shape(bf16, GROUP, rows, hidden),
        shape(bf16, GROUP, rows, hidden),
        shape(bf16, GROUP, rows, wide),
        shape(f32, 5, width),
        shape(f32, GROUP, hidden),
        shape(bf16, GROUP, wide, rows),
    ]
    return pl.pallas_call(
        functools.partial(feed_kernel, len(pieces)),
        out_shape=shapes,
        grid=(1,),
        in_specs=[SMEM]
        + [whole(x) for x in (tokens, upstream, vectors, mixtures)]
        + [ANY] * len(pieces),
        out_specs=[whole(x) for x in shapes],
        scratch_shapes=[
            pltpu.VMEM((GROUP, width, columns), bf16),
            pltpu.VMEM((GROUP, hidden), f32),
            pltpu.VMEM((GROUP, rows, hidden), f32),
            pltpu.VMEM((rows, width), f32),
            pltpu.VMEM((rows, width), f32),
            pltpu.SemaphoreType.DMA((GROUP * len(pieces),)),
        ],
        compiler_params=pltpu.CompilerParams(vmem_limit_bytes=60 << 20),
        cost_estimate=pl.CostEstimate(
            flops=4 * rows * width * GROUP * columns,
            bytes_accessed=2 * GROUP * (width + rows) * columns,
            transcendentals=GROUP * rows * hidden,
        ),
        name="feed",
    )(where, tokens, upstream, vectors, mixtures, *pieces)


def feed_grads_kernel(hidden, branch_one, branch_two, act, pre, attention, sums, out):
    t = pl.program_id(0)
    up = dot(hidden[...].T, pre[0]).astype(bf16)
    down = dot(branch_two[...].T, act[0]).astype(bf16)
    own = dot(branch_one[...].T, attention[0]).astype(bf16)
    line = lax.broadcasted_iota(jnp.int32, (8, 1), 0)
    lines = jnp.where(line == 0, sums[pl.ds(t, 1)], 0.0)
    for n in (1, 2):
        lines = jnp.where(line == n, sums[3 + n : 4 + n], lines)
    lines = jnp.concatenate([lines, jnp.zeros((120, lines.shape[1]), f32)])
    extra = lines.T[:, :64].astype(bf16)
    at = 0
    for value in (up, down, jnp.concatenate([own, extra], axis=1)):
        columns = slice(at, at + value.shape[1])
        at += value.shape[1]
        if len(out.shape) == 3:
            out[0, :, columns] = value
        else:
            out[:, 0, :, columns] = value.reshape(out.shape[0], out.shape[2], -1)


def feed_grads(dp_size, hidden, branch_one, branch_two, act, pre, attention, sums):
    rows, width = hidden.shape
    wide, inner = attention.shape[2], act.shape[2]
    columns = wide + 2 * inner + 64
    if dp_size == 8:
        shape = (dp_size, GROUP, width // dp_size, columns)
        out_spec = pl.BlockSpec((dp_size, 1, width // dp_size, columns), lambda t: (0, t, 0, 0))
    else:
        shape = (GROUP, width, columns)
        out_spec = pl.BlockSpec((1, width, columns), lambda t: (t, 0, 0))
    return pl.pallas_call(
        feed_grads_kernel,
        out_shape=jax.ShapeDtypeStruct(shape, bf16),
        grid=(GROUP,),
        in_specs=[whole(hidden)] * 3
        + [pl.BlockSpec((1, rows, inner), lambda t: (t, 0, 0))] * 2
        + [pl.BlockSpec((1, rows, wide), lambda t: (t, 0, 0)), whole(sums)],
        out_specs=out_spec,
        compiler_params=pltpu.CompilerParams(vmem_limit_bytes=60 << 20),
        cost_estimate=pl.CostEstimate(
            flops=2 * rows * width * GROUP * columns,
            bytes_accessed=2 * GROUP * (width + rows) * columns,
            transcendentals=0,
        ),
        name="feed_grads",
    )(hidden, branch_one, branch_two, act, pre, attention, sums)


def join_heads(received, i):
    return jnp.concatenate(
        [ref[i, c * HEAD_DIM : (c + 1) * HEAD_DIM] for c in range(3) for ref in received]
    )


def project_grads_kernel(heads, where, hidden, *refs):
    received, outs = refs[:heads], refs[heads:]
    me = where[0]
    for parity in range(2):

        @pl.when(me % 2 == parity)
        def _():
            hidden_t = hidden[...].T
            for i in range(GROUP):
                value = dot_nt(hidden_t, join_heads(received, i)).astype(bf16)
                store_blocks(me, parity, outs, i, value)


def project_grads(dp_size, where, hidden, received):
    rows, width = hidden.shape
    heads = len(received)
    columns = 3 * heads * HEAD_DIM
    shapes = grad_shapes(dp_size, width, columns)
    return pl.pallas_call(
        functools.partial(project_grads_kernel, heads),
        out_shape=shapes,
        grid=(1,),
        in_specs=[SMEM] + [whole(x) for x in (hidden, *received)],
        out_specs=[whole(x) for x in shapes],
        compiler_params=pltpu.CompilerParams(vmem_limit_bytes=32 << 20),
        cost_estimate=pl.CostEstimate(
            flops=2 * rows * width * GROUP * columns,
            bytes_accessed=2 * GROUP * (width + rows) * columns,
            transcendentals=0,
        ),
        name="project_grads",
    )(where, hidden, *received)


def project_back_kernel(count, heads, *refs):
    where, tokens, vectors, residual_grad = refs[:4]
    received, refs = refs[4 : 4 + heads], refs[4 + heads :]
    pieces, (input_grad, sums, full, sems) = refs[:count], refs[count:]
    me, z = where[0], where[1]
    copies = load_weights(me, pieces, full, sems)
    gain, scale = vectors[GAIN_ONE], vectors[SCALE_ONE]
    normed, inverse = normalize(tokens[...].astype(f32))
    for copy in copies:
        copy.wait()
    hidden_grad = None
    for i in range(GROUP):
        term = dot_nt(join_heads(received, i).T, full[z ^ i])
        hidden_grad = term if hidden_grad is None else hidden_grad + term
    sums[0:1] = total(hidden_grad)
    sums[1:2] = total(hidden_grad * normed)
    input_grad[...] = (
        residual_grad[...] + norm_back(hidden_grad * gain * (1.0 + scale), normed, inverse)
    ).astype(bf16)


def project_back(where, tokens, vectors, residual_grad, received, pieces):
    rows, width = tokens.shape
    columns = pieces[0].shape[2]
    shapes = [
        jax.ShapeDtypeStruct((rows, width), bf16),
        jax.ShapeDtypeStruct((2, width), f32),
    ]
    return pl.pallas_call(
        functools.partial(project_back_kernel, len(pieces), len(received)),
        out_shape=shapes,
        grid=(1,),
        in_specs=[SMEM]
        + [whole(x) for x in (tokens, vectors, residual_grad, *received)]
        + [ANY] * len(pieces),
        out_specs=[whole(x) for x in shapes],
        scratch_shapes=[
            pltpu.VMEM((GROUP, width, columns), bf16),
            pltpu.SemaphoreType.DMA((GROUP * len(pieces),)),
        ],
        compiler_params=pltpu.CompilerParams(vmem_limit_bytes=32 << 20),
        cost_estimate=pl.CostEstimate(
            flops=2 * rows * width * GROUP * columns,
            bytes_accessed=2 * GROUP * (width + rows) * columns,
            transcendentals=0,
        ),
        name="project_back",
    )(where, tokens, vectors, residual_grad, *received, *pieces)


def einsum(spec, a, b):
    return jnp.einsum(spec, a, b, preferred_element_type=f32)


def per_device(
    dp_size,
    tokens,
    time_embed,
    ada_weight,
    ada_bias,
    norm1_gain,
    qkv_weight,
    out_weight,
    norm2_gain,
    up_weight,
    up_bias,
    down_weight,
    down_bias,
    out_grad,
):
    me = lax.axis_index(DP)
    z = lax.axis_index(TENSOR)
    position = lax.axis_index(TEAM)
    where = jnp.stack([me, z]).astype(jnp.int32)
    rows, width = tokens.shape
    heads = qkv_weight.shape[2] // HEAD_DIM
    wide = heads * HEAD_DIM
    hidden = up_weight.shape[1]
    cond = time_embed.shape[1]
    per = norm1_gain.shape[0]

    first_shard = jnp.concatenate([*qkv_weight], axis=1)
    packs = pack(ada_weight, ada_bias, time_embed, norm1_gain, norm2_gain, down_bias)
    packs, *others = meet(first_step(packs, dp_size), *send_planes(first_shard, dp_size))
    packs = spread_dp(packs, dp_size)
    first_own = jnp.stack([first_shard, *others])
    extra = jnp.pad(up_bias[:, None], ((0, 0), (0, 63)))
    second_shard = jnp.concatenate([up_weight, down_weight.T, out_weight.T, extra], axis=1)
    sent = send_tokens(tokens, dp_size)
    first_pieces = gather_weights(first_own, gather_sides(first_own, dp_size), dp_size)
    moved = settle(tokens, sent)
    second_own = lax.all_gather(second_shard, TENSOR, axis=0, tiled=False)

    columns = ada_weight.shape[1]
    vectors, embeds = prepare(where, packs, width, per, cond)
    ada_full = packs[:, :cond, :columns]
    gain_one, gain_two = vectors[GAIN_ONE], vectors[GAIN_TWO]
    scale_one, scale_two = vectors[SCALE_ONE], vectors[SCALE_TWO]

    frequency = jnp.exp(
        jnp.arange(HALF, dtype=f32) * (-2.0 * math.log(ROPE_BASE) / HEAD_DIM)
    )
    angles = frequency[:, None] * jnp.arange(GROUP * rows, dtype=jnp.int32).astype(f32)[None, :]
    cosine, sine = jnp.cos(angles), jnp.sin(angles)
    cosine_own = lax.dynamic_slice_in_dim(cosine, position * rows, rows, axis=1)
    sine_own = lax.dynamic_slice_in_dim(sine, position * rows, rows, axis=1)

    cosine_own, second_own = meet(cosine_own, second_own)
    second_sides = gather_sides(second_own, dp_size)
    hidden_one, packed = project(where, moved, vectors, cosine_own, sine_own, first_pieces)
    packed = exchange(packed)
    out_grad, packed = meet(out_grad, packed)
    upstream = send_tokens(out_grad, dp_size)
    mixtures, lse = attend(packed)
    lse, *second_sides = meet(lse, *second_sides)
    second_pieces = gather_weights(second_own, second_sides, dp_size)
    mixtures, upstream = meet(mixtures, upstream)
    upstream = settle(out_grad, upstream)
    mixtures = exchange(mixtures)

    outs = feed(where, moved, upstream, vectors, mixtures, second_pieces)
    output, residual_grad, hidden_two, branch_one_grad, branch_two_grad = outs[:5]
    activated, pre_grad, attention, feed_sums, bias_sums, mixture_grads = outs[5:]
    incoming = exchange(mixture_grads)
    sums_two = jnp.concatenate(
        [bias_sums, feed_sums[1:2] * (1.0 + scale_two), feed_sums[4:5]]
    )
    second_grad = feed_grads(
        dp_size,
        hidden_two,
        branch_one_grad,
        branch_two_grad,
        activated,
        pre_grad,
        attention,
        jnp.pad(sums_two, ((0, 2), (0, 0))),
    )
    incoming, second_grad, output = meet(incoming, second_grad, output)
    output = regroup(output, dp_size)
    if dp_size == 8:
        second_sum = lax.psum_scatter(second_grad, DP, scatter_dimension=0, tiled=False)
    else:
        second_sum = lax.psum_scatter(second_grad, DP, scatter_dimension=1, tiled=True)

    received = []
    for h in range(heads):
        received.append(exchange(attend_back(h, packed, incoming, lse, cosine, sine)))
        if h == 0:
            incoming, output = meet(incoming, output)
    first_grad = list(project_grads(dp_size, where, hidden_one, received))
    first_far = reduce_cores(first_grad, dp_size)
    if dp_size == 8:
        first_diagonal = reduce_diagonal(first_grad, first_far, dp_size)
        *received, first_diagonal, second_sum = meet(*received, first_diagonal, second_sum)
        first_half = reduce_first(first_diagonal, dp_size)
    input_grad, project_sums = project_back(
        where, moved, vectors, residual_grad, received, first_pieces
    )
    sent = send_tokens(input_grad, dp_size)
    pull_one, pull_two = project_sums[1:2], feed_sums[1:2]
    mine = jnp.concatenate(
        [
            project_sums[:1],
            pull_one * gain_one,
            feed_sums[3:4],
            feed_sums[:1],
            pull_two * gain_two,
            feed_sums[2:3],
            pull_one * (1.0 + scale_one),
        ]
    )
    second_sum = lax.psum_scatter(second_sum, TENSOR, scatter_dimension=0, tiled=False)
    second_sum = second_sum.astype(f32)

    def widen(mods, swap, mask):
        return jnp.concatenate([mods, swap(mods, dp_size, mask)])

    mods = mine[None]
    mask = 2
    while mask < dp_size:
        mods = widen(mods, swap_dp, mask)
        mask *= 2
    mods = mods + swap_dp(mods, dp_size, 1)
    first_sides = None
    if dp_size == 8:
        first_sides = reduce_sides(first_grad, first_far, first_half, dp_size)
    first_sum = reduce_second(first_grad, first_far, first_sides, dp_size)
    mods, first_sum, second_sum = meet(mods, first_sum, second_sum)
    first_sum = [
        lax.dynamic_index_in_dim(first_sum.astype(bf16), z ^ t, 0, keepdims=False)
        for t in range(GROUP)
    ]
    first_sum = first_sum[:1] + [swap_z(first_sum[t], dp_size, t) for t in range(1, GROUP)]
    first_sum = sum(term.astype(f32) for term in first_sum)
    mods = mods + swap_z(mods, dp_size, 1)
    mods = mods.at[:, :6].set(mods[:, :6].astype(bf16).astype(f32))
    mods = widen(mods, swap_z, 2)
    tail = jnp.sum(mods[:, 6:], axis=0)
    mods = mods[:, :6]
    input_grad = settle(input_grad, sent)
    up_out = second_sum[:, :hidden]
    down_out = second_sum[:, hidden : 2 * hidden].T
    out_out = second_sum[:, 2 * hidden : 2 * hidden + wide].T
    bias_up_out, gain_two_out, bias_down_out = second_sum[:, wide + 2 * hidden :].T[:3]
    qkv_out = jnp.stack(jnp.split(first_sum, 3, axis=1))

    rel = jnp.arange(dp_size)
    quads = dp_size // 2
    seq_at = (me // 2 ^ rel % quads) * 2 + (z // 2 ^ rel // quads)
    mods = mods.reshape(dp_size, 6 * width).astype(bf16)
    own_mods = lax.dynamic_slice_in_dim(mods, me * columns, columns, axis=1)
    pick = (seq_at[:, None] == jnp.arange(dp_size)[None, :]).astype(bf16)
    ada_out = einsum("sc,se->ce", jnp.dot(pick, embeds.astype(bf16)), own_mods)
    ada_bias_out = jnp.sum(own_mods.astype(f32), axis=0)
    mine_at = (seq_at == me).astype(f32)
    own_row = jnp.sum(mods.astype(f32) * mine_at[:, None], axis=0).astype(bf16)
    own_row = reorder(own_row.reshape(dp_size, columns), me)
    time_out = jnp.sum(einsum("oe,oce->oc", own_row, ada_full), axis=0, keepdims=True)

    def own_part(row):
        return lax.dynamic_slice_in_dim(row, me * per, per)

    return (
        output,
        input_grad,
        time_out,
        ada_out,
        ada_bias_out,
        own_part(tail[0]),
        qkv_out,
        out_out,
        gain_two_out,
        up_out,
        bias_up_out,
        down_out,
        bias_down_out,
    )


def solution(mesh):
    dp_size, tensor_size = mesh.shape["dp"], mesh.shape["tensor"]
    parts = jax.sharding.Mesh(
        mesh.devices.reshape(dp_size // 2, 2, tensor_size // 2, 2), AXES
    )
    in_specs = (
        P(AXES, None),
        P(DP, None),
        P(None, DP),
        P(DP),
        P(DP),
        P(None, DP, TENSOR),
        P(TENSOR, DP),
        P(DP),
        P(DP, TENSOR),
        P(TENSOR + DP),
        P(TENSOR, DP),
        P(DP),
        P(AXES, None),
    )
    out_specs = (
        P(AXES, None),
        P(AXES, None),
        P(DP, None),
        P(None, DP),
        P(DP),
        P(DP),
        P(None, DP, TENSOR),
        P(TENSOR, DP),
        P(DP),
        P(DP, TENSOR),
        P(TENSOR + DP),
        P(TENSOR, DP),
        P(DP),
    )
    return jax.shard_map(
        functools.partial(per_device, dp_size),
        mesh=parts,
        in_specs=in_specs,
        out_specs=out_specs,
        check_vma=False,
    )
```
